32 devices in a mesh: rep: 8 (over y, x, core), shard: 4 (over z).
Axes of the slice: x: 2, y: 2, z: 4, core: 2. Of those that a mesh axis runs over, the one named last changes fastest.
Arguments:
- tokens: bfloat16 [8, 1024, 768], P('rep', 'shard'), may hold values from -6 to 6
- cotangent: bfloat16 [8, 1024, 768], P('rep', 'shard'), may hold values from -6 to 6
- lengths: int32 [8, 4], P('rep'), may hold values from 1 to 512, 1024 in all within a row
- deal: int32 [8, 1024], P('rep'), may hold values from 0 to 1023, each once within a row
- attn_master: float32 [4, 768, 768], P(None, 'shard'), may hold values from -3 to 3
- ffin_master: float32 [2, 768, 2048], P(None, 'shard'), may hold values from -0.21875 to 0.21875
- ffout_master: float32 [2048, 768], P('shard'), may hold values from -0.125 to 0.125
- gain_master: float32 [2, 768], P(None, 'shard'), may hold values from 0.5 to 1.5
- bias_master: float32 [32, 12], P('shard'), may hold values from -4 to 4
- attn_first: float32 [4, 768, 768], P(None, 'shard'), may hold values from -286.72 to 286.72
- ffin_first: float32 [2, 768, 2048], P(None, 'shard'), may hold values from -30.320738 to 30.320738
- ffout_first: float32 [2048, 768], P('shard'), may hold values from -32.58348 to 32.58348
- gain_first: float32 [2, 768], P(None, 'shard'), may hold values from -75.57557 to 75.57557
- bias_first: float32 [32, 12], P('shard'), may hold values from -284.16 to 284.16
- attn_second: float32 [4, 768, 768], P(None, 'shard'), may hold values from 32.768 to 112721.92
- ffin_second: float32 [2, 768, 2048], P(None, 'shard'), may hold values from 155.648 to 1245.184
- ffout_second: float32 [2048, 768], P('shard'), may hold values from 181.8624 to 1458.176
- gain_second: float32 [2, 768], P(None, 'shard'), may hold values from 966.656 to 7782.4
- bias_second: float32 [32, 12], P('shard'), may hold values from 2097.152 to 16777.217
Outputs:
- layer_out: bfloat16 [8, 1024, 768], P('rep', 'shard')
- input_grad: bfloat16 [8, 1024, 768], P('rep', 'shard')
- attn_new: float32 [4, 768, 768], P(None, 'shard')
- ffin_new: float32 [2, 768, 2048], P(None, 'shard')
- ffout_new: float32 [2048, 768], P('shard')
- gain_step: float32 [2, 768], P(None, 'shard')
- bias_step: float32 [32, 12], P('shard')
- attn_first_new: float32 [4, 768, 768], P(None, 'shard')
- ffin_first_new: float32 [2, 768, 2048], P(None, 'shard')
- ffout_first_new: float32 [2048, 768], P('shard')
- gain_first_new: float32 [2, 768], P(None, 'shard')
- bias_first_new: float32 [32, 12], P('shard')
- attn_second_new: float32 [3, 768, 768], P(None, 'shard')
- wo_second_new: float32 [768, 768], P('shard')
- ffin_second_new: float32 [2, 768, 2048], P(None, 'shard')
- ffout_second_new: float32 [2048, 768], P('shard')
- gain_second_new: float32 [2, 768], P(None, 'shard')
- bias_second_new: float32 [32, 12], P('shard')
- attn_copy: bfloat16 [4, 768, 768], P(None, 'shard')
- ffin_copy: bfloat16 [2, 768, 2048], P(None, 'shard')
- ffout_copy: bfloat16 [2048, 768], P('shard')
The draws below stay inside these ranges and needn't reach their ends.
Inputs may be any that keep to these rules, and one draw needn't show every extreme that they name: Each row holds the 4 lengths of one group's packed sequences; they sum to 1024 and the longest is exactly 512. `deal`: each row is a permutation of 0 to 1023.
All inputs are finite; a program needn't handle non-finite values.
Results may differ from the reference program's by a relative error of at most 0.03.
Values may be sent and summed in bfloat16 or wider, within the bound.
No kernel may reach another device: no remote copies, remote signals or barrier semaphores. Data moves between devices by JAX's collectives and lax.ppermute only.
A program may use at most 192 MiB of HBM per device.

```python
import math
import jax
import jax.numpy as jnp
import numpy as np
from jax import lax

D = 768
H = 12
HD = 64
FF = 2048
NB = 32
NSEQ = 4
TOKG = 1024
LONGEST = 512
N_REP = 8


def draw_attn_master(key, part):
    spread = jnp.array([(D * HD) ** (-0.5), D ** (-0.5), D ** (-0.5), (TOKG / (32.0 * D)) ** 0.5], jnp.float32)
    values = jnp.clip(jax.random.normal(key, (4, D, D), jnp.float32), -5.0, 5.0)
    return values * spread[:, None, None]


def grad_sizes():
    whole = (N_REP * TOKG) ** 0.5
    return jnp.array([(TOKG / 32.0) ** 0.5, 1.5, 1.5, 0.3], jnp.float32) * whole


def draw_attn_first(key, part):
    values = jnp.clip(jax.random.normal(key, (4, D, D), jnp.float32), -5.0, 5.0)
    return values * (0.111 * grad_sizes())[:, None, None]


def draw_attn_second(key, part):
    factor = jnp.exp(jax.random.uniform(key, (4, D, D), jnp.float32, 0.0, 2.0794))
    sizes = grad_sizes()
    return factor * (0.0526 * sizes * sizes)[:, None, None]


def level_of(rng, shape, cuts, low, top_value):
    def one(axis_at, shards_of):
        draws = jax.random.uniform(jax.random.fold_in(jax.random.fold_in(rng, 6), axis_at), (shards_of,), jnp.float32, low / len(cuts), top_value / len(cuts))
        return jnp.repeat(jnp.exp(draws), shape[axis_at] // shards_of).reshape((-1,) + (1,) * (len(shape) - axis_at - 1))

    factor_of = one(*cuts[0])
    for cut in cuts[1:]:
        factor_of = factor_of * one(*cut)
    return factor_of


def profile(amount, total, most, skew):
    weights = [(1 << 20) // math.isqrt(standing ** skew) + 1 for standing in range(2, amount + 1)]
    spare, holding = total - most - (amount - 1), [1] * (amount - 1)
    while spare > 0:
        movable = [i for i in range(amount - 1) if holding[i] < most]
        whole, left = sum([weights[i] for i in movable]), spare
        for i in movable:
            more = min(most - holding[i], max(1, left * weights[i] // whole), spare)
            holding[i] = holding[i] + more
            spare = spare - more
    return np.array([most] + holding)


def ragged(own_key, number_of, total, most, slope):
    if number_of == 2:
        one = jax.random.randint(own_key, (), max(1, total - most), min(most, total - 1) + 1)
        return jnp.stack([one, total - one])
    tallies = jnp.asarray(profile(number_of, total, most, slope), jnp.int32)
    twos = (number_of - 1) // 2
    donor, taker = tallies[1:1 + 2 * twos:2], tallies[2:2 + 2 * twos:2]
    room = jnp.minimum(donor - 1, most - taker)
    moved = jax.random.randint(jax.random.fold_in(own_key, 1), (twos,), 0, 1 << 20) % (room + 1)
    tallies = tallies.at[1:1 + 2 * twos:2].set(donor - moved).at[2:2 + 2 * twos:2].set(taker + moved)
    return tallies[jax.random.permutation(jax.random.fold_in(own_key, 2), number_of)]


def bell_draw(key, extent, scale, bound, shards=(), kind=jnp.bfloat16):
    drawn = scale * jax.random.normal(key, extent, jnp.float32)
    if shards:
        drawn = drawn * level_of(key, extent, shards, -0.22, 0.18)
    return jnp.clip(drawn, -bound, bound).astype(kind)


def setup_inputs(seed: int = 0) -> dict:
    streams_of = jax.random.split(jax.random.key(seed), 20)
    tokens = bell_draw(streams_of[0], (N_REP, TOKG, D), 1.0, 6.0, ((0, 8), (1, 4)))
    cotangent = bell_draw(streams_of[1], (N_REP, TOKG, D), 1.0, 6.0, ((0, 8), (1, 4)))
    lengths = jax.vmap(lambda own: ragged(own, NSEQ, TOKG, LONGEST, 0))(jax.random.split(streams_of[2], N_REP)).reshape((N_REP, NSEQ)).astype(jnp.int32)
    deal = jax.vmap(lambda own: jax.random.permutation(own, TOKG))(jax.random.split(streams_of[3], N_REP)).reshape((N_REP, TOKG)).astype(jnp.int32)
    attn_master = draw_attn_master(jax.random.fold_in(streams_of[19], 71), 0)
    ffin_master = bell_draw(streams_of[5], (2, D, FF), D ** -0.5, 0.21875, ((1, 4),), jnp.float32)
    ffout_master = bell_draw(streams_of[6], (FF, D), FF ** -0.5, 0.125, ((0, 4),), jnp.float32)
    gain_master = jnp.clip(1.0 + 0.1 * jax.random.normal(streams_of[7], (2, D), jnp.float32), 0.5, 1.5)
    bias_master = bell_draw(streams_of[8], (NB, H), 1.0, 4.0, ((0, 4),), jnp.float32)
    attn_first = draw_attn_first(jax.random.fold_in(streams_of[19], 71), 0)
    ffin_first = bell_draw(streams_of[10], (2, D, FF), (0.067 * (N_REP * TOKG) ** 0.5), 30.320738, ((1, 4),), jnp.float32)
    ffout_first = bell_draw(streams_of[11], (FF, D), (0.072 * (N_REP * TOKG) ** 0.5), 32.58348, ((0, 4),), jnp.float32)
    gain_first = bell_draw(streams_of[12], (2, D), (0.167 * (N_REP * TOKG) ** 0.5), 75.57557, ((1, 4),), jnp.float32)
    bias_first = bell_draw(streams_of[13], (NB, H), (0.111 * (N_REP * TOKG * TOKG / 32) ** 0.5), 284.16, ((0, 4),), jnp.float32)
    attn_second = draw_attn_second(jax.random.fold_in(streams_of[19], 71), 0)
    ffin_second = jnp.clip(jnp.exp(math.log(1245.184) - 2.0794415 * jax.random.uniform(streams_of[15], (2, D, FF), jnp.float32) ** level_of(streams_of[15], (2, D, FF), ((1, 4),), -0.2, 0.2)), 155.648, 1245.184)
    ffout_second = jnp.clip(jnp.exp(math.log(1458.176) - 2.0816913 * jax.random.uniform(streams_of[16], (FF, D), jnp.float32) ** level_of(streams_of[16], (FF, D), ((0, 4),), -0.2, 0.2)), 181.8624, 1458.176)
    gain_second = jnp.clip(jnp.exp(math.log(7782.4) - 2.0857773 * jax.random.uniform(streams_of[17], (2, D), jnp.float32) ** level_of(streams_of[17], (2, D), ((1, 4),), -0.2, 0.2)), 966.656, 7782.4)
    bias_second = jnp.clip(jnp.exp(math.log(16777.217) - 2.0794415 * jax.random.uniform(streams_of[18], (NB, H), jnp.float32) ** level_of(streams_of[18], (NB, H), ((0, 4),), -0.2, 0.2)), 2097.152, 16777.217)
    return {"tokens": tokens, "cotangent": cotangent, "lengths": lengths, "deal": deal, "attn_master": attn_master, "ffin_master": ffin_master, "ffout_master": ffout_master, "gain_master": gain_master, "bias_master": bias_master, "attn_first": attn_first, "ffin_first": ffin_first, "ffout_first": ffout_first, "gain_first": gain_first, "bias_first": bias_first, "attn_second": attn_second, "ffin_second": ffin_second, "ffout_second": ffout_second, "gain_second": gain_second, "bias_second": bias_second}


@jax.custom_vjp
def low(v):
    return lax.optimization_barrier(v.astype(jnp.bfloat16)).astype(jnp.float32)

@jax.custom_vjp
def low_back(v):
    return v

def low_keep(v):
    return (low(v), None)

def low_pass(kept, grad):
    return (grad,)

def back_keep(v):
    return (v, None)

def back_low(kept, grad):
    return (low(grad),)
low.defvjp(low_keep, low_pass)
low_back.defvjp(back_keep, back_low)
norm_eps = 1e-06
far_below = -1e+30
steps_beyond = (12, 16, 23, 32, 46, 64, 91)
first_rate = 0.9
second_rate = 0.95
learning = 0.05
shrink = 0.1
adam_eps = 1e-08
first_fix = 1.0 - 0.9 ** 8
second_fix = 1.0 - 0.95 ** 8

def hi_dot(left, right):
    return jnp.dot(left, right, precision=lax.Precision.HIGHEST, preferred_element_type=jnp.float32)

def bucket_of(relative):
    distance = jnp.abs(relative)
    beyond = 8 + sum(((distance >= threshold).astype(jnp.int32) for threshold in steps_beyond))
    near_part = jnp.where(distance < 8, distance, beyond)
    return (near_part + 16 * (relative > 0).astype(jnp.int32)).astype(jnp.int32)

def places(lengths_row, whole_len):
    starts = (jnp.cumsum(lengths_row) - lengths_row).astype(jnp.int32)
    index_all = jnp.arange(whole_len, dtype=jnp.int32)
    passed = index_all[:, None] >= starts[None, :]
    seg_ids = (lax.optimization_barrier(jnp.sum(passed.astype(jnp.int32), axis=1)) - 1).astype(jnp.int32)
    begins = lax.optimization_barrier(jnp.max(jnp.where(passed, starts[None, :], 0), axis=1)).astype(jnp.int32)
    return (seg_ids, (index_all - begins).astype(jnp.int32))

def rms_scale(values, gain):
    return values * lax.rsqrt(lax.optimization_barrier(jnp.mean(values * values, axis=-1, keepdims=True)) + norm_eps) * gain

def layer(x_val, params, seg_ids, positions):
    attn_w, in_w, out_w, gain_w, bias_w = [low(param) for param in params]
    act_one = low(rms_scale(x_val, gain_w[0]))
    query_all = low(low_back(hi_dot(act_one, attn_w[0])))
    key_all = low(low_back(hi_dot(act_one, attn_w[1])))
    value_all = low(low_back(hi_dot(act_one, attn_w[2])))
    key_heads = key_all.reshape(TOKG, H, HD)
    value_heads = value_all.reshape(TOKG, H, HD)
    block_len = min(512, TOKG)

    def attend_block(block_in):
        query_blk, seg_blk, pos_blk = block_in
        scores = jnp.einsum('qhd,khd->hqk', query_blk, key_heads, precision=lax.Precision.HIGHEST)
        bias_vals = jnp.transpose(bias_w[bucket_of(positions[None, :] - pos_blk[:, None])], (2, 0, 1))
        scores = low_back(scores + bias_vals)
        same_seq = seg_blk[:, None] == seg_ids[None, :]
        prob_vals = jax.nn.softmax(jnp.where(same_seq[None], scores, far_below), axis=-1)
        return jnp.einsum('hqk,khd->qhd', low(prob_vals), value_heads, precision=lax.Precision.HIGHEST)
    attn_mix = lax.map(jax.checkpoint(attend_block), (query_all.reshape(TOKG // block_len, block_len, H, HD), seg_ids.reshape(-1, block_len), positions.reshape(-1, block_len)))
    attn_mix = low(low_back(attn_mix.reshape(TOKG, D)))
    x_mid = x_val + low_back(hi_dot(attn_mix, attn_w[3]))
    act_two = low(rms_scale(x_mid, gain_w[1]))
    gate_pre = low_back(hi_dot(act_two, in_w[0]))
    up_pre = low_back(hi_dot(act_two, in_w[1]))
    hidden = low(jax.nn.gelu(gate_pre, approximate=True) * up_pre)
    return x_mid + low_back(hi_dot(hidden, out_w))

def adam_step(master, first, second, grad, decayed):
    new_first = first_rate * first + (1.0 - first_rate) * grad
    new_second = second_rate * second + (1.0 - second_rate) * grad * grad
    update = new_first / first_fix / (jnp.sqrt(new_second / second_fix) + adam_eps)
    if decayed:
        update = update + shrink * master
    new_master = master - learning * update
    return (new_master, new_first, new_second, new_master.astype(jnp.bfloat16))

def reference(tokens, cotangent, lengths, deal, attn_master, ffin_master, ffout_master, gain_master, bias_master, attn_first, ffin_first, ffout_first, gain_first, bias_first, attn_second, ffin_second, ffout_second, gain_second, bias_second):
    masters = (attn_master, ffin_master, ffout_master, gain_master, bias_master)

    def one_group(grad_sums, inputs):
        group_x, group_cot, group_len, group_deal = inputs
        seg_ids, positions = places(group_len, TOKG)

        def forward(x_val, params):
            return layer(x_val, params, seg_ids, positions)[group_deal]
        out_val, pull = jax.vjp(forward, group_x.astype(jnp.float32), masters)
        grad_x, grad_params = pull(group_cot.astype(jnp.float32))
        grad_sums = jax.tree.map(lambda acc_val, add_val: acc_val + add_val, grad_sums, grad_params)
        return (grad_sums, (out_val.astype(jnp.bfloat16), grad_x.astype(jnp.bfloat16)))
    zero_grads = jax.tree.map(jnp.zeros_like, masters)
    grad_sums, (layer_out, input_grad) = lax.scan(one_group, zero_grads, (tokens, cotangent, lengths, deal))
    attn_res = adam_step(attn_master, attn_first, attn_second, grad_sums[0], True)
    ffin_res = adam_step(ffin_master, ffin_first, ffin_second, grad_sums[1], True)
    ffout_res = adam_step(ffout_master, ffout_first, ffout_second, grad_sums[2], True)
    gain_res = adam_step(gain_master, gain_first, gain_second, grad_sums[3], False)
    bias_res = adam_step(bias_master, bias_first, bias_second, grad_sums[4], False)
    return (layer_out, input_grad, attn_res[0], ffin_res[0], ffout_res[0], gain_res[0] - gain_master, bias_res[0] - bias_master, attn_res[1], ffin_res[1], ffout_res[1], gain_res[1], bias_res[1], attn_res[2][:3], attn_res[2][3], ffin_res[2], ffout_res[2], gain_res[2], bias_res[2], attn_res[3], ffin_res[3], ffout_res[3])
```

```python
import functools

import jax
import jax.numpy as jnp
from jax import lax
from jax.experimental import pallas as pl
from jax.experimental.pallas import tpu as pltpu
from jax.sharding import Mesh
from jax.sharding import PartitionSpec as P

norm_eps = 1e-06
far_below = -1e30
steps_beyond = (12, 16, 23, 32, 46, 64, 91)
first_rate = 0.9
second_rate = 0.95
learning = 0.05
shrink = 0.1
adam_eps = 1e-08
first_fix = 1.0 - 0.9**8
second_fix = 1.0 - 0.95**8
chips = ("plane", "shard")
low = jnp.bfloat16
full = jnp.float32


def bucket_of(relative):
    distance = jnp.abs(relative)
    beyond = 8 + sum(((distance >= threshold).astype(jnp.int32) for threshold in steps_beyond))
    near_part = jnp.where(distance < 8, distance, beyond)
    return near_part + 16 * (relative > 0).astype(jnp.int32)


def ndot(left, right):
    return lax.dot_general(left, right, (((1,), (1,)), ((), ())), preferred_element_type=full)


def tdot(left, right):
    return lax.dot_general(left, right, (((0,), (0,)), ((), ())), preferred_element_type=full)


def mdot(left, right):
    return jnp.dot(left, right, preferred_element_type=full)


def swap(value):
    return lax.ppermute(value, "core", [(0, 1), (1, 0)])


def both_cores(mine, other, core, axis):
    first = jnp.where(core == 0, mine, other)
    second = jnp.where(core == 0, other, mine)
    return jnp.concatenate([first, second], axis)


def toeplitz_of(vector_row):
    wide = jnp.broadcast_to(vector_row, (128, vector_row.shape[1]))
    return pltpu.roll(wide, 0, 1, stride=1, stride_axis=0)


def attend_kernel(rows, q_ref, k_ref, v_ref, qseg_ref, kseg_ref, vec_ref, o_ref, p_ref, s_ref):
    keys = k_ref.shape[0]
    lane = lax.broadcasted_iota(jnp.int32, (rows, 128), 1)
    parts = []
    for head in range(2):
        mine = (lane < 64) if head == 0 else (lane >= 64)
        q_head = jnp.where(mine, q_ref[...], jnp.zeros((), low))
        s_ref[...] = ndot(q_head, k_ref[...])
        table = toeplitz_of(vec_ref[0, head : head + 1, :])
        for blk in range(rows // 128):
            here = slice(128 * blk, 128 * blk + 128)
            at = rows - 128 * blk
            scores = s_ref[here, :] + table[:, at : at + keys]
            scores = jnp.where(qseg_ref[here, :] == kseg_ref[...], scores, far_below)
            highest = jnp.max(scores, axis=1, keepdims=True)
            raised = jnp.exp(scores - highest)
            total = jnp.sum(raised, axis=1, keepdims=True)
            p_ref[head, here, :] = (raised * (1.0 / total)).astype(low)
        parts.append(mdot(p_ref[head], v_ref[...]))
    o_ref[...] = jnp.where(lane < 64, parts[0], parts[1]).astype(low)


def attend_back_kernel(
    rows, q_ref, k_ref, v_ref, do_ref, p_ref, dq_ref, dk_ref, dv_ref, diag_ref, s_ref, ds_ref, acc_ref
):
    keys = k_ref.shape[0]
    lane = lax.broadcasted_iota(jnp.int32, (rows, 128), 1)
    q_turned = q_ref[...].astype(full).T.astype(low)
    do_turned = do_ref[...].astype(full).T.astype(low)
    dq_parts, dk_parts, dv_parts = [], [], []
    for head in range(2):
        mine = (lane < 64) if head == 0 else (lane >= 64)
        do_head = jnp.where(mine, do_ref[...], jnp.zeros((), low))
        s_ref[...] = ndot(do_head, v_ref[...])
        acc_ref[...] = jnp.zeros_like(acc_ref)
        for blk in range(rows // 128):
            here = slice(128 * blk, 128 * blk + 128)
            at = rows - 128 * blk
            prob = p_ref[head, here, :].astype(full)
            grad = s_ref[here, :]
            delta = jnp.sum(prob * grad, axis=1, keepdims=True)
            dscore = (prob * (grad - delta)).astype(low)
            ds_ref[here, :] = dscore
            acc_ref[:, at : at + keys] += dscore.astype(full)
        dq_parts.append(mdot(ds_ref[...], k_ref[...]))
        own = slice(64 * head, 64 * head + 64)
        dk_parts.append(mdot(q_turned[own, :], ds_ref[...]))
        dv_parts.append(mdot(do_turned[own, :], p_ref[head]))
        summed = acc_ref[...]
        count = 128
        while count > 8:
            count //= 2
            width = summed.shape[1]
            summed = summed[:count] + pltpu.roll(summed[count:], width - count, 1)
        diag_ref[0, head] = summed
    dq_ref[...] = jnp.where(lane < 64, dq_parts[0], dq_parts[1]).astype(low)
    dk_ref[...] = jnp.concatenate(dk_parts, 0).T.astype(low)
    dv_ref[...] = jnp.concatenate(dv_parts, 0).T.astype(low)


def attend(query, key, value, query_seg, key_seg, vectors):
    rows, width = query.shape
    keys = key.shape[0]
    pairs = width // 128
    span = vectors.shape[-1]
    tall = pl.BlockSpec((rows, 128), lambda i: (0, i))
    wide = pl.BlockSpec((keys, 128), lambda i: (0, i))
    return pl.pallas_call(
        functools.partial(attend_kernel, rows),
        grid=(pairs,),
        in_specs=[
            tall,
            wide,
            wide,
            pl.BlockSpec((rows, 1), lambda i: (0, 0)),
            pl.BlockSpec((1, keys), lambda i: (0, 0)),
            pl.BlockSpec((1, 2, span), lambda i: (i, 0, 0)),
        ],
        out_specs=[tall, pl.BlockSpec((2, rows, keys), lambda i: (i, 0, 0))],
        out_shape=[
            jax.ShapeDtypeStruct((rows, width), low),
            jax.ShapeDtypeStruct((2 * pairs, rows, keys), low),
        ],
        scratch_shapes=[pltpu.VMEM((rows, keys), full)],
        name="attend",
        cost_estimate=pl.CostEstimate(
            flops=8 * pairs * rows * keys * 128,
            bytes_accessed=4 * pairs * rows * keys,
            transcendentals=2 * pairs * rows * keys,
        ),
    )(query, key, value, query_seg, key_seg, vectors.reshape(pairs, 2, span))


def attend_back(query, key, value, grad_out, probs, span):
    rows, width = query.shape
    keys = key.shape[0]
    pairs = width // 128
    tall = pl.BlockSpec((rows, 128), lambda i: (0, i))
    wide = pl.BlockSpec((keys, 128), lambda i: (0, i))
    return pl.pallas_call(
        functools.partial(attend_back_kernel, rows),
        grid=(pairs,),
        in_specs=[tall, wide, wide, tall, pl.BlockSpec((2, rows, keys), lambda i: (i, 0, 0))],
        out_specs=[tall, wide, wide, pl.BlockSpec((1, 2, 8, span), lambda i: (i, 0, 0, 0))],
        out_shape=[
            jax.ShapeDtypeStruct((rows, width), low),
            jax.ShapeDtypeStruct((keys, width), low),
            jax.ShapeDtypeStruct((keys, width), low),
            jax.ShapeDtypeStruct((pairs, 2, 8, span), full),
        ],
        scratch_shapes=[
            pltpu.VMEM((rows, keys), full),
            pltpu.VMEM((rows, keys), low),
            pltpu.VMEM((128, span), full),
        ],
        name="attend_back",
        cost_estimate=pl.CostEstimate(
            flops=20 * pairs * rows * keys * 128,
            bytes_accessed=4 * pairs * rows * keys,
            transcendentals=0,
        ),
    )(query, key, value, grad_out, probs)


def adam_step(master, first, second, grad, decayed):
    new_first = first_rate * first + (1.0 - first_rate) * grad
    new_second = second_rate * second + (1.0 - second_rate) * grad * grad
    update = new_first / first_fix / (jnp.sqrt(new_second / second_fix) + adam_eps)
    if decayed:
        update = update + shrink * master
    new_master = master - learning * update
    return (new_master, new_first, new_second, new_master.astype(low))


def body(
    tokens,
    cotangent,
    lengths,
    deal,
    attn_master,
    ffin_master,
    ffout_master,
    gain_master,
    bias_master,
    attn_first,
    ffin_first,
    ffout_first,
    gain_first,
    bias_first,
    attn_second,
    ffin_second,
    ffout_second,
    gain_second,
    bias_second,
):
    shards = lax.axis_size("shard")
    core = lax.axis_index("core")
    shard = lax.axis_index("shard")
    tok_rows, model = tokens.shape[1], tokens.shape[2]
    heads = bias_master.shape[1]
    own_heads = heads // 2
    part = model // 2
    whole_len = tok_rows * shards
    half_len = whole_len // 2
    per_half = shards // 4
    rows = half_len // per_half
    place, sub = shard // per_half, shard % per_half
    group, rest = place // 2, place % 2
    mine = group == core
    siblings = [[a * per_half + b for b in range(per_half)] for a in range(4)]

    def join_half(value):
        if per_half == 1:
            return value
        return lax.all_gather(value, "shard", axis=0, tiled=True, axis_index_groups=siblings)

    table_own = jnp.concatenate([lengths[0], deal[0]])
    table = jnp.where(mine, table_own, swap(table_own))
    count = lengths.shape[1]
    lens, order = table[:count], table[count:]
    starts = jnp.cumsum(lens) - lens
    long_start = jnp.sum(jnp.where(lens == half_len, starts, 0))
    at_half = jnp.arange(half_len, dtype=jnp.int32)
    token_half = jnp.where(
        rest == 0, long_start + at_half, at_half + half_len * (at_half >= long_start)
    )
    seg_half = jnp.sum((token_half[:, None] >= starts[None, :]).astype(jnp.int32), axis=1)
    first_row = sub * rows
    token_here = lax.dynamic_slice_in_dim(token_half, first_row, rows)
    seg_here = lax.dynamic_slice_in_dim(seg_half, first_row, rows)

    def rows_here(place_of, own):
        gathered = lax.all_gather(own, "shard", axis=0, tiled=True)
        gathered = jnp.where(mine, gathered, swap(gathered))
        picked = (place_of[None, :] == token_here[:, None]).astype(low)
        return mdot(picked, gathered).astype(low)

    def rows_back(place_of, here):
        picked = (place_of[:, None] == token_here[None, :]) & mine
        spread = mdot(picked.astype(low), here).astype(low)
        return lax.psum_scatter(spread, "shard", scatter_dimension=0, tiled=True)

    ff_rows = ffout_master.shape[0]
    ff_part = ff_rows // 2
    attn_low = attn_master.astype(low)
    cols = lax.dynamic_slice_in_dim(attn_low[:3], core * part, part, 2)
    ffin_low = ffin_master.astype(low).reshape(2, -1, shards, 2, ff_part)
    ffin_low = lax.dynamic_index_in_dim(ffin_low, core, 3, keepdims=False)
    ffin_low = ffin_low.reshape(2, -1, shards * ff_part)
    ffout_low = lax.dynamic_slice_in_dim(ffout_master.astype(low), core * ff_part, ff_part, 0)
    w_qkv = lax.all_gather(cols, "shard", axis=1, tiled=True)
    w_o = lax.all_gather(attn_low[3], "shard", axis=0, tiled=True)
    w_in = lax.all_gather(ffin_low, "shard", axis=1, tiled=True)
    w_out = lax.all_gather(ffout_low, "shard", axis=0, tiled=True)
    gains = lax.all_gather(gain_master.astype(low), "shard", axis=1, tiled=True).astype(full)
    bias = lax.all_gather(bias_master.astype(low), "shard", axis=0, tiled=True).astype(full)

    token_index = jnp.arange(whole_len, dtype=jnp.int32)
    x_low = rows_here(token_index, tokens[0])
    grad_y = rows_here(order, cotangent[0])

    x_in = x_low.astype(full)
    scale_one = lax.rsqrt(jnp.mean(x_in * x_in, axis=-1, keepdims=True) + norm_eps)
    act_one = (x_in * scale_one * gains[0]).astype(low)
    query = mdot(act_one, w_qkv[0]).astype(low)
    key_own = mdot(act_one, w_qkv[1]).astype(low)
    value_own = mdot(act_one, w_qkv[2]).astype(low)
    key, value = join_half(key_own), join_half(value_own)
    span = rows + half_len
    relative = jnp.arange(span, dtype=jnp.int32) - rows - first_row
    ids = jnp.arange(bias.shape[0], dtype=jnp.int32)
    one_hot = (bucket_of(relative)[None, :] == ids[:, None]).astype(full)
    bias_own = lax.dynamic_slice_in_dim(bias, core * own_heads, own_heads, 1)
    vectors = lax.dot_general(
        bias_own, one_hot, (((0,), (0,)), ((), ())), precision=lax.Precision.HIGHEST
    )
    mix_own, probs = attend(
        query, key, value, seg_here[:, None], seg_half[None, :], vectors
    )
    mix = both_cores(mix_own, swap(mix_own), core, 1)
    x_mid = x_in + mdot(mix, w_o)
    scale_two = lax.rsqrt(jnp.mean(x_mid * x_mid, axis=-1, keepdims=True) + norm_eps)
    act_two = (x_mid * scale_two * gains[1]).astype(low)
    gate_pre = mdot(act_two, w_in[0])
    up_pre = mdot(act_two, w_in[1])
    gated, gelu_pull = jax.vjp(
        lambda gate_val, up_val: jax.nn.gelu(gate_val, approximate=True) * up_val, gate_pre, up_pre
    )
    hidden = gated.astype(low)
    y_part = mdot(hidden, w_out)
    y_here = (x_mid + y_part + swap(y_part)).astype(low)
    layer_out = rows_back(order, y_here)

    grad_gate, grad_up = gelu_pull(ndot(grad_y, w_out))
    grad_gate, grad_up = grad_gate.astype(low), grad_up.astype(low)
    d_out = tdot(hidden, grad_y).astype(low)
    d_in = jnp.stack([tdot(act_two, grad_gate), tdot(act_two, grad_up)]).astype(low)
    part_two = ndot(grad_gate, w_in[0]) + ndot(grad_up, w_in[1])
    grad_act_two = part_two + swap(part_two)
    turned = grad_act_two * gains[1]
    grad_mid = (
        grad_y.astype(full)
        + scale_two * turned
        - x_mid * scale_two**3 * jnp.mean(turned * x_mid, axis=-1, keepdims=True)
    )
    d_gain_two = jnp.sum(grad_act_two * x_mid * scale_two, axis=0)
    grad_attn = grad_mid.astype(low)
    w_o_own = lax.dynamic_slice_in_dim(w_o, core * part, part, 0)
    grad_mix = ndot(grad_attn, w_o_own).astype(low)
    d_wo = tdot(mix, lax.dynamic_slice_in_dim(grad_attn, core * part, part, 1)).astype(low)
    grad_q, grad_k, grad_v, diagonals = attend_back(query, key, value, grad_mix, probs, span)
    if per_half > 1:
        grad_k = lax.psum_scatter(
            grad_k, "shard", scatter_dimension=0, tiled=True, axis_index_groups=siblings
        )
        grad_v = lax.psum_scatter(
            grad_v, "shard", scatter_dimension=0, tiled=True, axis_index_groups=siblings
        )
    d_wq = tdot(act_one, grad_q).astype(low)
    d_wk = tdot(act_one, grad_k).astype(low)
    d_wv = tdot(act_one, grad_v).astype(low)
    part_one = ndot(grad_q, w_qkv[0]) + ndot(grad_k, w_qkv[1]) + ndot(grad_v, w_qkv[2])
    grad_act_one = part_one + swap(part_one)
    turned = grad_act_one * gains[0]
    grad_x = (
        grad_mid
        + scale_one * turned
        - x_in * scale_one**3 * jnp.mean(turned * x_in, axis=-1, keepdims=True)
    ).astype(low)
    d_gain_one = jnp.sum(grad_act_one * x_in * scale_one, axis=0)
    input_grad = rows_back(token_index, grad_x)

    folded = diagonals.reshape(own_heads, 8, span)
    lined = sum((jnp.roll(folded[:, i], -i, axis=1) for i in range(8)))
    table_own = lax.dot_general(
        one_hot, lined, (((1,), (1,)), ((), ())), precision=lax.Precision.HIGHEST
    )
    empty = jnp.zeros_like(table_own)
    grad_table = jnp.where(
        core == 0,
        jnp.concatenate([table_own, empty], 1),
        jnp.concatenate([empty, table_own], 1),
    )
    grad_gain = jnp.where(core == 0, jnp.stack([d_gain_one, d_gain_two]), 0.0)

    d_attn = jnp.stack([d_wq, d_wk, d_wv, d_wo])

    def reduced(grad, axis):
        share = lax.psum_scatter(grad, "shard", scatter_dimension=axis, tiled=True)
        return lax.psum(share, "plane")

    g_attn = reduced(d_attn, 1)
    g_attn = both_cores(g_attn, swap(g_attn), core, 2).astype(full)
    g_in = reduced(d_in, 1)
    g_in = g_in.reshape(2, -1, shards, 1, ff_part)
    g_in = both_cores(g_in, swap(g_in), core, 3).reshape(ffin_master.shape).astype(full)
    g_out = reduced(d_out, 0)
    g_out = both_cores(g_out, swap(g_out), core, 0).astype(full)
    g_gain, g_bias = lax.psum((grad_gain, grad_table), ("plane", "core", "shard"))
    own_gain = gain_master.shape[1]
    g_gain = lax.dynamic_slice_in_dim(g_gain, shard * own_gain, own_gain, 1)
    own_bias = bias_master.shape[0]
    g_bias = lax.dynamic_slice_in_dim(g_bias, shard * own_bias, own_bias, 0)

    attn_res = adam_step(attn_master, attn_first, attn_second, g_attn, True)
    ffin_res = adam_step(ffin_master, ffin_first, ffin_second, g_in, True)
    ffout_res = adam_step(ffout_master, ffout_first, ffout_second, g_out, True)
    gain_res = adam_step(gain_master, gain_first, gain_second, g_gain, False)
    bias_res = adam_step(bias_master, bias_first, bias_second, g_bias, False)
    return (
        layer_out[None],
        input_grad[None],
        attn_res[0],
        ffin_res[0],
        ffout_res[0],
        gain_res[0] - gain_master,
        bias_res[0] - bias_master,
        attn_res[1],
        ffin_res[1],
        ffout_res[1],
        gain_res[1],
        bias_res[1],
        attn_res[2][:3],
        attn_res[2][3],
        ffin_res[2],
        ffout_res[2],
        gain_res[2],
        bias_res[2],
        attn_res[3],
        ffin_res[3],
        ffout_res[3],
    )


def solution(mesh):
    reps, shards = mesh.devices.shape
    cores = Mesh(mesh.devices.reshape(reps // 2, 2, shards), ("plane", "core", "shard"))
    rep = ("plane", "core")
    tok = P(rep, "shard", None)
    row = P(rep, None)
    second = P(None, "shard", None)
    first = P("shard", None)
    gain = P(None, "shard")
    states = (second, second, first, gain, first)
    in_specs = (tok, tok, row, row) + states * 3
    out_specs = (
        (tok, tok) + states + states + (second, first, second, first, gain, first) + states[:3]
    )
    return jax.shard_map(body, mesh=cores, in_specs=in_specs, out_specs=out_specs, check_vma=False)
```

```python
import functools

import jax
import jax.numpy as jnp
from jax import lax
from jax.experimental import pallas as pl
from jax.experimental.pallas import tpu as pltpu
from jax.sharding import Mesh
from jax.sharding import PartitionSpec as P

norm_eps = 1e-06
far_below = -1e30
steps_beyond = (12, 16, 23, 32, 46, 64, 91)
first_rate = 0.9
second_rate = 0.95
learning = 0.05
shrink = 0.1
adam_eps = 1e-08
first_fix = 1.0 - 0.9**8
second_fix = 1.0 - 0.95**8
chips = ("plane", "shard")
low = jnp.bfloat16
full = jnp.float32


def bucket_of(relative):
    distance = jnp.abs(relative)
    beyond = 8 + sum(((distance >= threshold).astype(jnp.int32) for threshold in steps_beyond))
    near_part = jnp.where(distance < 8, distance, beyond)
    return near_part + 16 * (relative > 0).astype(jnp.int32)


def ndot(left, right):
    return lax.dot_general(left, right, (((1,), (1,)), ((), ())), preferred_element_type=full)


def tdot(left, right):
    return lax.dot_general(left, right, (((0,), (0,)), ((), ())), preferred_element_type=full)


def mdot(left, right):
    return jnp.dot(left, right, preferred_element_type=full)


def swap(value):
    return lax.ppermute(value, "core", [(0, 1), (1, 0)])


def both_cores(mine, other, core, axis):
    first = jnp.where(core == 0, mine, other)
    second = jnp.where(core == 0, other, mine)
    return jnp.concatenate([first, second], axis)


def adam_step(master, first, second, grad, decayed):
    new_first = first_rate * first + (1.0 - first_rate) * grad
    new_second = second_rate * second + (1.0 - second_rate) * grad * grad
    update = new_first / first_fix / (jnp.sqrt(new_second / second_fix) + adam_eps)
    if decayed:
        update = update + shrink * master
    new_master = master - learning * update
    return (new_master, new_first, new_second, new_master.astype(low))


def toeplitz_of(vector_row):
    wide = jnp.broadcast_to(vector_row, (128, vector_row.shape[1]))
    return pltpu.roll(wide, 0, 1, stride=1, stride_axis=0)


def attend_kernel(rows, q_ref, k_ref, v_ref, qseg_ref, kseg_ref, vec_ref, o_ref, p_ref, s_ref):
    keys = k_ref.shape[0]
    lane = lax.broadcasted_iota(jnp.int32, (rows, 128), 1)
    parts = []
    for head in range(2):
        mine = (lane < 64) if head == 0 else (lane >= 64)
        q_head = jnp.where(mine, q_ref[...], jnp.zeros((), low))
        s_ref[...] = ndot(q_head, k_ref[...])
        table = toeplitz_of(vec_ref[0, head : head + 1, :])
        for blk in range(rows // 128):
            here = slice(128 * blk, 128 * blk + 128)
            at = rows - 128 * blk
            scores = s_ref[here, :] + table[:, at : at + keys]
            scores = jnp.where(qseg_ref[here, :] == kseg_ref[...], scores, far_below)
            highest = jnp.max(scores, axis=1, keepdims=True)
            raised = jnp.exp(scores - highest)
            total = jnp.sum(raised, axis=1, keepdims=True)
            p_ref[head, here, :] = (raised * (1.0 / total)).astype(low)
        parts.append(mdot(p_ref[head], v_ref[...]))
    o_ref[...] = jnp.where(lane < 64, parts[0], parts[1]).astype(low)


def attend_back_kernel(
    rows, q_ref, k_ref, v_ref, do_ref, p_ref, dq_ref, dk_ref, dv_ref, diag_ref, s_ref, ds_ref, acc_ref
):
    keys = k_ref.shape[0]
    lane = lax.broadcasted_iota(jnp.int32, (rows, 128), 1)
    q_turned = q_ref[...].astype(full).T.astype(low)
    do_turned = do_ref[...].astype(full).T.astype(low)
    dq_parts, dk_parts, dv_parts = [], [], []
    for head in range(2):
        mine = (lane < 64) if head == 0 else (lane >= 64)
        do_head = jnp.where(mine, do_ref[...], jnp.zeros((), low))
        s_ref[...] = ndot(do_head, v_ref[...])
        acc_ref[...] = jnp.zeros_like(acc_ref)
        for blk in range(rows // 128):
            here = slice(128 * blk, 128 * blk + 128)
            at = rows - 128 * blk
            prob = p_ref[head, here, :].astype(full)
            grad = s_ref[here, :]
            delta = jnp.sum(prob * grad, axis=1, keepdims=True)
            dscore = (prob * (grad - delta)).astype(low)
            ds_ref[here, :] = dscore
            acc_ref[:, at : at + keys] += dscore.astype(full)
        dq_parts.append(mdot(ds_ref[...], k_ref[...]))
        own = slice(64 * head, 64 * head + 64)
        dk_parts.append(mdot(q_turned[own, :], ds_ref[...]))
        dv_parts.append(mdot(do_turned[own, :], p_ref[head]))
        summed = acc_ref[...]
        count = 128
        while count > 8:
            count //= 2
            width = summed.shape[1]
            summed = summed[:count] + pltpu.roll(summed[count:], width - count, 1)
        row = lax.broadcasted_iota(jnp.int32, summed.shape, 0)
        for bit in (1, 2, 4):
            turned = pltpu.roll(summed, summed.shape[1] - bit, 1)
            summed = jnp.where(jnp.bitwise_and(row, bit) > 0, turned, summed)
        diag_ref[0, head : head + 1, :] = jnp.sum(summed, axis=0, keepdims=True)
    dq_ref[...] = jnp.where(lane < 64, dq_parts[0], dq_parts[1]).astype(low)
    dk_ref[...] = jnp.concatenate(dk_parts, 0).T.astype(low)
    dv_ref[...] = jnp.concatenate(dv_parts, 0).T.astype(low)


def attend(query, key, value, query_seg, key_seg, vectors):
    rows, width = query.shape
    keys = key.shape[0]
    pairs = width // 128
    span = vectors.shape[-1]
    tall = pl.BlockSpec((rows, 128), lambda i: (0, i))
    wide = pl.BlockSpec((keys, 128), lambda i: (0, i))
    return pl.pallas_call(
        functools.partial(attend_kernel, rows),
        grid=(pairs,),
        in_specs=[
            tall,
            wide,
            wide,
            pl.BlockSpec((rows, 1), lambda i: (0, 0)),
            pl.BlockSpec((1, keys), lambda i: (0, 0)),
            pl.BlockSpec((1, 2, span), lambda i: (i, 0, 0)),
        ],
        out_specs=[tall, pl.BlockSpec((2, rows, keys), lambda i: (i, 0, 0))],
        out_shape=[
            jax.ShapeDtypeStruct((rows, width), low),
            jax.ShapeDtypeStruct((2 * pairs, rows, keys), low),
        ],
        scratch_shapes=[pltpu.VMEM((rows, keys), full)],
        name="attend",
        cost_estimate=pl.CostEstimate(
            flops=8 * pairs * rows * keys * 128,
            bytes_accessed=4 * pairs * rows * keys,
            transcendentals=2 * pairs * rows * keys,
        ),
    )(query, key, value, query_seg, key_seg, vectors.reshape(pairs, 2, span))


def attend_back(query, key, value, grad_out, probs, span):
    rows, width = query.shape
    keys = key.shape[0]
    pairs = width // 128
    tall = pl.BlockSpec((rows, 128), lambda i: (0, i))
    wide = pl.BlockSpec((keys, 128), lambda i: (0, i))
    return pl.pallas_call(
        functools.partial(attend_back_kernel, rows),
        grid=(pairs,),
        in_specs=[tall, wide, wide, tall, pl.BlockSpec((2, rows, keys), lambda i: (i, 0, 0))],
        out_specs=[tall, wide, wide, pl.BlockSpec((1, 2, span), lambda i: (i, 0, 0))],
        out_shape=[
            jax.ShapeDtypeStruct((rows, width), low),
            jax.ShapeDtypeStruct((keys, width), low),
            jax.ShapeDtypeStruct((keys, width), low),
            jax.ShapeDtypeStruct((pairs, 2, span), full),
        ],
        scratch_shapes=[
            pltpu.VMEM((rows, keys), full),
            pltpu.VMEM((rows, keys), low),
            pltpu.VMEM((128, span), full),
        ],
        name="attend_back",
        cost_estimate=pl.CostEstimate(
            flops=20 * pairs * rows * keys * 128,
            bytes_accessed=4 * pairs * rows * keys,
            transcendentals=0,
        ),
    )(query, key, value, grad_out, probs)


def xor(left, right):
    return jnp.bitwise_xor(left, right)


def by_shard(value, shard):
    pairs = value.reshape((2, 2) + value.shape[1:])
    pairs = jnp.where(shard % 2 == 1, pairs[:, ::-1], pairs)
    return jnp.where(shard // 2 == 1, pairs[::-1], pairs).reshape(value.shape)


def after(value, *others):
    return lax.optimization_barrier((value,) + others)[0]


def send(value, pairs):
    return lax.ppermute(
        value,
        ("plane", "core", "shard"),
        [((p * 2 + c) * 4 + z, (q * 2 + d) * 4 + w) for (p, c, z), (q, d, w) in pairs],
    )


ALL = [(p, c, z) for p in range(4) for c in range(2) for z in range(4)]


def plane_first(value):
    return send(value, [((p, c, z), (p ^ (1 + c), c, z)) for p, c, z in ALL])


def plane_second(value):
    return send(value, [((p, c, z), (p ^ (2 - c), c, z)) for p, c, z in ALL])


def across(value, step):
    return send(value, [((p, c, z), (p, c, z ^ step)) for p, c, z in ALL])


def turns(core):
    return (0, 1 + core, 2 - core, 3)


def stack_at(turn, core):
    return jnp.where((core == 1) & ((turn == 1) | (turn == 2)), 3 - turn, turn)


def tile_at(start, size):
    return pl.ds(pl.multiple_of(start, size), size)


vmem = pl.BlockSpec(memory_space=pltpu.VMEM)
anywhere = pl.BlockSpec(memory_space=pl.ANY)
fixed = pl.BlockSpec(memory_space=pltpu.HBM)


def call(kernel, spot, inputs, outputs, scratch, name, flops=0, grant=16):
    arrays = [item[0] if isinstance(item, (tuple, list)) else item for item in inputs]
    specs = [
        anywhere if isinstance(item, tuple) else fixed if isinstance(item, list) else vmem for item in inputs
    ]
    return pl.pallas_call(
        kernel,
        in_specs=[pl.BlockSpec(memory_space=pltpu.SMEM)] + specs,
        out_specs=[vmem for _ in outputs],
        scratch_shapes=scratch,
        out_shape=[jax.ShapeDtypeStruct(shape, kind) for shape, kind in outputs],
        name=name,
        cost_estimate=pl.CostEstimate(flops=0, bytes_accessed=0, transcendentals=0),
        compiler_params=pltpu.CompilerParams(vmem_limit_bytes=grant << 20),
    )(spot, *arrays)


def fetch_part(source, target, sem):
    copy = pltpu.make_async_copy(source, target, sem)
    copy.start()
    return copy


def bring(pieces, near_ref, far_ref, sems, scalars):
    plane, core, shard = scalars[0], scalars[1], scalars[2]
    copies = []
    for k, turn in enumerate(turns(core)):
        quarter = xor(plane, turn)
        for step in (1, 2, 3):
            source = (near_ref, far_ref)[k // 2].at[3 * (k % 2) + step - 1]
            for part, target in pieces(source, quarter, xor(shard, step)):
                copies.append(fetch_part(part, target, sems.at[len(copies)]))
    return copies


def attend_all_kernel(scalars, q_ref, k_ref, v_ref, qseg_ref, kseg_ref, vec_ref, o_ref, p_ref, s_ref):
    def one(pair, _):
        lanes = tile_at(128 * pair, 128)
        attend_kernel(
            512, q_ref.at[:, lanes], k_ref.at[:, lanes], v_ref.at[:, lanes], qseg_ref, kseg_ref,
            vec_ref.at[pl.ds(pair, 1)], o_ref.at[:, lanes], p_ref.at[pl.ds(2 * pair, 2)], s_ref,
        )
        return 0

    lax.fori_loop(0, 3, one, 0)


def hot_buckets():
    relative = lax.broadcasted_iota(jnp.int32, (32, 1024), 1) - 512
    return jnp.where(bucket_of(relative) == lax.broadcasted_iota(jnp.int32, (32, 1024), 0), 1.0, 0.0)


def unpack_kernel(scalars, r0, r1, r2, r3, gain_ref, vec_ref, bias_ref):
    core, shard = scalars[1], scalars[2]
    for z in range(4):
        rows = jnp.zeros((16, 384), full)
        for step, ref in enumerate((r0, r1, r2, r3)):
            rows = rows + jnp.where(xor(shard, step) == z, ref[192:208, :].astype(full), 0.0)
        gain_ref[:, 192 * z : 192 * z + 192] = rows[0:2, :192]
        bias_ref[8 * z : 8 * z + 8, :] = rows[2:10, :12]
    found = lax.dot_general(
        bias_ref[...], hot_buckets(), (((0,), (0,)), ((), ())),
        precision=lax.Precision.HIGHEST, preferred_element_type=full,
    )
    own = jnp.where(core == 0, found[0:6], found[6:12])
    for i in range(6):
        vec_ref[i // 2, i % 2 : i % 2 + 1, :] = own[i : i + 1]


def cat_kernel(rows, scalars, *refs):
    at = 0
    for ref in refs[:-1]:
        value = ref[...]
        if len(value.shape) == 2:
            value = value[None]
        refs[-1][at : at + value.shape[0]] = value[:, :rows]
        at += value.shape[0]


def cat(spot, pieces, rows, name):
    count = sum(1 if len(piece.shape) == 2 else piece.shape[0] for piece in pieces)
    shape = (count, rows, pieces[0].shape[-1])
    return call(functools.partial(cat_kernel, rows), spot, pieces, [(shape, pieces[0].dtype)], [], name, 0, 4)[0]


def pass_ffn_kernel(scalars, keep, first, out):
    def one(i, _):
        rows, later = tile_at(576 * i, 576), tile_at(2304 + 576 * i, 576)
        out[rows, :] = (wide(keep[later, :]) + wide(first[later, :])).astype(low)
        return 0

    lax.fori_loop(0, 4, one, 0)


def sum_ffn_kernel(scalars, keep, first, second, *outs):
    for step, out in enumerate(outs):
        rows = tile_at(576 * xor(scalars[2], step), 576)
        total = wide(keep[rows, :]) + wide(first[rows, :]) + wide(second[rows, :])
        out[...] = total.astype(out.dtype)


def pass_attn_kernel(scalars, keep, sent, first, out):
    out[0:768, :] = (wide(keep[768:1536, :]) + wide(first[768:1536, :])).astype(low)
    out[768:784, :] = (wide(sent[1536:1552, :]) + wide(first[1536:1552, :])).astype(low)


def sum_attn_kernel(scalars, keep, passed, first, second, *outs):
    for step, out in enumerate(outs):
        rows = tile_at(192 * xor(scalars[2], step), 192)
        total = wide(keep[rows, :]) + wide(first[rows, :]) + wide(second[rows, :])
        out[0:192, :] = total.astype(out.dtype)
        small = wide(passed[768:784, :]) + wide(second[768:784, :])
        out[192:208, :] = small.astype(out.dtype)


def total_kernel(scalars, own, r1, r2, r3, out, *rest):
    total = own[...] + wide(r1[...]) + wide(r2[...]) + wide(r3[...])
    out[...] = total[: out.shape[0]].astype(low)
    if rest:
        rest[0][...] = total[out.shape[0] :]


def pack_attn_kernel(scalars, master_ref, gain_ref, bias_ref, out_ref, part_ref, gain_part, bias_part, sems):
    columns = tile_at(384 * scalars[1], 384)
    copies = [
        fetch_part(master_ref.at[scalars[0], :, columns], part_ref, sems.at[0]),
        fetch_part(gain_ref, gain_part, sems.at[1]),
        fetch_part(bias_ref, bias_part, sems.at[2]),
    ]
    for copy in copies:
        copy.wait()
    gains = jnp.concatenate([gain_part[...], jnp.zeros((2, 192), full)], 1)
    bias = jnp.concatenate([bias_part[...], jnp.zeros((8, 372), full)], 1)
    out_ref[192:208, :] = jnp.concatenate([gains, bias, jnp.zeros((6, 384), full)], 0).astype(low)
    out_ref[0:192, :] = part_ref[...].astype(low)


def pack_ffn_kernel(scalars, in_ref, out_ref, unit_ref, part_ref, rows_ref, sems):
    plane, core = scalars[0], scalars[1]
    copies = []
    for k in range(2):
        columns = tile_at(1024 * (plane % 2) + 512 * k + 256 * core, 256)
        copies.append(fetch_part(in_ref.at[plane // 2, :, columns], part_ref.at[k], sems.at[k]))
    rows = tile_at(256 * core + 64 * plane, 64)
    copies.append(fetch_part(out_ref.at[rows, :], rows_ref, sems.at[2]))
    for copy in copies:
        copy.wait()
    unit_ref[0:192, :] = part_ref[0].astype(low)
    unit_ref[192:384, :] = part_ref[1].astype(low)
    for i in range(3):
        unit_ref[384 + 64 * i : 448 + 64 * i, :] = rows_ref[:, 256 * i : 256 * i + 256].astype(low)


def project_kernel(
    scalars, x_ref, gain_ref, master_ref, near_ref, far_ref, w_ref, act_ref, q_ref, k_ref, v_ref, own_ref, sems
):
    columns = tile_at(384 * scalars[1], 384)
    own_copy = fetch_part(master_ref.at[:, :, columns], own_ref, sems.at[12])

    def pieces(source, quarter, shard):
        return [(source, w_ref.at[quarter, tile_at(192 * shard, 192), :])]

    copies = bring(pieces, near_ref, far_ref, sems, scalars)
    x_in = x_ref[...].astype(full)
    scale = lax.rsqrt(jnp.mean(x_in * x_in, axis=-1, keepdims=True) + norm_eps)
    act_ref[...] = (x_in * scale * gain_ref[0:1, :]).astype(low)
    own_copy.wait()
    for quarter in range(4):
        w_ref[quarter, tile_at(192 * scalars[2], 192), :] = own_ref[quarter].astype(low)
    for copy in copies:
        copy.wait()
    for quarter, out in enumerate((q_ref, k_ref, v_ref)):
        out[...] = mdot(act_ref[...], w_ref[quarter]).astype(low)


def gelu_parts(gate):
    inner = 0.7978845608028654 * (gate + 0.044715 * gate * gate * gate)
    bent = jnp.tanh(inner)
    slope = 0.7978845608028654 * (1.0 + 3.0 * 0.044715 * gate * gate)
    value = 0.5 * gate * (1.0 + bent)
    return value, 0.5 * (1.0 + bent) + 0.5 * gate * (1.0 - bent * bent) * slope


def feed_kernel(
    scalars, x_ref, mix_own, mix_other, w_attn, wo_other, gain_ref, gy_ref, in_master, out_master, near_ref, far_ref,
    mid_ref, act_ref, hid_ref, part_ref, y_ref, grad_ref,
    mix_ref, wo_ref, win_ref, wout_ref, own_ref, gate_ref, up_ref, sems,
):
    core, shard = scalars[1], scalars[2]
    own_copy = fetch_part(out_master.at[tile_at(256 * core, 256), :], own_ref, sems.at[60])

    def pieces(source, quarter, shard):
        rows = tile_at(192 * shard, 192)
        found = []
        for k in range(2):
            columns = tile_at(512 * (quarter % 2) + 256 * k, 256)
            found.append((source.at[192 * k : 192 * k + 192, :], win_ref.at[quarter // 2, rows, columns]))
        rows = tile_at(256 * shard + 64 * quarter, 64)
        for i in range(3):
            part = source.at[384 + 64 * i : 448 + 64 * i, :]
            found.append((part, wout_ref.at[rows, 256 * i : 256 * i + 256]))
        return found

    copies = bring(pieces, near_ref, far_ref, sems, scalars)
    here, there = tile_at(384 * core, 384), tile_at(384 * (1 - core), 384)
    mix_ref[:, here] = mix_own[...]
    mix_ref[:, there] = mix_other[...]
    wo_ref[:, here] = w_attn[3]
    wo_ref[:, there] = wo_other[...]

    def middle(half, _):
        rows = tile_at(256 * half, 256)
        x_mid = x_ref[rows, :].astype(full) + mdot(mix_ref[rows, :], wo_ref[...])
        mid_ref[rows, :] = x_mid
        scale = lax.rsqrt(jnp.mean(x_mid * x_mid, axis=-1, keepdims=True) + norm_eps)
        act_ref[rows, :] = (x_mid * scale * gain_ref[1:2, :]).astype(low)
        return 0

    lax.fori_loop(0, 2, middle, 0)
    for i in range(2):
        for k in range(4):
            pair = in_master[i, :, 512 * k : 512 * k + 512]
            win_ref[i, tile_at(192 * shard, 192), 256 * k : 256 * k + 256] = jnp.where(
                core == 0, pair[:, :256], pair[:, 256:]
            ).astype(low)
    own_copy.wait()
    wout_ref[tile_at(256 * shard, 256), :] = own_ref[...].astype(low)
    for copy in copies:
        copy.wait()

    def hidden(at, _):
        rows, columns = tile_at(256 * (at // 2), 256), tile_at(512 * (at % 2), 512)
        gate = mdot(act_ref[rows, :], win_ref[0, :, columns])
        up = mdot(act_ref[rows, :], win_ref[1, :, columns])
        value, slope = gelu_parts(gate)
        hid_ref[rows, columns] = (value * up).astype(low)
        gate_ref[rows, columns] = slope * up
        up_ref[rows, columns] = value
        return 0

    lax.fori_loop(0, 4, hidden, 0)

    def inner(half, _):
        rows = tile_at(256 * half, 256)
        part = jnp.zeros((256, 768), full)
        for h in range(2):
            columns = slice(512 * h, 512 * h + 512)
            grad_hid = ndot(gy_ref[rows, :], wout_ref[columns, :])
            grad_gate = (grad_hid * gate_ref[rows, columns]).astype(low)
            grad_up = (grad_hid * up_ref[rows, columns]).astype(low)
            grad_ref[h, rows, :] = grad_gate
            grad_ref[2 + h, rows, :] = grad_up
            part = part + ndot(grad_gate, win_ref[0, :, columns]) + ndot(grad_up, win_ref[1, :, columns])
        part_ref[rows, :] = part
        y_ref[rows, :] = mdot(hid_ref[rows, :], wout_ref[...])
        return 0

    lax.fori_loop(0, 2, inner, 0)


def outer_kernel(scalars, act_ref, grad_ref, hid_ref, gy_ref, send_ref, keep_ref, turned_ref, sum_ref):
    plane, core = scalars[0], scalars[1]
    turned_ref[...] = act_ref[...].astype(full).T.astype(low)

    def outer(j, _):
        for odd, out in enumerate((keep_ref, send_ref)):
            turn = odd * (1 + core) + j * (2 - core)
            found = mdot(turned_ref[...], grad_ref[xor(plane, turn)]).astype(low)
            for z in range(4):
                for i in range(2):
                    out[tile_at(2304 * j + 576 * z + 192 * i, 192), :] = found[
                        192 * z : 192 * z + 192, 256 * i : 256 * i + 256
                    ]
        return 0

    lax.fori_loop(0, 2, outer, 0)

    def last(z, _):
        sum_ref[...] = tdot(hid_ref[:, tile_at(256 * z, 256)], gy_ref[...])
        for k, turn in enumerate(turns(core)):
            out = (keep_ref, send_ref)[k % 2]
            found = sum_ref[tile_at(64 * xor(plane, turn), 64), :].astype(low)
            for i in range(3):
                out[tile_at(2304 * (k // 2) + 576 * z + 384 + 64 * i, 64), :] = found[:, 256 * i : 256 * i + 256]
        return 0

    lax.fori_loop(0, 4, last, 0)


def pick_kernel(scalars, b0, b1, b2, b3, place_ref, token_ref, out_ref):
    def rows_of(half, _):
        rows = tile_at(256 * half, 256)
        total = jnp.zeros((256, 768), full)
        for i, ref in enumerate((b0, b1, b2, b3)):
            same = place_ref[:, 256 * i : 256 * i + 256] == token_ref[rows, :]
            total = total + mdot(jnp.where(same, 1.0, 0.0).astype(low), ref[...])
        out_ref[rows, :] = total.astype(low)
        return 0

    lax.fori_loop(0, 2, rows_of, 0)


def spread(wanted_ref, token_ref, value, outs):
    for i, out in enumerate(outs):
        same = wanted_ref[256 * i : 256 * i + 256, :] == token_ref[...]
        out[...] = mdot(jnp.where(same, 1.0, 0.0).astype(low), value).astype(low)


def spread_y_kernel(scalars, mid_ref, own_ref, other_ref, wanted_ref, token_ref, o0, o1, o2, o3, value_ref):
    value_ref[...] = (mid_ref[...] + own_ref[...] + other_ref[...]).astype(low)
    spread(wanted_ref, token_ref, value_ref[...], (o0, o1, o2, o3))


def spread_x_kernel(
    scalars, own_ref, other_ref, x_ref, gain_ref, mid_ref, wanted_ref, token_ref, o0, o1, o2, o3, value_ref
):
    x_in = x_ref[...].astype(full)
    scale = lax.rsqrt(jnp.mean(x_in * x_in, axis=-1, keepdims=True) + norm_eps)
    turned = (own_ref[...] + other_ref[...]) * gain_ref[0:1, :]
    lean = jnp.mean(turned * x_in, axis=-1, keepdims=True)
    value_ref[...] = (mid_ref[...] + scale * turned - x_in * (scale * scale * scale * lean)).astype(low)
    spread(wanted_ref, token_ref, value_ref[...], (o0, o1, o2, o3))


def back_kernel(
    scalars, own_part, other_part, mid_ref, gy_ref, gain_ref, w_ref, wo_other, q_ref, k_ref, v_ref, p_ref,
    grad_ref, right_ref, lined_ref, gain_out, attn_ref, mixed_ref, s_ref, ds_ref, acc_ref, *rest
):
    core = scalars[1]
    here, there = tile_at(384 * core, 384), tile_at(384 * (1 - core), 384)
    late = (q_ref, k_ref, v_ref, p_ref)
    copies = [fetch_part(ref, held, rest[-1].at[i]) for i, (ref, held) in enumerate(zip(late, rest[:-1]))]
    q_ref, k_ref, v_ref, p_ref = rest[:-1]
    x_mid = mid_ref[...]
    scale = lax.rsqrt(jnp.mean(x_mid * x_mid, axis=-1, keepdims=True) + norm_eps)
    gain_out[...] = jnp.sum(own_part[...] * x_mid * scale, axis=0, keepdims=True)
    turned = (own_part[...] + other_part[...]) * gain_ref[1:2, :]
    lean = jnp.mean(turned * x_mid, axis=-1, keepdims=True)
    grad_mid = gy_ref[...].astype(full) + scale * turned - x_mid * (scale * scale * scale * lean)
    grad_ref[...] = grad_mid
    attn_ref[...] = grad_mid.astype(low)
    mixed_ref[...] = (
        ndot(attn_ref[:, here], w_ref[3, here, :]) + ndot(attn_ref[:, there], wo_other[here, :])
    ).astype(low)
    for copy in copies:
        copy.wait()

    def one(pair, _):
        lanes = tile_at(128 * pair, 128)
        attend_back_kernel(
            512, *[ref.at[:, lanes] for ref in (q_ref, k_ref, v_ref, mixed_ref)], p_ref.at[pl.ds(2 * pair, 2)],
            *[right_ref.at[i, :, lanes] for i in range(3)], lined_ref.at[pl.ds(pair, 1)], s_ref, ds_ref, acc_ref,
        )
        return 0

    lax.fori_loop(0, 3, one, 0)
    right_ref[3] = attn_ref[:, here]


def last_kernel(
    scalars, act_ref, mix_own, mix_other, right_ref, w_ref, x_ref, lined_ref, other_ref,
    send_ref, keep_ref, part_ref, turned_ref, *rest
):
    plane, core = scalars[0], scalars[1]
    here, there = tile_at(384 * core, 384), tile_at(384 * (1 - core), 384)
    late = (act_ref, mix_own, mix_other, right_ref, w_ref, x_ref)
    copies = [fetch_part(ref, held, rest[-1].at[i]) for i, (ref, held) in enumerate(zip(late, rest[:-1]))]
    act_ref, mix_own, mix_other, right_ref, w_ref, x_ref = rest[:-1]
    for copy in copies:
        copy.wait()
    turned_ref[0] = act_ref[...].astype(full).T.astype(low)
    turned_ref[1, here, :] = mix_own[...].astype(full).T.astype(low)
    turned_ref[1, there, :] = mix_other[...].astype(full).T.astype(low)

    def outer(j, _):
        for odd, out in enumerate((keep_ref, send_ref)):
            quarter = xor(plane, odd * (1 + core) + j * (2 - core))
            out[tile_at(768 * j, 768), :] = mdot(turned_ref[quarter // 3], right_ref[quarter]).astype(low)
        return 0

    lax.fori_loop(0, 2, outer, 0)
    part = ndot(right_ref[0], w_ref[0]) + ndot(right_ref[1], w_ref[1]) + ndot(right_ref[2], w_ref[2])
    part_ref[...] = part
    x_in = x_ref[...].astype(full)
    scale = lax.rsqrt(jnp.mean(x_in * x_in, axis=-1, keepdims=True) + norm_eps)
    gain = jnp.sum(part * x_in * scale, axis=0, keepdims=True)
    lined = jnp.concatenate([lined_ref[0], lined_ref[1], lined_ref[2]], 0)
    table = lax.dot_general(
        lined, hot_buckets(), (((1,), (1,)), ((), ())),
        precision=lax.Precision.HIGHEST, preferred_element_type=full,
    )
    table = jnp.concatenate([table, jnp.zeros((6, 352), full)], 1)
    other = other_ref[...]
    send_ref[1536:1552, :] = jnp.concatenate(
        [gain[:, :384], gain[:, 384:], other[:, :384], other[:, 384:], table, jnp.zeros((6, 384), full)], 0
    ).astype(low)


def wide(value):
    return value.astype(full)


def adam_kernel(join, scalars, master, first, second, own, other, *outs):
    lower = scalars[1] == 0
    left = jnp.where(lower, own[0], other[0]).astype(full)
    right = jnp.where(lower, other[0], own[0]).astype(full)
    grad = join(left, right).reshape(master.shape)
    new_master, new_first, new_second, copy = adam_step(master[...], first[...], second[...], grad, True)
    outs[0][...] = new_master
    outs[1][...] = new_first
    outs[2][...] = copy
    if len(outs) == 4:
        outs[3][...] = new_second
    else:

        @pl.when(pl.program_id(0) < 3)
        def _():
            outs[3][...] = new_second

        @pl.when(pl.program_id(0) == 3)
        def _():
            outs[4][...] = new_second[0]


def adam_call(grid, join, state, quarter_of, states, grads, spot, name, sizes, rows_at, second=None):

    def grad_spec(other):
        def where(*idx):
            scalars = idx[-1]
            core = 1 - scalars[1] if other else scalars[1]
            return (stack_at(xor(scalars[0], quarter_of(*idx[:-1])), core), rows_at, 0)

        return pl.BlockSpec(sizes, where)

    shape = states[0].shape
    kinds = [full, full, low] + ([full] if second is None else [])
    count = functools.reduce(lambda a, b: a * b, shape)
    return pl.pallas_call(
        functools.partial(adam_kernel, join),
        grid_spec=pltpu.PrefetchScalarGridSpec(
            num_scalar_prefetch=1,
            grid=grid,
            in_specs=[state] * 3 + [grad_spec(False), grad_spec(True)],
            out_specs=[state] * len(kinds) + ([] if second is None else second[0]),
        ),
        out_shape=[jax.ShapeDtypeStruct(shape, kind) for kind in kinds]
        + ([] if second is None else second[1]),
        name=name,
        cost_estimate=pl.CostEstimate(flops=0, bytes_accessed=0, transcendentals=0),
    )(spot, *states, *grads)


def body_fast(
    tokens,
    cotangent,
    lengths,
    deal,
    attn_master,
    ffin_master,
    ffout_master,
    gain_master,
    bias_master,
    attn_first,
    ffin_first,
    ffout_first,
    gain_first,
    bias_first,
    attn_second,
    ffin_second,
    ffout_second,
    gain_second,
    bias_second,
):
    plane, core, shard = (lax.axis_index(name) for name in ("plane", "core", "shard"))
    spot = jnp.stack([plane, core, shard])
    group, rest = shard // 2, shard % 2
    mine = group == core

    quarter = call(
        pack_attn_kernel, spot, [[attn_master], [gain_master], [bias_master]], [((208, 384), low)],
        [
            pltpu.VMEM((192, 384), full), pltpu.VMEM((2, 192), full), pltpu.VMEM((8, 12), full),
            pltpu.SemaphoreType.DMA((3,)),
        ],
        "pack_attn", 0, 60,
    )[0]
    attn_came = [across(quarter, step) for step in (1, 2, 3)]

    unit = call(
        pack_ffn_kernel, spot, [[ffin_master], [ffout_master]], [((576, 256), low)],
        [pltpu.VMEM((2, 192, 256), full), pltpu.VMEM((64, 768), full), pltpu.SemaphoreType.DMA((3,))],
        "pack_ffn", 0, 60,
    )[0]
    attn_came = [after(value, unit) for value in attn_came]

    def fetch(own, gates=(None, None)):
        up = lambda pairs: [((p, 1, z), (p, 1, w)) for p in range(4) for z, w in pairs]
        down = lambda pairs: [((p, 0, 3 - z), (p, 0, 3 - w)) for p in range(4) for z, w in pairs]
        pairs = lambda *which: up(which) + down(which)
        held = lambda value, gate: value if gate is None else after(value, gate())
        one = held(send(own, pairs((0, 1), (1, 2), (2, 3))), gates[0])
        two = held(send(one, pairs((1, 2), (2, 3))), gates[1])
        three = send(jnp.where(at_end, own, two), pairs((2, 3), (3, 2)))
        return own, one, two, three

    way = 1 - 2 * core
    at_end = shard == 3 * core
    blocks = jnp.stack(
        [shard, shard + way, shard + 2 * way, jnp.where(at_end, shard + 3 * way, shard - way)]
    )
    blocks = jnp.clip(blocks, 0, 3)
    tok_blocks = fetch(tokens[0])

    table_own = jnp.concatenate([lengths[0], deal[0]])
    table = jnp.where(mine, table_own, swap(table_own))
    lens, order = table[:4], table[4:]
    starts = jnp.cumsum(lens) - lens
    long_start = jnp.sum(jnp.where(lens == 512, starts, 0))
    at_half = jnp.arange(512, dtype=jnp.int32)
    token_here = jnp.where(rest == 0, long_start + at_half, at_half + 512 * (at_half >= long_start))
    seg_here = jnp.sum((token_here[:, None] >= starts[None, :]).astype(jnp.int32), axis=1)
    token_index = jnp.arange(1024, dtype=jnp.int32)

    token_column = token_here[:, None]
    token_row = jnp.where(mine, token_here, -1)[None, :]

    def rows_here(place_of, pieces, gate=None):
        place = [lax.dynamic_slice_in_dim(place_of, blocks[i] * 256, 256) for i in range(4)]
        place = jnp.concatenate(place).reshape(1, 1024)
        chosen = call(
            pick_kernel, spot, [*pieces, place, token_column], [((512, 768), low)], [], "pick", 0, 8
        )[0]
        chosen = chosen if gate is None else after(chosen, *gate)
        return jnp.where(mine, chosen, swap(chosen))

    def wanted_by(place_of):
        return by_shard(place_of.reshape(4, 256), shard).reshape(1024, 1)

    def rows_back(rows, gate):
        pairs = lambda step: [((p, c, z), (p, c, z ^ step)) for p, c, z in ALL if z // 2 == c]
        return [after(send(rows[step], pairs(step)), gate) for step in (1, 2, 3)]

    wanted_y = wanted_by(order)
    wanted_x = wanted_by(token_index)

    gains, vectors = call(
        unpack_kernel, spot, [quarter, *attn_came], [((2, 768), full), ((3, 2, 1024), full)],
        [pltpu.VMEM((32, 12), full)], "unpack", 0, 8,
    )

    def spread_plane(pieces, rows, gate=None, late=None):
        near = cat(spot, pieces, rows, "near")
        arrived = plane_first(near)
        if gate is not None:
            arrived = after(arrived, gate)
        near = cat(spot, [near, arrived], rows, "nearest")
        return near, plane_second(near if late is None else after(near, late))

    near, far = spread_plane(attn_came, 192)
    unit = after(unit, near, tok_blocks[2], gains)
    ffn_came = [across(unit, step) for step in (1, 2, 3)]
    x_low = rows_here(token_index, tok_blocks, (far, ffn_came[0]))
    w_attn, act_one, query, key, value = call(
        project_kernel, spot,
        [x_low, gains, [attn_master], (near,), (far,)],
        [((4, 768, 384), low), ((512, 768), low)] + [((512, 384), low)] * 3,
        [pltpu.VMEM((4, 192, 384), full), pltpu.SemaphoreType.DMA((13,))], "project", 0, 60,
    )
    wo_other = swap(w_attn[3])


    mix_own, probs = call(
        attend_all_kernel, spot, [query, key, value, seg_here[:, None], seg_here[None, :], vectors],
        [((512, 384), low), ((6, 512, 512), low)], [pltpu.VMEM((512, 512), full)], "attend", 0, 8,
    )
    ffn_came = [after(piece, mix_own) for piece in ffn_came]
    ffn_near, ffn_far = spread_plane(ffn_came, 576)
    cot_blocks = fetch(after(cotangent[0], *ffn_came), (lambda: ffn_near, None))
    grad_y = rows_here(order, cot_blocks)
    mix_other = swap(mix_own)
    x_mid, act_two, hidden, part_two, y_part, grads_up = call(
        feed_kernel, spot,
        [
            x_low, mix_own, mix_other, w_attn, wo_other, gains, grad_y, ffin_master, [ffout_master],
            (ffn_near,), (ffn_far,),
        ],
        [
            ((512, 768), full), ((512, 768), low), ((512, 1024), low), ((512, 768), full), ((512, 768), full),
            ((4, 512, 512), low),
        ],
        [
            pltpu.VMEM((512, 768), low), pltpu.VMEM((768, 768), low), pltpu.VMEM((2, 768, 1024), low),
            pltpu.VMEM((1024, 768), low), pltpu.VMEM((256, 768), full), pltpu.VMEM((512, 1024), full),
            pltpu.VMEM((512, 1024), full), pltpu.SemaphoreType.DMA((61,)),
        ],
        "feed", 0, 24,
    )
    ffn_send, ffn_keep = call(
        outer_kernel, spot, [act_two, grads_up, hidden, grad_y], [((4608, 256), low)] * 2,
        [pltpu.VMEM((768, 512), low), pltpu.VMEM((256, 768), full)], "outer", 0, 12,
    )
    part_other = after(swap(part_two), ffn_send)
    ffn_first = plane_first(ffn_send)

    y_other = swap(after(y_part, part_other))
    y_rows = call(
        spread_y_kernel, spot, [x_mid, y_part, y_other, wanted_y, token_row], [((256, 768), low)] * 4,
        [pltpu.VMEM((512, 768), low)], "spread_y", 0, 10,
    )
    grad_mid, right, lined, gain_two = call(
        back_kernel, spot,
        [
            after(part_two, *y_rows), part_other, x_mid, grad_y, gains, w_attn, wo_other,
            (query,), (key,), (value,), (probs,),
        ],
        [
            ((512, 768), full), ((4, 512, 384), low), ((3, 2, 1024), full), ((1, 768), full),
        ],
        [
            pltpu.VMEM((512, 768), low), pltpu.VMEM((512, 384), low), pltpu.VMEM((512, 512), full), pltpu.VMEM((512, 512), low),
            pltpu.VMEM((128, 1024), full), *[pltpu.VMEM((512, 384), low)] * 3, pltpu.VMEM((6, 512, 512), low),
            pltpu.SemaphoreType.DMA((4,)),
        ],
        "back", 0, 24,
    )
    ffn_first = after(ffn_first, right)
    one_out = lambda kernel, inputs, shape, name: call(kernel, spot, inputs, [(shape, low)], [], name, 0, 8)[0]
    ffn_passed = one_out(pass_ffn_kernel, [ffn_keep, ffn_first], (2304, 256), "pass_ffn")
    ffn_second = plane_second(ffn_passed)
    attn_send, attn_keep, part_one = call(
        last_kernel, spot,
        [
            (after(act_one, ffn_passed),), (mix_own,), (mix_other,), (right,), (w_attn,), (x_low,), lined, gain_two,
        ],
        [((1552, 384), low), ((1536, 384), low), ((512, 768), full)],
        [
            pltpu.VMEM((2, 768, 512), low), pltpu.VMEM((512, 768), low), *[pltpu.VMEM((512, 384), low)] * 2,
            pltpu.VMEM((4, 512, 384), low), pltpu.VMEM((4, 768, 384), low), pltpu.VMEM((512, 768), low),
            pltpu.SemaphoreType.DMA((6,)),
        ],
        "last", 0, 24,
    )
    y_came = rows_back(y_rows, part_one)
    ffn_second = after(ffn_second, part_one, *y_came)
    layer_out = y_rows[0] + y_came[0] + y_came[1] + y_came[2]
    ffn_own, *ffn_outs = call(
        sum_ffn_kernel, spot, [ffn_keep, ffn_first, ffn_second],
        [((576, 256), full)] + [((576, 256), low)] * 3, [], "sum_ffn", 0, 8,
    )
    ffn_came = [across(out, step) for step, out in zip((1, 2, 3), ffn_outs)]
    attn_first_came = after(plane_first(after(attn_send, ffn_second)), *ffn_came[:2])
    passed = one_out(pass_attn_kernel, [attn_keep, attn_send, attn_first_came], (784, 384), "pass_attn")
    attn_second_came = plane_second(passed)
    attn_own, *attn_outs = call(
        sum_attn_kernel, spot, [attn_keep, passed, attn_first_came, attn_second_came],
        [((208, 384), full)] + [((208, 384), low)] * 3, [], "sum_attn", 0, 8,
    )
    x_rows = call(
        spread_x_kernel, spot, [part_one, swap(part_one), x_low, gains, grad_mid, wanted_x, token_row],
        [((256, 768), low)] * 4, [pltpu.VMEM((512, 768), low)], "spread_x", 0, 10,
    )

    ffn_came = [after(value, attn_second_came) for value in ffn_came]
    attn_outs = [across(out, step) for step, out in zip((1, 2, 3), attn_outs)]
    ffn_sum = one_out(total_kernel, [ffn_own, *ffn_came], (576, 256), "total_ffn")
    ffn_pair = cat(spot, [ffn_sum, after(plane_first(ffn_sum), attn_outs[0])], 576, "pair_ffn")
    ffn_stack = cat(spot, [ffn_pair, after(plane_second(ffn_pair), attn_outs[1], attn_outs[2])], 576, "stack_ffn")
    ffn_sum = (ffn_stack, swap(ffn_stack))
    ffout_state = pl.BlockSpec((2, 1, 64, 768), lambda q, s: (0, q, 0, 0))
    unfold = lambda value: jnp.concatenate([value[:64], value[64:128], value[128:]], 1)
    ffout_res = adam_call(
        (4,), lambda left, right: jnp.stack([unfold(left), unfold(right)]), ffout_state, lambda q: q,
        [state.reshape(2, 4, 64, 768) for state in (ffout_master, ffout_first, ffout_second)],
        ffn_sum, spot, "adam_ffout", (1, 192, 256), 2,
    )
    ffout_res = [value.reshape(512, 768) for value in ffout_res]
    ffin_res = adam_call(
        (2, 2),
        lambda left, right: jnp.concatenate(
            [left[:192], right[:192], left[192:], right[192:]], 1
        ),
        pl.BlockSpec((1, 192, 1024), lambda i, h, s: (i, 0, h)), lambda i, h: 2 * i + h,
        [ffin_master, ffin_first, ffin_second], ffn_sum, spot, "adam_ffin", (1, 384, 256), 0,
    )
    attn_outs = [after(value, ffn_stack) for value in attn_outs]
    attn_sum, small = call(
        total_kernel, spot, [attn_own, *attn_outs], [((192, 384), low), ((16, 384), full)], [], "total_attn", 0, 8
    )
    attn_near = cat(spot, [attn_sum, after(plane_first(attn_sum), ffin_res[0])], 192, "pair_attn")
    attn_stack = cat(spot, [attn_near, after(plane_second(attn_near), ffout_res[0])], 192, "stack_attn")
    attn_sum = (attn_stack, swap(attn_stack))
    x_rows = [after(value, small) for value in x_rows]
    x_came = rows_back(x_rows, attn_stack)
    input_grad = x_rows[0] + x_came[0] + x_came[1] + x_came[2]
    small_other = swap(small)
    gain_sum = (small[:4] + small_other[:4]).reshape(2, 768)
    g_gain = lax.dynamic_slice_in_dim(gain_sum, shard * 192, 192, 1)
    g_bias = both_cores(small[4:10, :32], small_other[4:10, :32], core, 0)
    g_bias = lax.dynamic_slice_in_dim(g_bias, shard * 8, 8, 1).T

    attn_res = adam_call(
        (4,), lambda left, right: jnp.concatenate([left, right], 1),
        pl.BlockSpec((1, 192, 768), lambda m, s: (m, 0, 0)), lambda m: m,
        [attn_master, attn_first, attn_second], attn_sum, spot, "adam_attn", (1, 192, 384), 0,
        (
            [
                pl.BlockSpec((1, 192, 768), lambda m, s: (jnp.minimum(m, 2), 0, 0)),
                pl.BlockSpec((192, 768), lambda m, s: (0, 0)),
            ],
            [jax.ShapeDtypeStruct((3, 192, 768), full), jax.ShapeDtypeStruct((192, 768), full)],
        ),
    )
    gain_res = adam_step(gain_master, gain_first, gain_second, g_gain, False)
    bias_res = adam_step(bias_master, bias_first, bias_second, g_bias, False)
    return (
        layer_out[None],
        input_grad[None],
        attn_res[0],
        ffin_res[0],
        ffout_res[0],
        gain_res[0] - gain_master,
        bias_res[0] - bias_master,
        attn_res[1],
        ffin_res[1],
        ffout_res[1],
        gain_res[1],
        bias_res[1],
        attn_res[3],
        attn_res[4],
        ffin_res[3],
        ffout_res[3],
        gain_res[2],
        bias_res[2],
        attn_res[2],
        ffin_res[2],
        ffout_res[2],
    )


def body_any(
    tokens,
    cotangent,
    lengths,
    deal,
    attn_master,
    ffin_master,
    ffout_master,
    gain_master,
    bias_master,
    attn_first,
    ffin_first,
    ffout_first,
    gain_first,
    bias_first,
    attn_second,
    ffin_second,
    ffout_second,
    gain_second,
    bias_second,
):
    shards = lax.axis_size("shard")
    core = lax.axis_index("core")
    shard = lax.axis_index("shard")
    tok_rows, model = tokens.shape[1], tokens.shape[2]
    heads = bias_master.shape[1]
    own_heads = heads // 2
    part = model // 2
    whole_len = tok_rows * shards
    half_len = whole_len // 2
    per_half = shards // 4
    rows = half_len // per_half
    place, sub = shard // per_half, shard % per_half
    group, rest = place // 2, place % 2
    mine = group == core
    siblings = [[a * per_half + b for b in range(per_half)] for a in range(4)]

    def join_half(value):
        if per_half == 1:
            return value
        return lax.all_gather(value, "shard", axis=0, tiled=True, axis_index_groups=siblings)

    table_own = jnp.concatenate([lengths[0], deal[0]])
    table = jnp.where(mine, table_own, swap(table_own))
    count = lengths.shape[1]
    lens, order = table[:count], table[count:]
    starts = jnp.cumsum(lens) - lens
    long_start = jnp.sum(jnp.where(lens == half_len, starts, 0))
    at_half = jnp.arange(half_len, dtype=jnp.int32)
    token_half = jnp.where(
        rest == 0, long_start + at_half, at_half + half_len * (at_half >= long_start)
    )
    seg_half = jnp.sum((token_half[:, None] >= starts[None, :]).astype(jnp.int32), axis=1)
    first_row = sub * rows
    token_here = lax.dynamic_slice_in_dim(token_half, first_row, rows)
    seg_here = lax.dynamic_slice_in_dim(seg_half, first_row, rows)

    def rows_here(place_of, own):
        gathered = lax.all_gather(own, "shard", axis=0, tiled=True)
        gathered = jnp.where(mine, gathered, swap(gathered))
        picked = (place_of[None, :] == token_here[:, None]).astype(low)
        return mdot(picked, gathered).astype(low)

    def rows_back(place_of, here):
        picked = (place_of[:, None] == token_here[None, :]) & mine
        spread = mdot(picked.astype(low), here).astype(low)
        return lax.psum_scatter(spread, "shard", scatter_dimension=0, tiled=True)

    ff_rows = ffout_master.shape[0]
    ff_part = ff_rows // 2
    attn_low = attn_master.astype(low)
    cols = lax.dynamic_slice_in_dim(attn_low[:3], core * part, part, 2)
    ffin_low = ffin_master.astype(low).reshape(2, -1, shards, 2, ff_part)
    ffin_low = lax.dynamic_index_in_dim(ffin_low, core, 3, keepdims=False)
    ffin_low = ffin_low.reshape(2, -1, shards * ff_part)
    ffout_low = lax.dynamic_slice_in_dim(ffout_master.astype(low), core * ff_part, ff_part, 0)
    w_qkv = lax.all_gather(cols, "shard", axis=1, tiled=True)
    w_o = lax.all_gather(attn_low[3], "shard", axis=0, tiled=True)
    w_in = lax.all_gather(ffin_low, "shard", axis=1, tiled=True)
    w_out = lax.all_gather(ffout_low, "shard", axis=0, tiled=True)
    gains = lax.all_gather(gain_master.astype(low), "shard", axis=1, tiled=True).astype(full)
    bias = lax.all_gather(bias_master.astype(low), "shard", axis=0, tiled=True).astype(full)

    token_index = jnp.arange(whole_len, dtype=jnp.int32)
    x_low = rows_here(token_index, tokens[0])
    grad_y = rows_here(order, cotangent[0])

    x_in = x_low.astype(full)
    scale_one = lax.rsqrt(jnp.mean(x_in * x_in, axis=-1, keepdims=True) + norm_eps)
    act_one = (x_in * scale_one * gains[0]).astype(low)
    query = mdot(act_one, w_qkv[0]).astype(low)
    key_own = mdot(act_one, w_qkv[1]).astype(low)
    value_own = mdot(act_one, w_qkv[2]).astype(low)
    key, value = join_half(key_own), join_half(value_own)
    span = rows + half_len
    relative = jnp.arange(span, dtype=jnp.int32) - rows - first_row
    ids = jnp.arange(bias.shape[0], dtype=jnp.int32)
    one_hot = (bucket_of(relative)[None, :] == ids[:, None]).astype(full)
    bias_own = lax.dynamic_slice_in_dim(bias, core * own_heads, own_heads, 1)
    vectors = lax.dot_general(
        bias_own, one_hot, (((0,), (0,)), ((), ())), precision=lax.Precision.HIGHEST
    )
    mix_own, probs = attend(
        query, key, value, seg_here[:, None], seg_half[None, :], vectors
    )
    mix = both_cores(mix_own, swap(mix_own), core, 1)
    x_mid = x_in + mdot(mix, w_o)
    scale_two = lax.rsqrt(jnp.mean(x_mid * x_mid, axis=-1, keepdims=True) + norm_eps)
    act_two = (x_mid * scale_two * gains[1]).astype(low)
    gate_pre = mdot(act_two, w_in[0])
    up_pre = mdot(act_two, w_in[1])
    gated, gelu_pull = jax.vjp(
        lambda gate_val, up_val: jax.nn.gelu(gate_val, approximate=True) * up_val, gate_pre, up_pre
    )
    hidden = gated.astype(low)
    y_part = mdot(hidden, w_out)
    y_here = (x_mid + y_part + swap(y_part)).astype(low)
    layer_out = rows_back(order, y_here)

    grad_gate, grad_up = gelu_pull(ndot(grad_y, w_out))
    grad_gate, grad_up = grad_gate.astype(low), grad_up.astype(low)
    d_out = tdot(hidden, grad_y).astype(low)
    d_in = jnp.stack([tdot(act_two, grad_gate), tdot(act_two, grad_up)]).astype(low)
    part_two = ndot(grad_gate, w_in[0]) + ndot(grad_up, w_in[1])
    grad_act_two = part_two + swap(part_two)
    turned = grad_act_two * gains[1]
    grad_mid = (
        grad_y.astype(full)
        + scale_two * turned
        - x_mid * scale_two**3 * jnp.mean(turned * x_mid, axis=-1, keepdims=True)
    )
    d_gain_two = jnp.sum(grad_act_two * x_mid * scale_two, axis=0)
    grad_attn = grad_mid.astype(low)
    w_o_own = lax.dynamic_slice_in_dim(w_o, core * part, part, 0)
    grad_mix = ndot(grad_attn, w_o_own).astype(low)
    d_wo = tdot(mix, lax.dynamic_slice_in_dim(grad_attn, core * part, part, 1)).astype(low)
    grad_q, grad_k, grad_v, diagonals = attend_back(query, key, value, grad_mix, probs, span)
    if per_half > 1:
        grad_k = lax.psum_scatter(
            grad_k, "shard", scatter_dimension=0, tiled=True, axis_index_groups=siblings
        )
        grad_v = lax.psum_scatter(
            grad_v, "shard", scatter_dimension=0, tiled=True, axis_index_groups=siblings
        )
    d_wq = tdot(act_one, grad_q).astype(low)
    d_wk = tdot(act_one, grad_k).astype(low)
    d_wv = tdot(act_one, grad_v).astype(low)
    part_one = ndot(grad_q, w_qkv[0]) + ndot(grad_k, w_qkv[1]) + ndot(grad_v, w_qkv[2])
    grad_act_one = part_one + swap(part_one)
    turned = grad_act_one * gains[0]
    grad_x = (
        grad_mid
        + scale_one * turned
        - x_in * scale_one**3 * jnp.mean(turned * x_in, axis=-1, keepdims=True)
    ).astype(low)
    d_gain_one = jnp.sum(grad_act_one * x_in * scale_one, axis=0)
    input_grad = rows_back(token_index, grad_x)

    lined = diagonals.reshape(own_heads, span)
    table_own = lax.dot_general(
        one_hot, lined, (((1,), (1,)), ((), ())), precision=lax.Precision.HIGHEST
    )
    empty = jnp.zeros_like(table_own)
    grad_table = jnp.where(
        core == 0,
        jnp.concatenate([table_own, empty], 1),
        jnp.concatenate([empty, table_own], 1),
    )
    grad_gain = jnp.where(core == 0, jnp.stack([d_gain_one, d_gain_two]), 0.0)

    d_attn = jnp.stack([d_wq, d_wk, d_wv, d_wo])

    def reduced(grad, axis):
        share = lax.psum_scatter(grad, "shard", scatter_dimension=axis, tiled=True)
        return lax.psum(share, "plane")

    g_attn = reduced(d_attn, 1)
    g_attn = both_cores(g_attn, swap(g_attn), core, 2).astype(full)
    g_in = reduced(d_in, 1)
    g_in = g_in.reshape(2, -1, shards, 1, ff_part)
    g_in = both_cores(g_in, swap(g_in), core, 3).reshape(ffin_master.shape).astype(full)
    g_out = reduced(d_out, 0)
    g_out = both_cores(g_out, swap(g_out), core, 0).astype(full)
    g_gain, g_bias = lax.psum((grad_gain, grad_table), ("plane", "core", "shard"))
    own_gain = gain_master.shape[1]
    g_gain = lax.dynamic_slice_in_dim(g_gain, shard * own_gain, own_gain, 1)
    own_bias = bias_master.shape[0]
    g_bias = lax.dynamic_slice_in_dim(g_bias, shard * own_bias, own_bias, 0)

    attn_res = adam_step(attn_master, attn_first, attn_second, g_attn, True)
    ffin_res = adam_step(ffin_master, ffin_first, ffin_second, g_in, True)
    ffout_res = adam_step(ffout_master, ffout_first, ffout_second, g_out, True)
    gain_res = adam_step(gain_master, gain_first, gain_second, g_gain, False)
    bias_res = adam_step(bias_master, bias_first, bias_second, g_bias, False)
    return (
        layer_out[None],
        input_grad[None],
        attn_res[0],
        ffin_res[0],
        ffout_res[0],
        gain_res[0] - gain_master,
        bias_res[0] - bias_master,
        attn_res[1],
        ffin_res[1],
        ffout_res[1],
        gain_res[1],
        bias_res[1],
        attn_res[2][:3],
        attn_res[2][3],
        ffin_res[2],
        ffout_res[2],
        gain_res[2],
        bias_res[2],
        attn_res[3],
        ffin_res[3],
        ffout_res[3],
    )


def solution(mesh):
    reps, shards = mesh.devices.shape
    cores = Mesh(mesh.devices.reshape(reps // 2, 2, shards), ("plane", "core", "shard"))
    rep = ("plane", "core")
    tok = P(rep, "shard", None)
    row = P(rep, None)
    second = P(None, "shard", None)
    first = P("shard", None)
    gain = P(None, "shard")
    states = (second, second, first, gain, first)
    in_specs = (tok, tok, row, row) + states * 3
    out_specs = (
        (tok, tok) + states + states + (second, first, second, first, gain, first) + states[:3]
    )
    body = body_fast if (reps, shards) == (8, 4) else body_any
    return jax.shard_map(body, mesh=cores, in_specs=in_specs, out_specs=out_specs, check_vma=False)
```

```python
import functools

import jax
import jax.numpy as jnp
from jax import lax
from jax.experimental import pallas as pl
from jax.experimental.pallas import tpu as pltpu
from jax.sharding import Mesh
from jax.sharding import PartitionSpec as P

norm_eps = 1e-06
far_below = -1e30
steps_beyond = (12, 16, 23, 32, 46, 64, 91)
first_rate = 0.9
second_rate = 0.95
learning = 0.05
shrink = 0.1
adam_eps = 1e-08
first_fix = 1.0 - 0.9**8
second_fix = 1.0 - 0.95**8
chips = ("plane", "shard")
low = jnp.bfloat16
full = jnp.float32


def bucket_of(relative):
    distance = jnp.abs(relative)
    beyond = 8 + sum(((distance >= threshold).astype(jnp.int32) for threshold in steps_beyond))
    near_part = jnp.where(distance < 8, distance, beyond)
    return near_part + 16 * (relative > 0).astype(jnp.int32)


def ndot(left, right):
    return lax.dot_general(left, right, (((1,), (1,)), ((), ())), preferred_element_type=full)


def tdot(left, right):
    return lax.dot_general(left, right, (((0,), (0,)), ((), ())), preferred_element_type=full)


def mdot(left, right):
    return jnp.dot(left, right, preferred_element_type=full)


def swap(value):
    return lax.ppermute(value, "core", [(0, 1), (1, 0)])


def both_cores(mine, other, core, axis):
    first = jnp.where(core == 0, mine, other)
    second = jnp.where(core == 0, other, mine)
    return jnp.concatenate([first, second], axis)


def adam_step(master, first, second, grad, decayed):
    new_first = first_rate * first + (1.0 - first_rate) * grad
    new_second = second_rate * second + (1.0 - second_rate) * grad * grad
    update = new_first / first_fix / (jnp.sqrt(new_second / second_fix) + adam_eps)
    if decayed:
        update = update + shrink * master
    new_master = master - learning * update
    return (new_master, new_first, new_second, new_master.astype(low))


def toeplitz_of(vector_row):
    wide = jnp.broadcast_to(vector_row, (128, vector_row.shape[1]))
    return pltpu.roll(wide, 0, 1, stride=1, stride_axis=0)


def attend_kernel(rows, q_ref, k_ref, v_ref, qseg_ref, kseg_ref, vec_ref, o_ref, p_ref, s_ref):
    keys = k_ref.shape[0]
    lane = lax.broadcasted_iota(jnp.int32, (rows, 128), 1)
    parts = []
    for head in range(2):
        mine = (lane < 64) if head == 0 else (lane >= 64)
        q_head = jnp.where(mine, q_ref[...], jnp.zeros((), low))
        s_ref[...] = ndot(q_head, k_ref[...])
        table = toeplitz_of(vec_ref[0, head : head + 1, :])
        for blk in range(rows // 128):
            here = slice(128 * blk, 128 * blk + 128)
            at = rows - 128 * blk
            scores = s_ref[here, :] + table[:, at : at + keys]
            scores = jnp.where(qseg_ref[here, :] == kseg_ref[...], scores, far_below)
            highest = jnp.max(scores, axis=1, keepdims=True)
            raised = jnp.exp(scores - highest)
            total = jnp.sum(raised, axis=1, keepdims=True)
            p_ref[head, here, :] = (raised * (1.0 / total)).astype(low)
        parts.append(mdot(p_ref[head], v_ref[...]))
    o_ref[...] = jnp.where(lane < 64, parts[0], parts[1]).astype(low)


def attend_back_kernel(
    rows, q_ref, k_ref, v_ref, do_ref, p_ref, dq_ref, dk_ref, dv_ref, diag_ref, s_ref, ds_ref, acc_ref
):
    keys = k_ref.shape[0]
    lane = lax.broadcasted_iota(jnp.int32, (rows, 128), 1)
    q_turned = q_ref[...].astype(full).T.astype(low)
    do_turned = do_ref[...].astype(full).T.astype(low)
    dq_parts, dk_parts, dv_parts = [], [], []
    for head in range(2):
        mine = (lane < 64) if head == 0 else (lane >= 64)
        do_head = jnp.where(mine, do_ref[...], jnp.zeros((), low))
        s_ref[...] = ndot(do_head, v_ref[...])
        acc_ref[...] = jnp.zeros_like(acc_ref)
        for blk in range(rows // 128):
            here = slice(128 * blk, 128 * blk + 128)
            at = rows - 128 * blk
            prob = p_ref[head, here, :].astype(full)
            grad = s_ref[here, :]
            delta = jnp.sum(prob * grad, axis=1, keepdims=True)
            dscore = (prob * (grad - delta)).astype(low)
            ds_ref[here, :] = dscore
            acc_ref[:, at : at + keys] += dscore.astype(full)
        dq_parts.append(mdot(ds_ref[...], k_ref[...]))
        own = slice(64 * head, 64 * head + 64)
        dk_parts.append(mdot(q_turned[own, :], ds_ref[...]))
        dv_parts.append(mdot(do_turned[own, :], p_ref[head]))
        summed = acc_ref[...]
        count = 128
        while count > 8:
            count //= 2
            width = summed.shape[1]
            summed = summed[:count] + pltpu.roll(summed[count:], width - count, 1)
        row = lax.broadcasted_iota(jnp.int32, summed.shape, 0)
        for bit in (1, 2, 4):
            turned = pltpu.roll(summed, summed.shape[1] - bit, 1)
            summed = jnp.where(jnp.bitwise_and(row, bit) > 0, turned, summed)
        diag_ref[0, head : head + 1, :] = jnp.sum(summed, axis=0, keepdims=True)
    dq_ref[...] = jnp.where(lane < 64, dq_parts[0], dq_parts[1]).astype(low)
    dk_ref[...] = jnp.concatenate(dk_parts, 0).T.astype(low)
    dv_ref[...] = jnp.concatenate(dv_parts, 0).T.astype(low)


def attend(query, key, value, query_seg, key_seg, vectors):
    rows, width = query.shape
    keys = key.shape[0]
    pairs = width // 128
    span = vectors.shape[-1]
    tall = pl.BlockSpec((rows, 128), lambda i: (0, i))
    wide = pl.BlockSpec((keys, 128), lambda i: (0, i))
    return pl.pallas_call(
        functools.partial(attend_kernel, rows),
        grid=(pairs,),
        in_specs=[
            tall,
            wide,
            wide,
            pl.BlockSpec((rows, 1), lambda i: (0, 0)),
            pl.BlockSpec((1, keys), lambda i: (0, 0)),
            pl.BlockSpec((1, 2, span), lambda i: (i, 0, 0)),
        ],
        out_specs=[tall, pl.BlockSpec((2, rows, keys), lambda i: (i, 0, 0))],
        out_shape=[
            jax.ShapeDtypeStruct((rows, width), low),
            jax.ShapeDtypeStruct((2 * pairs, rows, keys), low),
        ],
        scratch_shapes=[pltpu.VMEM((rows, keys), full)],
        name="attend",
        cost_estimate=pl.CostEstimate(
            flops=8 * pairs * rows * keys * 128,
            bytes_accessed=4 * pairs * rows * keys,
            transcendentals=2 * pairs * rows * keys,
        ),
    )(query, key, value, query_seg, key_seg, vectors.reshape(pairs, 2, span))


def attend_back(query, key, value, grad_out, probs, span):
    rows, width = query.shape
    keys = key.shape[0]
    pairs = width // 128
    tall = pl.BlockSpec((rows, 128), lambda i: (0, i))
    wide = pl.BlockSpec((keys, 128), lambda i: (0, i))
    return pl.pallas_call(
        functools.partial(attend_back_kernel, rows),
        grid=(pairs,),
        in_specs=[tall, wide, wide, tall, pl.BlockSpec((2, rows, keys), lambda i: (i, 0, 0))],
        out_specs=[tall, wide, wide, pl.BlockSpec((1, 2, span), lambda i: (i, 0, 0))],
        out_shape=[
            jax.ShapeDtypeStruct((rows, width), low),
            jax.ShapeDtypeStruct((keys, width), low),
            jax.ShapeDtypeStruct((keys, width), low),
            jax.ShapeDtypeStruct((pairs, 2, span), full),
        ],
        scratch_shapes=[
            pltpu.VMEM((rows, keys), full),
            pltpu.VMEM((rows, keys), low),
            pltpu.VMEM((128, span), full),
        ],
        name="attend_back",
        cost_estimate=pl.CostEstimate(
            flops=20 * pairs * rows * keys * 128,
            bytes_accessed=4 * pairs * rows * keys,
            transcendentals=0,
        ),
    )(query, key, value, grad_out, probs)


def xor(left, right):
    return jnp.bitwise_xor(left, right)


def by_shard(value, shard):
    pairs = value.reshape((2, 2) + value.shape[1:])
    pairs = jnp.where(shard % 2 == 1, pairs[:, ::-1], pairs)
    return jnp.where(shard // 2 == 1, pairs[::-1], pairs).reshape(value.shape)


def after(value, *others):
    return lax.optimization_barrier((value,) + others)[0]


def send(value, pairs):
    return lax.ppermute(
        value,
        ("plane", "core", "shard"),
        [((p * 2 + c) * 4 + z, (q * 2 + d) * 4 + w) for (p, c, z), (q, d, w) in pairs],
    )


ALL = [(p, c, z) for p in range(4) for c in range(2) for z in range(4)]


def plane_first(value):
    return send(value, [((p, c, z), (p ^ (1 + c), c, z)) for p, c, z in ALL])


def plane_second(value):
    return send(value, [((p, c, z), (p ^ (2 - c), c, z)) for p, c, z in ALL])


def across(value, step):
    return send(value, [((p, c, z), (p, c, z ^ step)) for p, c, z in ALL])


def turns(core):
    return (0, 1 + core, 2 - core, 3)


def stack_at(turn, core):
    return jnp.where((core == 1) & ((turn == 1) | (turn == 2)), 3 - turn, turn)


def tile_at(start, size):
    return pl.ds(pl.multiple_of(start, size), size)


vmem = pl.BlockSpec(memory_space=pltpu.VMEM)
anywhere = pl.BlockSpec(memory_space=pl.ANY)
fixed = pl.BlockSpec(memory_space=pltpu.HBM)


def call(kernel, spot, inputs, outputs, scratch, name, flops=0, grant=16, loose=()):
    arrays = [item[0] if isinstance(item, (tuple, list)) else item for item in inputs]
    specs = [
        anywhere if isinstance(item, tuple) else fixed if isinstance(item, list) else vmem for item in inputs
    ]
    return pl.pallas_call(
        kernel,
        in_specs=[pl.BlockSpec(memory_space=pltpu.SMEM)] + specs,
        out_specs=[anywhere if i in loose else vmem for i in range(len(outputs))],
        scratch_shapes=scratch,
        out_shape=[jax.ShapeDtypeStruct(shape, kind) for shape, kind in outputs],
        name=name,
        cost_estimate=pl.CostEstimate(flops=0, bytes_accessed=0, transcendentals=0),
        compiler_params=pltpu.CompilerParams(vmem_limit_bytes=grant << 20),
    )(spot, *arrays)


def fetch_part(source, target, sem):
    copy = pltpu.make_async_copy(source, target, sem)
    copy.start()
    return copy


def bring(pieces, near_ref, far_ref, sems, scalars):
    plane, core, shard = scalars[0], scalars[1], scalars[2]
    copies = []
    for k, turn in enumerate(turns(core)):
        quarter = xor(plane, turn)
        for step in (1, 2, 3):
            source = (near_ref, far_ref)[k // 2].at[3 * (k % 2) + step - 1]
            for part, target in pieces(source, quarter, xor(shard, step)):
                copies.append(fetch_part(part, target, sems.at[len(copies)]))
    return copies


def attend_all_kernel(scalars, q_ref, k_ref, v_ref, qseg_ref, kseg_ref, vec_ref, o_ref, p_out, s_ref, p_ref, sems):
    def leave(pair):
        here = pl.ds(2 * pair, 2)
        return pltpu.make_async_copy(p_ref.at[here], p_out.at[here], sems.at[pair])

    def one(pair, _):
        lanes = tile_at(128 * pair, 128)
        attend_kernel(
            512, q_ref.at[:, lanes], k_ref.at[:, lanes], v_ref.at[:, lanes], qseg_ref, kseg_ref,
            vec_ref.at[pl.ds(pair, 1)], o_ref.at[:, lanes], p_ref.at[pl.ds(2 * pair, 2)], s_ref,
        )
        leave(pair).start()
        return 0

    lax.fori_loop(0, 3, one, 0)
    for pair in range(3):
        leave(pair).wait()


def hot_buckets():
    relative = lax.broadcasted_iota(jnp.int32, (32, 1024), 1) - 512
    return jnp.where(bucket_of(relative) == lax.broadcasted_iota(jnp.int32, (32, 1024), 0), 1.0, 0.0)


def unpack_kernel(scalars, r0, r1, r2, r3, gain_ref, vec_ref, bias_ref):
    core, shard = scalars[1], scalars[2]
    for z in range(4):
        rows = jnp.zeros((16, 384), full)
        for step, ref in enumerate((r0, r1, r2, r3)):
            rows = rows + jnp.where(xor(shard, step) == z, ref[192:208, :].astype(full), 0.0)
        gain_ref[:, 192 * z : 192 * z + 192] = rows[0:2, :192]
        bias_ref[8 * z : 8 * z + 8, :] = rows[2:10, :12]
    found = lax.dot_general(
        bias_ref[...], hot_buckets(), (((0,), (0,)), ((), ())),
        precision=lax.Precision.HIGHEST, preferred_element_type=full,
    )
    own = jnp.where(core == 0, found[0:6], found[6:12])
    for i in range(6):
        vec_ref[i // 2, i % 2 : i % 2 + 1, :] = own[i : i + 1]


def cat_kernel(rows, scalars, *refs):
    at = 0
    for ref in refs[:-1]:
        value = ref[...]
        if len(value.shape) == 2:
            value = value[None]
        refs[-1][at : at + value.shape[0]] = value[:, :rows]
        at += value.shape[0]


def cat(spot, pieces, rows, name):
    count = sum(1 if len(piece.shape) == 2 else piece.shape[0] for piece in pieces)
    shape = (count, rows, pieces[0].shape[-1])
    return call(functools.partial(cat_kernel, rows), spot, pieces, [(shape, pieces[0].dtype)], [], name, 0, 4)[0]


def pass_ffn_kernel(scalars, keep, first, out):
    def one(i, _):
        rows, later = tile_at(576 * i, 576), tile_at(2304 + 576 * i, 576)
        out[rows, :] = (wide(keep[later, :]) + wide(first[later, :])).astype(low)
        return 0

    lax.fori_loop(0, 4, one, 0)


def sum_ffn_kernel(scalars, keep, first, second, *outs):
    for step, out in enumerate(outs):
        rows = tile_at(576 * xor(scalars[2], step), 576)
        total = wide(keep[rows, :]) + wide(first[rows, :]) + wide(second[rows, :])
        out[...] = total.astype(out.dtype)


def pass_attn_kernel(scalars, keep, sent, first, out):
    out[0:768, :] = (wide(keep[768:1536, :]) + wide(first[768:1536, :])).astype(low)
    out[768:784, :] = (wide(sent[1536:1552, :]) + wide(first[1536:1552, :])).astype(low)


def sum_attn_kernel(scalars, keep, passed, first, second, *outs):
    for step, out in enumerate(outs):
        rows = tile_at(192 * xor(scalars[2], step), 192)
        total = wide(keep[rows, :]) + wide(first[rows, :]) + wide(second[rows, :])
        out[0:192, :] = total.astype(out.dtype)
        small = wide(passed[768:784, :]) + wide(second[768:784, :])
        out[192:208, :] = small.astype(out.dtype)


def total_kernel(scalars, own, r1, r2, r3, out, *rest):
    total = own[...] + wide(r1[...]) + wide(r2[...]) + wide(r3[...])
    out[...] = total[: out.shape[0]].astype(low)
    if rest:
        rest[0][...] = total[out.shape[0] :]


def pack_attn_kernel(scalars, master_ref, gain_ref, bias_ref, out_ref, part_ref, gain_part, bias_part, sems):
    columns = tile_at(384 * scalars[1], 384)
    copies = [
        fetch_part(master_ref.at[scalars[0], :, columns], part_ref, sems.at[0]),
        fetch_part(gain_ref, gain_part, sems.at[1]),
        fetch_part(bias_ref, bias_part, sems.at[2]),
    ]
    for copy in copies:
        copy.wait()
    gains = jnp.concatenate([gain_part[...], jnp.zeros((2, 192), full)], 1)
    bias = jnp.concatenate([bias_part[...], jnp.zeros((8, 372), full)], 1)
    out_ref[192:208, :] = jnp.concatenate([gains, bias, jnp.zeros((6, 384), full)], 0).astype(low)
    out_ref[0:192, :] = part_ref[...].astype(low)


def pack_ffn_kernel(scalars, in_ref, out_ref, unit_ref, part_ref, rows_ref, sems):
    plane, core = scalars[0], scalars[1]
    copies = []
    for k in range(2):
        columns = tile_at(1024 * (plane % 2) + 512 * k + 256 * core, 256)
        copies.append(fetch_part(in_ref.at[plane // 2, :, columns], part_ref.at[k], sems.at[k]))
    rows = tile_at(256 * core + 64 * plane, 64)
    copies.append(fetch_part(out_ref.at[rows, :], rows_ref, sems.at[2]))
    for copy in copies:
        copy.wait()
    unit_ref[0:192, :] = part_ref[0].astype(low)
    unit_ref[192:384, :] = part_ref[1].astype(low)
    for i in range(3):
        unit_ref[384 + 64 * i : 448 + 64 * i, :] = rows_ref[:, 256 * i : 256 * i + 256].astype(low)


def project_kernel(
    scalars, x_ref, gain_ref, master_ref, near_ref, far_ref, w_ref, act_ref, q_ref, k_ref, v_ref, own_ref, sems
):
    columns = tile_at(384 * scalars[1], 384)
    own_copy = fetch_part(master_ref.at[:, :, columns], own_ref, sems.at[12])

    def pieces(source, quarter, shard):
        return [(source, w_ref.at[quarter, tile_at(192 * shard, 192), :])]

    copies = bring(pieces, near_ref, far_ref, sems, scalars)
    x_in = x_ref[...].astype(full)
    scale = lax.rsqrt(jnp.mean(x_in * x_in, axis=-1, keepdims=True) + norm_eps)
    act_ref[...] = (x_in * scale * gain_ref[0:1, :]).astype(low)
    own_copy.wait()
    for quarter in range(4):
        w_ref[quarter, tile_at(192 * scalars[2], 192), :] = own_ref[quarter].astype(low)
    for copy in copies:
        copy.wait()
    for quarter, out in enumerate((q_ref, k_ref, v_ref)):
        out[...] = mdot(act_ref[...], w_ref[quarter]).astype(low)


def gelu_parts(gate):
    inner = 0.7978845608028654 * (gate + 0.044715 * gate * gate * gate)
    bent = jnp.tanh(inner)
    slope = 0.7978845608028654 * (1.0 + 3.0 * 0.044715 * gate * gate)
    value = 0.5 * gate * (1.0 + bent)
    return value, 0.5 * (1.0 + bent) + 0.5 * gate * (1.0 - bent * bent) * slope


def feed_kernel(
    scalars, x_ref, mix_own, mix_other, w_attn, wo_other, gain_ref, gy_ref, in_master, out_master, near_ref, far_ref,
    mid_ref, act_ref, hid_ref, part_ref, y_ref, grad_ref,
    mix_ref, wo_ref, win_ref, wout_ref, own_ref, gate_ref, up_ref, sems,
):
    core, shard = scalars[1], scalars[2]
    own_copy = fetch_part(out_master.at[tile_at(256 * core, 256), :], own_ref, sems.at[60])

    def pieces(source, quarter, shard):
        rows = tile_at(192 * shard, 192)
        found = []
        for k in range(2):
            columns = tile_at(512 * (quarter % 2) + 256 * k, 256)
            found.append((source.at[192 * k : 192 * k + 192, :], win_ref.at[quarter // 2, rows, columns]))
        rows = tile_at(256 * shard + 64 * quarter, 64)
        for i in range(3):
            part = source.at[384 + 64 * i : 448 + 64 * i, :]
            found.append((part, wout_ref.at[rows, 256 * i : 256 * i + 256]))
        return found

    copies = bring(pieces, near_ref, far_ref, sems, scalars)
    here, there = tile_at(384 * core, 384), tile_at(384 * (1 - core), 384)
    mix_ref[:, here] = mix_own[...]
    mix_ref[:, there] = mix_other[...]
    wo_ref[:, here] = w_attn[3]
    wo_ref[:, there] = wo_other[...]

    def middle(half, _):
        rows = tile_at(256 * half, 256)
        x_mid = x_ref[rows, :].astype(full) + mdot(mix_ref[rows, :], wo_ref[...])
        mid_ref[rows, :] = x_mid
        scale = lax.rsqrt(jnp.mean(x_mid * x_mid, axis=-1, keepdims=True) + norm_eps)
        act_ref[rows, :] = (x_mid * scale * gain_ref[1:2, :]).astype(low)
        return 0

    lax.fori_loop(0, 2, middle, 0)
    for i in range(2):
        for k in range(4):
            pair = in_master[i, :, 512 * k : 512 * k + 512]
            win_ref[i, tile_at(192 * shard, 192), 256 * k : 256 * k + 256] = jnp.where(
                core == 0, pair[:, :256], pair[:, 256:]
            ).astype(low)
    own_copy.wait()
    wout_ref[tile_at(256 * shard, 256), :] = own_ref[...].astype(low)
    for copy in copies:
        copy.wait()

    def hidden(at, _):
        rows, columns = tile_at(256 * (at // 2), 256), tile_at(512 * (at % 2), 512)
        gate = mdot(act_ref[rows, :], win_ref[0, :, columns])
        up = mdot(act_ref[rows, :], win_ref[1, :, columns])
        value, slope = gelu_parts(gate)
        hid_ref[rows, columns] = (value * up).astype(low)
        gate_ref[rows, columns] = slope * up
        up_ref[rows, columns] = value
        return 0

    lax.fori_loop(0, 4, hidden, 0)

    def inner(half, _):
        rows = tile_at(256 * half, 256)
        part = jnp.zeros((256, 768), full)
        for h in range(2):
            columns = slice(512 * h, 512 * h + 512)
            grad_hid = ndot(gy_ref[rows, :], wout_ref[columns, :])
            grad_gate = (grad_hid * gate_ref[rows, columns]).astype(low)
            grad_up = (grad_hid * up_ref[rows, columns]).astype(low)
            grad_ref[h, rows, :] = grad_gate
            grad_ref[2 + h, rows, :] = grad_up
            part = part + ndot(grad_gate, win_ref[0, :, columns]) + ndot(grad_up, win_ref[1, :, columns])
        part_ref[rows, :] = part
        y_ref[rows, :] = mdot(hid_ref[rows, :], wout_ref[...])
        return 0

    lax.fori_loop(0, 2, inner, 0)


def outer_kernel(scalars, act_ref, grad_ref, hid_ref, gy_ref, send_ref, keep_ref, turned_ref, sum_ref):
    plane, core = scalars[0], scalars[1]
    turned_ref[...] = act_ref[...].astype(full).T.astype(low)

    def outer(j, _):
        for odd, out in enumerate((keep_ref, send_ref)):
            turn = odd * (1 + core) + j * (2 - core)
            found = mdot(turned_ref[...], grad_ref[xor(plane, turn)]).astype(low)
            for z in range(4):
                for i in range(2):
                    out[tile_at(2304 * j + 576 * z + 192 * i, 192), :] = found[
                        192 * z : 192 * z + 192, 256 * i : 256 * i + 256
                    ]
        return 0

    lax.fori_loop(0, 2, outer, 0)

    def last(z, _):
        sum_ref[...] = tdot(hid_ref[:, tile_at(256 * z, 256)], gy_ref[...])
        for k, turn in enumerate(turns(core)):
            out = (keep_ref, send_ref)[k % 2]
            found = sum_ref[tile_at(64 * xor(plane, turn), 64), :].astype(low)
            for i in range(3):
                out[tile_at(2304 * (k // 2) + 576 * z + 384 + 64 * i, 64), :] = found[:, 256 * i : 256 * i + 256]
        return 0

    lax.fori_loop(0, 4, last, 0)


def pick_kernel(scalars, b0, b1, b2, b3, place_ref, token_ref, out_ref):
    def rows_of(half, _):
        rows = tile_at(256 * half, 256)
        total = jnp.zeros((256, 768), full)
        for i, ref in enumerate((b0, b1, b2, b3)):
            same = place_ref[:, 256 * i : 256 * i + 256] == token_ref[rows, :]
            total = total + mdot(jnp.where(same, 1.0, 0.0).astype(low), ref[...])
        out_ref[rows, :] = total.astype(low)
        return 0

    lax.fori_loop(0, 2, rows_of, 0)


def spread(wanted_ref, token_ref, value, near_ref, own_ref, far_ref):
    for step, out in enumerate((own_ref, near_ref.at[0:256], far_ref, near_ref.at[256:512])):
        same = wanted_ref[256 * step : 256 * step + 256, :] == token_ref[...]
        out[...] = mdot(jnp.where(same, 1.0, 0.0).astype(low), value).astype(low)


def spread_y_kernel(
    scalars, mid_ref, own_part, other_part, wanted_ref, token_ref, near_ref, own_ref, far_ref, value_ref, *rest
):
    parts = (mid_ref, own_part, other_part)
    copies = [fetch_part(ref, held, rest[-1].at[i]) for i, (ref, held) in enumerate(zip(parts, rest[:-1]))]
    for copy in copies:
        copy.wait()
    value_ref[...] = (rest[0][...] + rest[1][...] + rest[2][...]).astype(low)
    spread(wanted_ref, token_ref, value_ref[...], near_ref, own_ref, far_ref)


def spread_x_kernel(
    scalars, own_part, other_part, x_ref, gain_ref, mid_ref, wanted_ref, token_ref, near_ref, own_ref, far_ref,
    value_ref, *rest
):
    parts = (own_part, other_part, mid_ref, x_ref)
    copies = [fetch_part(ref, held, rest[-1].at[i]) for i, (ref, held) in enumerate(zip(parts, rest[:-1]))]
    for copy in copies:
        copy.wait()
    own_part, other_part, mid_ref, x_ref = rest[:-1]
    x_in = x_ref[...].astype(full)
    scale = lax.rsqrt(jnp.mean(x_in * x_in, axis=-1, keepdims=True) + norm_eps)
    turned = (own_part[...] + other_part[...]) * gain_ref[0:1, :]
    lean = jnp.mean(turned * x_in, axis=-1, keepdims=True)
    value_ref[...] = (mid_ref[...] + scale * turned - x_in * (scale * scale * scale * lean)).astype(low)
    spread(wanted_ref, token_ref, value_ref[...], near_ref, own_ref, far_ref)


def add_kernel(scalars, value_ref, more_ref, out_ref):
    out_ref[...] = value_ref[...] + more_ref[256:512, :]


def back_kernel(
    scalars, own_part, other_part, mid_ref, gy_ref, gain_ref, w_ref, wo_other, q_ref, k_ref, v_ref, p_ref,
    grad_ref, right_ref, lined_ref, gain_out, attn_ref, mixed_ref, s_ref, ds_ref, acc_ref, *rest
):
    core = scalars[1]
    here, there = tile_at(384 * core, 384), tile_at(384 * (1 - core), 384)
    late = (own_part, other_part, mid_ref, gy_ref, wo_other, w_ref.at[3], q_ref, k_ref, v_ref, p_ref)
    copies = [fetch_part(ref, held, rest[-1].at[i]) for i, (ref, held) in enumerate(zip(late, rest[:-1]))]
    own_part, other_part, mid_ref, gy_ref, wo_other, wo_own, q_ref, k_ref, v_ref, p_ref = rest[:-1]
    for copy in copies[:4]:
        copy.wait()
    x_mid = mid_ref[...]
    scale = lax.rsqrt(jnp.mean(x_mid * x_mid, axis=-1, keepdims=True) + norm_eps)
    gain_out[...] = jnp.sum(own_part[...] * x_mid * scale, axis=0, keepdims=True)
    turned = (own_part[...] + other_part[...]) * gain_ref[1:2, :]
    lean = jnp.mean(turned * x_mid, axis=-1, keepdims=True)
    grad_mid = gy_ref[...].astype(full) + scale * turned - x_mid * (scale * scale * scale * lean)
    grad_ref[...] = grad_mid
    attn_ref[...] = grad_mid.astype(low)
    for copy in copies[4:]:
        copy.wait()
    mixed_ref[...] = (
        ndot(attn_ref[:, here], wo_own[here, :]) + ndot(attn_ref[:, there], wo_other[here, :])
    ).astype(low)

    def one(pair, _):
        lanes = tile_at(128 * pair, 128)
        attend_back_kernel(
            512, *[ref.at[:, lanes] for ref in (q_ref, k_ref, v_ref, mixed_ref)], p_ref.at[pl.ds(2 * pair, 2)],
            *[right_ref.at[i, :, lanes] for i in range(3)], lined_ref.at[pl.ds(pair, 1)], s_ref, ds_ref, acc_ref,
        )
        return 0

    lax.fori_loop(0, 3, one, 0)
    right_ref[3] = attn_ref[:, here]


def last_kernel(
    scalars, act_ref, mix_own, mix_other, right_ref, w_ref, x_ref, lined_ref, other_ref,
    send_ref, keep_ref, part_ref, turned_ref, *rest
):
    plane, core = scalars[0], scalars[1]
    here, there = tile_at(384 * core, 384), tile_at(384 * (1 - core), 384)
    late = (act_ref, mix_own, mix_other, right_ref, w_ref, x_ref)
    copies = [fetch_part(ref, held, rest[-1].at[i]) for i, (ref, held) in enumerate(zip(late, rest[:-1]))]
    act_ref, mix_own, mix_other, right_ref, w_ref, x_ref = rest[:-1]
    for copy in copies:
        copy.wait()
    turned_ref[0] = act_ref[...].astype(full).T.astype(low)
    turned_ref[1, here, :] = mix_own[...].astype(full).T.astype(low)
    turned_ref[1, there, :] = mix_other[...].astype(full).T.astype(low)

    def outer(j, _):
        for odd, out in enumerate((keep_ref, send_ref)):
            quarter = xor(plane, odd * (1 + core) + j * (2 - core))
            out[tile_at(768 * j, 768), :] = mdot(turned_ref[quarter // 3], right_ref[quarter]).astype(low)
        return 0

    lax.fori_loop(0, 2, outer, 0)
    part = ndot(right_ref[0], w_ref[0]) + ndot(right_ref[1], w_ref[1]) + ndot(right_ref[2], w_ref[2])
    part_ref[...] = part
    x_in = x_ref[...].astype(full)
    scale = lax.rsqrt(jnp.mean(x_in * x_in, axis=-1, keepdims=True) + norm_eps)
    gain = jnp.sum(part * x_in * scale, axis=0, keepdims=True)
    lined = jnp.concatenate([lined_ref[0], lined_ref[1], lined_ref[2]], 0)
    table = lax.dot_general(
        lined, hot_buckets(), (((1,), (1,)), ((), ())),
        precision=lax.Precision.HIGHEST, preferred_element_type=full,
    )
    table = jnp.concatenate([table, jnp.zeros((6, 352), full)], 1)
    other = other_ref[...]
    send_ref[1536:1552, :] = jnp.concatenate(
        [gain[:, :384], gain[:, 384:], other[:, :384], other[:, 384:], table, jnp.zeros((6, 384), full)], 0
    ).astype(low)


def wide(value):
    return value.astype(full)


def adam_kernel(join, scalars, master, first, second, own, other, *outs):
    lower = scalars[1] == 0
    left = jnp.where(lower, own[0], other[0]).astype(full)
    right = jnp.where(lower, other[0], own[0]).astype(full)
    grad = join(left, right).reshape(master.shape)
    new_master, new_first, new_second, copy = adam_step(master[...], first[...], second[...], grad, True)
    outs[0][...] = new_master
    outs[1][...] = new_first
    outs[2][...] = copy
    if len(outs) == 4:
        outs[3][...] = new_second
    else:

        @pl.when(pl.program_id(0) < 3)
        def _():
            outs[3][...] = new_second

        @pl.when(pl.program_id(0) == 3)
        def _():
            outs[4][...] = new_second[0]


def adam_call(grid, join, state, quarter_of, states, grads, spot, name, sizes, rows_at, second=None):

    def grad_spec(other):
        def where(*idx):
            scalars = idx[-1]
            core = 1 - scalars[1] if other else scalars[1]
            return (stack_at(xor(scalars[0], quarter_of(*idx[:-1])), core), rows_at, 0)

        return pl.BlockSpec(sizes, where)

    shape = states[0].shape
    kinds = [full, full, low] + ([full] if second is None else [])
    count = functools.reduce(lambda a, b: a * b, shape)
    return pl.pallas_call(
        functools.partial(adam_kernel, join),
        grid_spec=pltpu.PrefetchScalarGridSpec(
            num_scalar_prefetch=1,
            grid=grid,
            in_specs=[state] * 3 + [grad_spec(False), grad_spec(True)],
            out_specs=[state] * len(kinds) + ([] if second is None else second[0]),
        ),
        out_shape=[jax.ShapeDtypeStruct(shape, kind) for kind in kinds]
        + ([] if second is None else second[1]),
        name=name,
        cost_estimate=pl.CostEstimate(flops=0, bytes_accessed=0, transcendentals=0),
    )(spot, *states, *grads)


def body_fast(
    tokens,
    cotangent,
    lengths,
    deal,
    attn_master,
    ffin_master,
    ffout_master,
    gain_master,
    bias_master,
    attn_first,
    ffin_first,
    ffout_first,
    gain_first,
    bias_first,
    attn_second,
    ffin_second,
    ffout_second,
    gain_second,
    bias_second,
):
    plane, core, shard = (lax.axis_index(name) for name in ("plane", "core", "shard"))
    spot = jnp.stack([plane, core, shard])
    group, rest = shard // 2, shard % 2
    mine = group == core

    quarter = call(
        pack_attn_kernel, spot, [[attn_master], [gain_master], [bias_master]], [((208, 384), low)],
        [
            pltpu.VMEM((192, 384), full), pltpu.VMEM((2, 192), full), pltpu.VMEM((8, 12), full),
            pltpu.SemaphoreType.DMA((3,)),
        ],
        "pack_attn", 0, 60,
    )[0]
    attn_came = [across(quarter, step) for step in (1, 2, 3)]

    unit = call(
        pack_ffn_kernel, spot, [[ffin_master], [ffout_master]], [((576, 256), low)],
        [pltpu.VMEM((2, 192, 256), full), pltpu.VMEM((64, 768), full), pltpu.SemaphoreType.DMA((3,))],
        "pack_ffn", 0, 60,
    )[0]
    attn_came = [after(value, unit) for value in attn_came]

    up_pairs = lambda pairs: [((p, 1, z), (p, 1, w)) for p in range(4) for z, w in pairs]
    down_pairs = lambda pairs: [((p, 0, 3 - z), (p, 0, 3 - w)) for p in range(4) for z, w in pairs]
    along = lambda value, *which: send(value, up_pairs(which) + down_pairs(which))

    def fetch_rest(own, one, gate=None):
        two = along(one, (1, 2), (2, 3))
        two = two if gate is None else after(two, gate)
        three = along(jnp.where(at_end, own, two), (2, 3), (3, 2))
        return own, one, two, three

    way = 1 - 2 * core
    at_end = shard == 3 * core
    blocks = jnp.stack(
        [shard, shard + way, shard + 2 * way, jnp.where(at_end, shard + 3 * way, shard - way)]
    )
    blocks = jnp.clip(blocks, 0, 3)
    tok_blocks = fetch_rest(tokens[0], along(tokens[0], (0, 1), (1, 2), (2, 3)))

    table_own = jnp.concatenate([lengths[0], deal[0]])
    table = jnp.where(mine, table_own, swap(table_own))
    lens, order = table[:4], table[4:]
    starts = jnp.cumsum(lens) - lens
    long_start = jnp.sum(jnp.where(lens == 512, starts, 0))
    at_half = jnp.arange(512, dtype=jnp.int32)
    token_here = jnp.where(rest == 0, long_start + at_half, at_half + 512 * (at_half >= long_start))
    seg_here = jnp.sum((token_here[:, None] >= starts[None, :]).astype(jnp.int32), axis=1)
    token_index = jnp.arange(1024, dtype=jnp.int32)

    token_column = token_here[:, None]
    token_row = jnp.where(mine, token_here, -1)[None, :]

    def wanted_by(place_of):
        rows = [lax.dynamic_slice_in_dim(place_of, 256 * xor(shard, step), 256) for step in range(4)]
        return jnp.concatenate(rows).reshape(1024, 1)

    wanted_y = wanted_by(order)
    wanted_x = wanted_by(token_index)

    def rows_here(place_of, pieces, gate=None):
        place = [lax.dynamic_slice_in_dim(place_of, blocks[i] * 256, 256) for i in range(4)]
        place = jnp.concatenate(place).reshape(1, 1024)
        chosen = call(
            pick_kernel, spot, [*pieces, after(place, wanted_y, wanted_x, token_row), token_column], [((512, 768), low)], [], "pick", 0, 8
        )[0]
        chosen = chosen if gate is None else after(chosen, *gate)
        return jnp.where(mine, chosen, swap(chosen))

    def rows_back(rows, first_gate, second_gate):
        pairs = lambda step: [((p, c, z), (p, c, z ^ step)) for p, c, z in ALL if z // 2 == c]
        near, own, far = rows
        came = after(send(near, pairs(1)), first_gate)
        far = call(add_kernel, spot, [far, came], [((256, 768), low)], [], "add_rows", 0, 4)[0]
        last = after(send(far, pairs(2)), second_gate)
        return own + came[:256] + last, last


    gains, vectors = call(
        unpack_kernel, spot, [quarter, *attn_came], [((2, 768), full), ((3, 2, 1024), full)],
        [pltpu.VMEM((32, 12), full)], "unpack", 0, 8,
    )

    def spread_plane(pieces, rows, gate=None, late=None):
        near = cat(spot, pieces, rows, "near")
        arrived = plane_first(near)
        if gate is not None:
            arrived = after(arrived, gate)
        near = cat(spot, [near, arrived], rows, "nearest")
        return near, plane_second(near if late is None else after(near, late))

    unit = after(unit, *attn_came)
    ffn_came = [across(unit, step) for step in (1, 2, 3)]
    attn_came = [after(value, ffn_came[0]) for value in attn_came]
    near, far = spread_plane(attn_came, 192, ffn_came[1])
    x_low = rows_here(token_index, tok_blocks, (far, *ffn_came))
    w_attn, act_one, query, key, value = call(
        project_kernel, spot,
        [x_low, gains, [attn_master], (near,), (far,)],
        [((4, 768, 384), low), ((512, 768), low)] + [((512, 384), low)] * 3,
        [pltpu.VMEM((4, 192, 384), full), pltpu.SemaphoreType.DMA((13,))], "project", 0, 60,
    )
    wo_other = swap(w_attn[3])


    ffn_near, ffn_far = spread_plane(ffn_came, 576, query)
    cot_own = after(cotangent[0], *ffn_came)
    cot_one = after(along(cot_own, (0, 1), (1, 2), (2, 3)), query)
    cot_two = along(cot_one, (1, 2), (2, 3))
    mix_own, probs = call(
        attend_all_kernel, spot, [after(query, ffn_near, cot_two), key, value, seg_here[:, None], seg_here[None, :], vectors],
        [((512, 384), low), ((6, 512, 512), low)],
        [pltpu.VMEM((512, 512), full), pltpu.VMEM((6, 512, 512), low), pltpu.SemaphoreType.DMA((3,))],
        "attend", 0, 60, (1,),
    )
    cot_three = after(along(jnp.where(at_end, cot_own, cot_two), (2, 3), (3, 2)), mix_own)
    cot_blocks = (cot_own, cot_one, cot_two, cot_three)
    grad_y = rows_here(order, cot_blocks)
    mix_other = swap(mix_own)
    x_mid, act_two, hidden, part_two, y_part, grads_up = call(
        feed_kernel, spot,
        [
            x_low, mix_own, mix_other, w_attn, wo_other, gains, grad_y, ffin_master, [ffout_master],
            (ffn_near,), (ffn_far,),
        ],
        [
            ((512, 768), full), ((512, 768), low), ((512, 1024), low), ((512, 768), full), ((512, 768), full),
            ((4, 512, 512), low),
        ],
        [
            pltpu.VMEM((512, 768), low), pltpu.VMEM((768, 768), low), pltpu.VMEM((2, 768, 1024), low),
            pltpu.VMEM((1024, 768), low), pltpu.VMEM((256, 768), full), pltpu.VMEM((512, 1024), full),
            pltpu.VMEM((512, 1024), full), pltpu.SemaphoreType.DMA((61,)),
        ],
        "feed", 0, 24,
    )
    ffn_send, ffn_keep = call(
        outer_kernel, spot, [act_two, grads_up, hidden, grad_y], [((4608, 256), low)] * 2,
        [pltpu.VMEM((768, 512), low), pltpu.VMEM((256, 768), full)], "outer", 0, 12,
    )
    part_other = after(swap(part_two), ffn_send)
    ffn_first = plane_first(ffn_send)

    y_other = swap(after(y_part, part_other))
    y_rows = call(
        spread_y_kernel, spot, [(x_mid,), (y_part,), (y_other,), wanted_y, token_row],
        [((512, 768), low), ((256, 768), low), ((256, 768), low)],
        [pltpu.VMEM((512, 768), low), *[pltpu.VMEM((512, 768), full)] * 3, pltpu.SemaphoreType.DMA((3,))],
        "spread_y", 0, 60,
    )
    grad_mid, right, lined, gain_two = call(
        back_kernel, spot,
        [
            (after(part_two, *y_rows),), (part_other,), (x_mid,), (grad_y,), gains, (w_attn,), (wo_other,),
            (query,), (key,), (value,), (probs,),
        ],
        [
            ((512, 768), full), ((4, 512, 384), low), ((3, 2, 1024), full), ((1, 768), full),
        ],
        [
            pltpu.VMEM((512, 768), low), pltpu.VMEM((512, 384), low), pltpu.VMEM((512, 512), full), pltpu.VMEM((512, 512), low),
            pltpu.VMEM((128, 1024), full), *[pltpu.VMEM((512, 768), full)] * 3, pltpu.VMEM((512, 768), low),
            *[pltpu.VMEM((768, 384), low)] * 2, *[pltpu.VMEM((512, 384), low)] * 3, pltpu.VMEM((6, 512, 512), low),
            pltpu.SemaphoreType.DMA((10,)),
        ],
        "back", 0, 60,
    )
    ffn_first = after(ffn_first, right)
    one_out = lambda kernel, inputs, shape, name: call(kernel, spot, inputs, [(shape, low)], [], name, 0, 8)[0]
    ffn_passed = one_out(pass_ffn_kernel, [ffn_keep, ffn_first], (2304, 256), "pass_ffn")
    ffn_second = plane_second(ffn_passed)
    attn_send, attn_keep, part_one = call(
        last_kernel, spot,
        [
            (after(act_one, ffn_passed),), (mix_own,), (mix_other,), (right,), (w_attn,), (x_low,), lined, gain_two,
        ],
        [((1552, 384), low), ((1536, 384), low), ((512, 768), full)],
        [
            pltpu.VMEM((2, 768, 512), low), pltpu.VMEM((512, 768), low), *[pltpu.VMEM((512, 384), low)] * 2,
            pltpu.VMEM((4, 512, 384), low), pltpu.VMEM((4, 768, 384), low), pltpu.VMEM((512, 768), low),
            pltpu.SemaphoreType.DMA((6,)),
        ],
        "last", 0, 60,
    )
    layer_out, y_last = rows_back(y_rows, right, part_one)
    ffn_second = after(ffn_second, part_one, y_last)
    x_rows = call(
        spread_x_kernel, spot,
        [(part_one,), (swap(part_one),), (x_low,), gains, (grad_mid,), wanted_x, token_row],
        [((512, 768), low), ((256, 768), low), ((256, 768), low)],
        [
            pltpu.VMEM((512, 768), low), *[pltpu.VMEM((512, 768), full)] * 3, pltpu.VMEM((512, 768), low),
            pltpu.SemaphoreType.DMA((4,)),
        ],
        "spread_x", 0, 60,
    )
    ffn_own, *ffn_outs = call(
        sum_ffn_kernel, spot, [ffn_keep, ffn_first, ffn_second],
        [((576, 256), full)] + [((576, 256), low)] * 3, [], "sum_ffn", 0, 8,
    )
    ffn_came = [across(out, step) for step, out in zip((1, 2, 3), ffn_outs)]
    attn_first_came = after(plane_first(after(attn_send, ffn_second)), *ffn_came[:2], *x_rows)
    passed = one_out(pass_attn_kernel, [attn_keep, attn_send, attn_first_came], (784, 384), "pass_attn")
    attn_second_came = plane_second(passed)
    attn_own, *attn_outs = call(
        sum_attn_kernel, spot, [attn_keep, passed, attn_first_came, attn_second_came],
        [((208, 384), full)] + [((208, 384), low)] * 3, [], "sum_attn", 0, 8,
    )
    ffn_came = [after(value, attn_second_came) for value in ffn_came]
    attn_outs = [across(out, step) for step, out in zip((1, 2, 3), attn_outs)]
    ffn_sum = one_out(total_kernel, [ffn_own, *ffn_came], (576, 256), "total_ffn")
    ffn_pair = cat(spot, [ffn_sum, after(plane_first(ffn_sum), attn_outs[0])], 576, "pair_ffn")
    ffn_stack = cat(spot, [ffn_pair, after(plane_second(ffn_pair), attn_outs[1], attn_outs[2])], 576, "stack_ffn")
    ffn_sum = (ffn_stack, swap(ffn_stack))
    ffout_state = pl.BlockSpec((2, 1, 64, 768), lambda q, s: (0, q, 0, 0))
    unfold = lambda value: jnp.concatenate([value[:64], value[64:128], value[128:]], 1)
    ffout_res = adam_call(
        (4,), lambda left, right: jnp.stack([unfold(left), unfold(right)]), ffout_state, lambda q: q,
        [state.reshape(2, 4, 64, 768) for state in (ffout_master, ffout_first, ffout_second)],
        ffn_sum, spot, "adam_ffout", (1, 192, 256), 2,
    )
    ffout_res = [value.reshape(512, 768) for value in ffout_res]
    ffin_res = adam_call(
        (2, 2),
        lambda left, right: jnp.concatenate(
            [left[:192], right[:192], left[192:], right[192:]], 1
        ),
        pl.BlockSpec((1, 192, 1024), lambda i, h, s: (i, 0, h)), lambda i, h: 2 * i + h,
        [ffin_master, ffin_first, ffin_second], ffn_sum, spot, "adam_ffin", (1, 384, 256), 0,
    )
    attn_outs = [after(value, ffn_stack) for value in attn_outs]
    attn_sum, small = call(
        total_kernel, spot, [attn_own, *attn_outs], [((192, 384), low), ((16, 384), full)], [], "total_attn", 0, 8
    )
    attn_near = cat(spot, [attn_sum, after(plane_first(attn_sum), ffin_res[0])], 192, "pair_attn")
    attn_stack = cat(spot, [attn_near, after(plane_second(attn_near), ffout_res[0])], 192, "stack_attn")
    attn_sum = (attn_stack, swap(attn_stack))
    x_rows = [after(value, small) for value in x_rows]
    input_grad, _ = rows_back(x_rows, ffin_res[0], ffout_res[0])
    small_other = swap(small)
    gain_sum = (small[:4] + small_other[:4]).reshape(2, 768)
    g_gain = lax.dynamic_slice_in_dim(gain_sum, shard * 192, 192, 1)
    g_bias = both_cores(small[4:10, :32], small_other[4:10, :32], core, 0)
    g_bias = lax.dynamic_slice_in_dim(g_bias, shard * 8, 8, 1).T

    attn_res = adam_call(
        (4,), lambda left, right: jnp.concatenate([left, right], 1),
        pl.BlockSpec((1, 192, 768), lambda m, s: (m, 0, 0)), lambda m: m,
        [attn_master, attn_first, attn_second], attn_sum, spot, "adam_attn", (1, 192, 384), 0,
        (
            [
                pl.BlockSpec((1, 192, 768), lambda m, s: (jnp.minimum(m, 2), 0, 0)),
                pl.BlockSpec((192, 768), lambda m, s: (0, 0)),
            ],
            [jax.ShapeDtypeStruct((3, 192, 768), full), jax.ShapeDtypeStruct((192, 768), full)],
        ),
    )
    gain_res = adam_step(gain_master, gain_first, gain_second, g_gain, False)
    bias_res = adam_step(bias_master, bias_first, bias_second, g_bias, False)
    return (
        layer_out[None],
        input_grad[None],
        attn_res[0],
        ffin_res[0],
        ffout_res[0],
        gain_res[0] - gain_master,
        bias_res[0] - bias_master,
        attn_res[1],
        ffin_res[1],
        ffout_res[1],
        gain_res[1],
        bias_res[1],
        attn_res[3],
        attn_res[4],
        ffin_res[3],
        ffout_res[3],
        gain_res[2],
        bias_res[2],
        attn_res[2],
        ffin_res[2],
        ffout_res[2],
    )


def body_any(
    tokens,
    cotangent,
    lengths,
    deal,
    attn_master,
    ffin_master,
    ffout_master,
    gain_master,
    bias_master,
    attn_first,
    ffin_first,
    ffout_first,
    gain_first,
    bias_first,
    attn_second,
    ffin_second,
    ffout_second,
    gain_second,
    bias_second,
):
    shards = lax.axis_size("shard")
    core = lax.axis_index("core")
    shard = lax.axis_index("shard")
    tok_rows, model = tokens.shape[1], tokens.shape[2]
    heads = bias_master.shape[1]
    own_heads = heads // 2
    part = model // 2
    whole_len = tok_rows * shards
    half_len = whole_len // 2
    per_half = shards // 4
    rows = half_len // per_half
    place, sub = shard // per_half, shard % per_half
    group, rest = place // 2, place % 2
    mine = group == core
    siblings = [[a * per_half + b for b in range(per_half)] for a in range(4)]

    def join_half(value):
        if per_half == 1:
            return value
        return lax.all_gather(value, "shard", axis=0, tiled=True, axis_index_groups=siblings)

    table_own = jnp.concatenate([lengths[0], deal[0]])
    table = jnp.where(mine, table_own, swap(table_own))
    count = lengths.shape[1]
    lens, order = table[:count], table[count:]
    starts = jnp.cumsum(lens) - lens
    long_start = jnp.sum(jnp.where(lens == half_len, starts, 0))
    at_half = jnp.arange(half_len, dtype=jnp.int32)
    token_half = jnp.where(
        rest == 0, long_start + at_half, at_half + half_len * (at_half >= long_start)
    )
    seg_half = jnp.sum((token_half[:, None] >= starts[None, :]).astype(jnp.int32), axis=1)
    first_row = sub * rows
    token_here = lax.dynamic_slice_in_dim(token_half, first_row, rows)
    seg_here = lax.dynamic_slice_in_dim(seg_half, first_row, rows)

    def rows_here(place_of, own):
        gathered = lax.all_gather(own, "shard", axis=0, tiled=True)
        gathered = jnp.where(mine, gathered, swap(gathered))
        picked = (place_of[None, :] == token_here[:, None]).astype(low)
        return mdot(picked, gathered).astype(low)

    def rows_back(place_of, here):
        picked = (place_of[:, None] == token_here[None, :]) & mine
        spread = mdot(picked.astype(low), here).astype(low)
        return lax.psum_scatter(spread, "shard", scatter_dimension=0, tiled=True)

    ff_rows = ffout_master.shape[0]
    ff_part = ff_rows // 2
    attn_low = attn_master.astype(low)
    cols = lax.dynamic_slice_in_dim(attn_low[:3], core * part, part, 2)
    ffin_low = ffin_master.astype(low).reshape(2, -1, shards, 2, ff_part)
    ffin_low = lax.dynamic_index_in_dim(ffin_low, core, 3, keepdims=False)
    ffin_low = ffin_low.reshape(2, -1, shards * ff_part)
    ffout_low = lax.dynamic_slice_in_dim(ffout_master.astype(low), core * ff_part, ff_part, 0)
    w_qkv = lax.all_gather(cols, "shard", axis=1, tiled=True)
    w_o = lax.all_gather(attn_low[3], "shard", axis=0, tiled=True)
    w_in = lax.all_gather(ffin_low, "shard", axis=1, tiled=True)
    w_out = lax.all_gather(ffout_low, "shard", axis=0, tiled=True)
    gains = lax.all_gather(gain_master.astype(low), "shard", axis=1, tiled=True).astype(full)
    bias = lax.all_gather(bias_master.astype(low), "shard", axis=0, tiled=True).astype(full)

    token_index = jnp.arange(whole_len, dtype=jnp.int32)
    x_low = rows_here(token_index, tokens[0])
    grad_y = rows_here(order, cotangent[0])

    x_in = x_low.astype(full)
    scale_one = lax.rsqrt(jnp.mean(x_in * x_in, axis=-1, keepdims=True) + norm_eps)
    act_one = (x_in * scale_one * gains[0]).astype(low)
    query = mdot(act_one, w_qkv[0]).astype(low)
    key_own = mdot(act_one, w_qkv[1]).astype(low)
    value_own = mdot(act_one, w_qkv[2]).astype(low)
    key, value = join_half(key_own), join_half(value_own)
    span = rows + half_len
    relative = jnp.arange(span, dtype=jnp.int32) - rows - first_row
    ids = jnp.arange(bias.shape[0], dtype=jnp.int32)
    one_hot = (bucket_of(relative)[None, :] == ids[:, None]).astype(full)
    bias_own = lax.dynamic_slice_in_dim(bias, core * own_heads, own_heads, 1)
    vectors = lax.dot_general(
        bias_own, one_hot, (((0,), (0,)), ((), ())), precision=lax.Precision.HIGHEST
    )
    mix_own, probs = attend(
        query, key, value, seg_here[:, None], seg_half[None, :], vectors
    )
    mix = both_cores(mix_own, swap(mix_own), core, 1)
    x_mid = x_in + mdot(mix, w_o)
    scale_two = lax.rsqrt(jnp.mean(x_mid * x_mid, axis=-1, keepdims=True) + norm_eps)
    act_two = (x_mid * scale_two * gains[1]).astype(low)
    gate_pre = mdot(act_two, w_in[0])
    up_pre = mdot(act_two, w_in[1])
    gated, gelu_pull = jax.vjp(
        lambda gate_val, up_val: jax.nn.gelu(gate_val, approximate=True) * up_val, gate_pre, up_pre
    )
    hidden = gated.astype(low)
    y_part = mdot(hidden, w_out)
    y_here = (x_mid + y_part + swap(y_part)).astype(low)
    layer_out = rows_back(order, y_here)

    grad_gate, grad_up = gelu_pull(ndot(grad_y, w_out))
    grad_gate, grad_up = grad_gate.astype(low), grad_up.astype(low)
    d_out = tdot(hidden, grad_y).astype(low)
    d_in = jnp.stack([tdot(act_two, grad_gate), tdot(act_two, grad_up)]).astype(low)
    part_two = ndot(grad_gate, w_in[0]) + ndot(grad_up, w_in[1])
    grad_act_two = part_two + swap(part_two)
    turned = grad_act_two * gains[1]
    grad_mid = (
        grad_y.astype(full)
        + scale_two * turned
        - x_mid * scale_two**3 * jnp.mean(turned * x_mid, axis=-1, keepdims=True)
    )
    d_gain_two = jnp.sum(grad_act_two * x_mid * scale_two, axis=0)
    grad_attn = grad_mid.astype(low)
    w_o_own = lax.dynamic_slice_in_dim(w_o, core * part, part, 0)
    grad_mix = ndot(grad_attn, w_o_own).astype(low)
    d_wo = tdot(mix, lax.dynamic_slice_in_dim(grad_attn, core * part, part, 1)).astype(low)
    grad_q, grad_k, grad_v, diagonals = attend_back(query, key, value, grad_mix, probs, span)
    if per_half > 1:
        grad_k = lax.psum_scatter(
            grad_k, "shard", scatter_dimension=0, tiled=True, axis_index_groups=siblings
        )
        grad_v = lax.psum_scatter(
            grad_v, "shard", scatter_dimension=0, tiled=True, axis_index_groups=siblings
        )
    d_wq = tdot(act_one, grad_q).astype(low)
    d_wk = tdot(act_one, grad_k).astype(low)
    d_wv = tdot(act_one, grad_v).astype(low)
    part_one = ndot(grad_q, w_qkv[0]) + ndot(grad_k, w_qkv[1]) + ndot(grad_v, w_qkv[2])
    grad_act_one = part_one + swap(part_one)
    turned = grad_act_one * gains[0]
    grad_x = (
        grad_mid
        + scale_one * turned
        - x_in * scale_one**3 * jnp.mean(turned * x_in, axis=-1, keepdims=True)
    ).astype(low)
    d_gain_one = jnp.sum(grad_act_one * x_in * scale_one, axis=0)
    input_grad = rows_back(token_index, grad_x)

    lined = diagonals.reshape(own_heads, span)
    table_own = lax.dot_general(
        one_hot, lined, (((1,), (1,)), ((), ())), precision=lax.Precision.HIGHEST
    )
    empty = jnp.zeros_like(table_own)
    grad_table = jnp.where(
        core == 0,
        jnp.concatenate([table_own, empty], 1),
        jnp.concatenate([empty, table_own], 1),
    )
    grad_gain = jnp.where(core == 0, jnp.stack([d_gain_one, d_gain_two]), 0.0)

    d_attn = jnp.stack([d_wq, d_wk, d_wv, d_wo])

    def reduced(grad, axis):
        share = lax.psum_scatter(grad, "shard", scatter_dimension=axis, tiled=True)
        return lax.psum(share, "plane")

    g_attn = reduced(d_attn, 1)
    g_attn = both_cores(g_attn, swap(g_attn), core, 2).astype(full)
    g_in = reduced(d_in, 1)
    g_in = g_in.reshape(2, -1, shards, 1, ff_part)
    g_in = both_cores(g_in, swap(g_in), core, 3).reshape(ffin_master.shape).astype(full)
    g_out = reduced(d_out, 0)
    g_out = both_cores(g_out, swap(g_out), core, 0).astype(full)
    g_gain, g_bias = lax.psum((grad_gain, grad_table), ("plane", "core", "shard"))
    own_gain = gain_master.shape[1]
    g_gain = lax.dynamic_slice_in_dim(g_gain, shard * own_gain, own_gain, 1)
    own_bias = bias_master.shape[0]
    g_bias = lax.dynamic_slice_in_dim(g_bias, shard * own_bias, own_bias, 0)

    attn_res = adam_step(attn_master, attn_first, attn_second, g_attn, True)
    ffin_res = adam_step(ffin_master, ffin_first, ffin_second, g_in, True)
    ffout_res = adam_step(ffout_master, ffout_first, ffout_second, g_out, True)
    gain_res = adam_step(gain_master, gain_first, gain_second, g_gain, False)
    bias_res = adam_step(bias_master, bias_first, bias_second, g_bias, False)
    return (
        layer_out[None],
        input_grad[None],
        attn_res[0],
        ffin_res[0],
        ffout_res[0],
        gain_res[0] - gain_master,
        bias_res[0] - bias_master,
        attn_res[1],
        ffin_res[1],
        ffout_res[1],
        gain_res[1],
        bias_res[1],
        attn_res[2][:3],
        attn_res[2][3],
        ffin_res[2],
        ffout_res[2],
        gain_res[2],
        bias_res[2],
        attn_res[3],
        ffin_res[3],
        ffout_res[3],
    )


def solution(mesh):
    reps, shards = mesh.devices.shape
    cores = Mesh(mesh.devices.reshape(reps // 2, 2, shards), ("plane", "core", "shard"))
    rep = ("plane", "core")
    tok = P(rep, "shard", None)
    row = P(rep, None)
    second = P(None, "shard", None)
    first = P("shard", None)
    gain = P(None, "shard")
    states = (second, second, first, gain, first)
    in_specs = (tok, tok, row, row) + states * 3
    out_specs = (
        (tok, tok) + states + states + (second, first, second, first, gain, first) + states[:3]
    )
    body = body_fast if (reps, shards) == (8, 4) else body_any
    return jax.shard_map(body, mesh=cores, in_specs=in_specs, out_specs=out_specs, check_vma=False)
```

```python
import functools

import jax
import jax.numpy as jnp
from jax import lax
from jax.experimental import pallas as pl
from jax.experimental.pallas import tpu as pltpu
from jax.sharding import Mesh
from jax.sharding import PartitionSpec as P

norm_eps = 1e-06
far_below = -1e30
steps_beyond = (12, 16, 23, 32, 46, 64, 91)
first_rate = 0.9
second_rate = 0.95
learning = 0.05
shrink = 0.1
adam_eps = 1e-08
first_fix = 1.0 - 0.9**8
second_fix = 1.0 - 0.95**8
chips = ("plane", "shard")
low = jnp.bfloat16
full = jnp.float32


def bucket_of(relative):
    distance = jnp.abs(relative)
    beyond = 8 + sum(((distance >= threshold).astype(jnp.int32) for threshold in steps_beyond))
    near_part = jnp.where(distance < 8, distance, beyond)
    return near_part + 16 * (relative > 0).astype(jnp.int32)


def ndot(left, right):
    return lax.dot_general(left, right, (((1,), (1,)), ((), ())), preferred_element_type=full)


def tdot(left, right):
    return lax.dot_general(left, right, (((0,), (0,)), ((), ())), preferred_element_type=full)


def mdot(left, right):
    return jnp.dot(left, right, preferred_element_type=full)


def swap(value):
    return lax.ppermute(value, "core", [(0, 1), (1, 0)])


def both_cores(mine, other, core, axis):
    first = jnp.where(core == 0, mine, other)
    second = jnp.where(core == 0, other, mine)
    return jnp.concatenate([first, second], axis)


def adam_step(master, first, second, grad, decayed):
    new_first = first_rate * first + (1.0 - first_rate) * grad
    new_second = second_rate * second + (1.0 - second_rate) * grad * grad
    update = new_first / first_fix / (jnp.sqrt(new_second / second_fix) + adam_eps)
    if decayed:
        update = update + shrink * master
    new_master = master - learning * update
    return (new_master, new_first, new_second, new_master.astype(low))


def toeplitz_of(vector_row):
    wide = jnp.broadcast_to(vector_row, (128, vector_row.shape[1]))
    return pltpu.roll(wide, 0, 1, stride=1, stride_axis=0)


def attend_kernel(rows, q_ref, k_ref, v_ref, qseg_ref, kseg_ref, vec_ref, o_ref, p_ref, s_ref):
    keys = k_ref.shape[0]
    lane = lax.broadcasted_iota(jnp.int32, (rows, 128), 1)
    parts = []
    for head in range(2):
        mine = (lane < 64) if head == 0 else (lane >= 64)
        q_head = jnp.where(mine, q_ref[...], jnp.zeros((), low))
        s_ref[...] = ndot(q_head, k_ref[...])
        table = toeplitz_of(vec_ref[0, head : head + 1, :])
        for blk in range(rows // 128):
            here = slice(128 * blk, 128 * blk + 128)
            at = rows - 128 * blk
            scores = s_ref[here, :] + table[:, at : at + keys]
            scores = jnp.where(qseg_ref[here, :] == kseg_ref[...], scores, far_below)
            highest = jnp.max(scores, axis=1, keepdims=True)
            raised = jnp.exp(scores - highest)
            total = jnp.sum(raised, axis=1, keepdims=True)
            p_ref[head, here, :] = (raised * (1.0 / total)).astype(low)
        parts.append(mdot(p_ref[head], v_ref[...]))
    o_ref[...] = jnp.where(lane < 64, parts[0], parts[1]).astype(low)


def attend_back_kernel(
    rows, q_ref, k_ref, v_ref, do_ref, p_ref, dq_ref, dk_ref, dv_ref, diag_ref, s_ref, ds_ref, acc_ref
):
    keys = k_ref.shape[0]
    lane = lax.broadcasted_iota(jnp.int32, (rows, 128), 1)
    q_turned = q_ref[...].astype(full).T.astype(low)
    do_turned = do_ref[...].astype(full).T.astype(low)
    dq_parts, dk_parts, dv_parts = [], [], []
    for head in range(2):
        mine = (lane < 64) if head == 0 else (lane >= 64)
        do_head = jnp.where(mine, do_ref[...], jnp.zeros((), low))
        s_ref[...] = ndot(do_head, v_ref[...])
        acc_ref[...] = jnp.zeros_like(acc_ref)
        for blk in range(rows // 128):
            here = slice(128 * blk, 128 * blk + 128)
            at = rows - 128 * blk
            prob = p_ref[head, here, :].astype(full)
            grad = s_ref[here, :]
            delta = jnp.sum(prob * grad, axis=1, keepdims=True)
            dscore = (prob * (grad - delta)).astype(low)
            ds_ref[here, :] = dscore
            acc_ref[:, at : at + keys] += dscore.astype(full)
        dq_parts.append(mdot(ds_ref[...], k_ref[...]))
        own = slice(64 * head, 64 * head + 64)
        dk_parts.append(mdot(q_turned[own, :], ds_ref[...]))
        dv_parts.append(mdot(do_turned[own, :], p_ref[head]))
        summed = acc_ref[...]
        count = 128
        while count > 8:
            count //= 2
            width = summed.shape[1]
            summed = summed[:count] + pltpu.roll(summed[count:], width - count, 1)
        row = lax.broadcasted_iota(jnp.int32, summed.shape, 0)
        for bit in (1, 2, 4):
            turned = pltpu.roll(summed, summed.shape[1] - bit, 1)
            summed = jnp.where(jnp.bitwise_and(row, bit) > 0, turned, summed)
        diag_ref[0, head : head + 1, :] = jnp.sum(summed, axis=0, keepdims=True)
    dq_ref[...] = jnp.where(lane < 64, dq_parts[0], dq_parts[1]).astype(low)
    dk_ref[...] = jnp.concatenate(dk_parts, 0).T.astype(low)
    dv_ref[...] = jnp.concatenate(dv_parts, 0).T.astype(low)


def attend(query, key, value, query_seg, key_seg, vectors):
    rows, width = query.shape
    keys = key.shape[0]
    pairs = width // 128
    span = vectors.shape[-1]
    tall = pl.BlockSpec((rows, 128), lambda i: (0, i))
    wide = pl.BlockSpec((keys, 128), lambda i: (0, i))
    return pl.pallas_call(
        functools.partial(attend_kernel, rows),
        grid=(pairs,),
        in_specs=[
            tall,
            wide,
            wide,
            pl.BlockSpec((rows, 1), lambda i: (0, 0)),
            pl.BlockSpec((1, keys), lambda i: (0, 0)),
            pl.BlockSpec((1, 2, span), lambda i: (i, 0, 0)),
        ],
        out_specs=[tall, pl.BlockSpec((2, rows, keys), lambda i: (i, 0, 0))],
        out_shape=[
            jax.ShapeDtypeStruct((rows, width), low),
            jax.ShapeDtypeStruct((2 * pairs, rows, keys), low),
        ],
        scratch_shapes=[pltpu.VMEM((rows, keys), full)],
        name="attend",
        cost_estimate=pl.CostEstimate(
            flops=8 * pairs * rows * keys * 128,
            bytes_accessed=4 * pairs * rows * keys,
            transcendentals=2 * pairs * rows * keys,
        ),
    )(query, key, value, query_seg, key_seg, vectors.reshape(pairs, 2, span))


def attend_back(query, key, value, grad_out, probs, span):
    rows, width = query.shape
    keys = key.shape[0]
    pairs = width // 128
    tall = pl.BlockSpec((rows, 128), lambda i: (0, i))
    wide = pl.BlockSpec((keys, 128), lambda i: (0, i))
    return pl.pallas_call(
        functools.partial(attend_back_kernel, rows),
        grid=(pairs,),
        in_specs=[tall, wide, wide, tall, pl.BlockSpec((2, rows, keys), lambda i: (i, 0, 0))],
        out_specs=[tall, wide, wide, pl.BlockSpec((1, 2, span), lambda i: (i, 0, 0))],
        out_shape=[
            jax.ShapeDtypeStruct((rows, width), low),
            jax.ShapeDtypeStruct((keys, width), low),
            jax.ShapeDtypeStruct((keys, width), low),
            jax.ShapeDtypeStruct((pairs, 2, span), full),
        ],
        scratch_shapes=[
            pltpu.VMEM((rows, keys), full),
            pltpu.VMEM((rows, keys), low),
            pltpu.VMEM((128, span), full),
        ],
        name="attend_back",
        cost_estimate=pl.CostEstimate(
            flops=20 * pairs * rows * keys * 128,
            bytes_accessed=4 * pairs * rows * keys,
            transcendentals=0,
        ),
    )(query, key, value, grad_out, probs)


def xor(left, right):
    return jnp.bitwise_xor(left, right)


def by_shard(value, shard):
    pairs = value.reshape((2, 2) + value.shape[1:])
    pairs = jnp.where(shard % 2 == 1, pairs[:, ::-1], pairs)
    return jnp.where(shard // 2 == 1, pairs[::-1], pairs).reshape(value.shape)


def after(value, *others):
    return lax.optimization_barrier((value,) + others)[0]


def send(value, pairs):
    return lax.ppermute(
        value,
        ("plane", "core", "shard"),
        [((p * 2 + c) * 4 + z, (q * 2 + d) * 4 + w) for (p, c, z), (q, d, w) in pairs],
    )


ALL = [(p, c, z) for p in range(4) for c in range(2) for z in range(4)]


def plane_first(value):
    return send(value, [((p, c, z), (p ^ (1 + c), c, z)) for p, c, z in ALL])


def plane_second(value):
    return send(value, [((p, c, z), (p ^ (2 - c), c, z)) for p, c, z in ALL])


def across(value, step):
    return send(value, [((p, c, z), (p, c, z ^ step)) for p, c, z in ALL])


def turns(core):
    return (0, 1 + core, 2 - core, 3)


def stack_at(turn, core):
    return jnp.where((core == 1) & ((turn == 1) | (turn == 2)), 3 - turn, turn)


def tile_at(start, size):
    return pl.ds(pl.multiple_of(start, size), size)


vmem = pl.BlockSpec(memory_space=pltpu.VMEM)
anywhere = pl.BlockSpec(memory_space=pl.ANY)
fixed = pl.BlockSpec(memory_space=pltpu.HBM)


def call(kernel, spot, inputs, outputs, scratch, name, flops=0, grant=16, loose=()):
    arrays = [item[0] if isinstance(item, (tuple, list)) else item for item in inputs]
    specs = [
        anywhere if isinstance(item, tuple) else fixed if isinstance(item, list) else vmem for item in inputs
    ]
    return pl.pallas_call(
        kernel,
        in_specs=[pl.BlockSpec(memory_space=pltpu.SMEM)] + specs,
        out_specs=[anywhere if i in loose else vmem for i in range(len(outputs))],
        scratch_shapes=scratch,
        out_shape=[jax.ShapeDtypeStruct(shape, kind) for shape, kind in outputs],
        name=name,
        cost_estimate=pl.CostEstimate(flops=0, bytes_accessed=0, transcendentals=0),
        compiler_params=pltpu.CompilerParams(vmem_limit_bytes=grant << 20),
    )(spot, *arrays)


def fetch_part(source, target, sem):
    copy = pltpu.make_async_copy(source, target, sem)
    copy.start()
    return copy


def bring(pieces, near_ref, far_ref, sems, scalars):
    plane, core, shard = scalars[0], scalars[1], scalars[2]
    copies = []
    for k, turn in enumerate(turns(core)):
        quarter = xor(plane, turn)
        for step in (1, 2, 3):
            source = (near_ref, far_ref)[k // 2].at[3 * (k % 2) + step - 1]
            for part, target in pieces(source, quarter, xor(shard, step)):
                copies.append(fetch_part(part, target, sems.at[len(copies)]))
    return copies


def attend_all_kernel(scalars, q_ref, k_ref, v_ref, qseg_ref, kseg_ref, vec_ref, o_ref, p_out, s_ref, p_ref, sems):
    def leave(pair):
        here = pl.ds(2 * pair, 2)
        return pltpu.make_async_copy(p_ref.at[here], p_out.at[here], sems.at[pair])

    def one(pair, _):
        lanes = tile_at(128 * pair, 128)
        attend_kernel(
            512, q_ref.at[:, lanes], k_ref.at[:, lanes], v_ref.at[:, lanes], qseg_ref, kseg_ref,
            vec_ref.at[pl.ds(pair, 1)], o_ref.at[:, lanes], p_ref.at[pl.ds(2 * pair, 2)], s_ref,
        )
        leave(pair).start()
        return 0

    lax.fori_loop(0, 3, one, 0)
    for pair in range(3):
        leave(pair).wait()


def hot_buckets():
    relative = lax.broadcasted_iota(jnp.int32, (32, 1024), 1) - 512
    return jnp.where(bucket_of(relative) == lax.broadcasted_iota(jnp.int32, (32, 1024), 0), 1.0, 0.0)


def unpack_kernel(scalars, r0, pair, r3, gain_ref, vec_ref, bias_ref):
    core, shard = scalars[1], scalars[2]
    for z in range(4):
        rows = jnp.zeros((16, 384), full)
        for step, ref in enumerate((r0, pair.at[0], pair.at[1], r3)):
            rows = rows + jnp.where(xor(shard, step) == z, ref[192:208, :].astype(full), 0.0)
        gain_ref[:, 192 * z : 192 * z + 192] = rows[0:2, :192]
        bias_ref[8 * z : 8 * z + 8, :] = rows[2:10, :12]
    found = lax.dot_general(
        bias_ref[...], hot_buckets(), (((0,), (0,)), ((), ())),
        precision=lax.Precision.HIGHEST, preferred_element_type=full,
    )
    own = jnp.where(core == 0, found[0:6], found[6:12])
    for i in range(6):
        vec_ref[i // 2, i % 2 : i % 2 + 1, :] = own[i : i + 1]


def cat_kernel(rows, scalars, *refs):
    at = 0
    for ref in refs[:-1]:
        value = ref[...]
        if len(value.shape) == 2:
            value = value[None]
        refs[-1][at : at + value.shape[0]] = value[:, :rows]
        at += value.shape[0]


def cat(spot, pieces, rows, name):
    count = sum(1 if len(piece.shape) == 2 else piece.shape[0] for piece in pieces)
    shape = (count, rows, pieces[0].shape[-1])
    return call(functools.partial(cat_kernel, rows), spot, pieces, [(shape, pieces[0].dtype)], [], name, 0, 4)[0]


def pass_ffn_kernel(scalars, keep, first, out):
    def one(i, _):
        rows, later = tile_at(576 * i, 576), tile_at(2304 + 576 * i, 576)
        out[rows, :] = keep[later, :] + first[later, :]
        return 0

    lax.fori_loop(0, 4, one, 0)


def sum_ffn_kernel(scalars, keep, first, second, own, pair, far):
    for step, out in enumerate((own, pair.at[0:576], pair.at[576:1152], far)):
        rows = tile_at(576 * xor(scalars[2], step), 576)
        total = wide(keep[rows, :]) + wide(first[rows, :]) + wide(second[rows, :])
        out[...] = total.astype(out.dtype)


def pass_attn_kernel(scalars, keep, sent, first, out):
    out[0:768, :] = (wide(keep[768:1536, :]) + wide(first[768:1536, :])).astype(low)
    out[768:784, :] = (wide(sent[1536:1552, :]) + wide(first[1536:1552, :])).astype(low)


def sum_attn_kernel(scalars, keep, passed, first, second, own, pair, far):
    for step, out in enumerate((own, pair.at[0:208], pair.at[208:416], far)):
        rows = tile_at(192 * xor(scalars[2], step), 192)
        total = wide(keep[rows, :]) + wide(first[rows, :]) + wide(second[rows, :])
        out[0:192, :] = total.astype(out.dtype)
        small = wide(passed[768:784, :]) + wide(second[768:784, :])
        out[192:208, :] = small.astype(out.dtype)


def far_kernel(scalars, far, came, out):
    count = far.shape[0]
    out[...] = (far[...] + wide(came[count : 2 * count, :])).astype(low)


def total_kernel(scalars, own, near, far, out, *rest):
    total = own[...] + wide(near[0 : own.shape[0], :]) + wide(far[...])
    out[...] = total[: out.shape[0]].astype(low)
    if rest:
        rest[0][...] = total[out.shape[0] :]


def pack_attn_kernel(scalars, master_ref, gain_ref, bias_ref, out_ref, part_ref, gain_part, bias_part, sems):
    columns = tile_at(384 * scalars[1], 384)
    copies = [
        fetch_part(master_ref.at[scalars[0], :, columns], part_ref, sems.at[0]),
        fetch_part(gain_ref, gain_part, sems.at[1]),
        fetch_part(bias_ref, bias_part, sems.at[2]),
    ]
    for copy in copies:
        copy.wait()
    gains = jnp.concatenate([gain_part[...], jnp.zeros((2, 192), full)], 1)
    bias = jnp.concatenate([bias_part[...], jnp.zeros((8, 372), full)], 1)
    out_ref[192:208, :] = jnp.concatenate([gains, bias, jnp.zeros((6, 384), full)], 0).astype(low)
    out_ref[0:192, :] = part_ref[...].astype(low)


def pack_ffn_kernel(scalars, in_ref, out_ref, unit_ref, part_ref, rows_ref, sems):
    plane, core = scalars[0], scalars[1]
    copies = []
    for k in range(2):
        columns = tile_at(1024 * (plane % 2) + 512 * k + 256 * core, 256)
        copies.append(fetch_part(in_ref.at[plane // 2, :, columns], part_ref.at[k], sems.at[k]))
    rows = tile_at(256 * core + 64 * plane, 64)
    copies.append(fetch_part(out_ref.at[rows, :], rows_ref, sems.at[2]))
    for copy in copies:
        copy.wait()
    unit_ref[0:192, :] = part_ref[0].astype(low)
    unit_ref[192:384, :] = part_ref[1].astype(low)
    for i in range(3):
        unit_ref[384 + 64 * i : 448 + 64 * i, :] = rows_ref[:, 256 * i : 256 * i + 256].astype(low)


def project_kernel(
    scalars, x_ref, gain_ref, master_ref, near_ref, far_ref, w_ref, act_ref, q_ref, k_ref, v_ref, own_ref, sems
):
    columns = tile_at(384 * scalars[1], 384)
    own_copy = fetch_part(master_ref.at[:, :, columns], own_ref, sems.at[12])

    def pieces(source, quarter, shard):
        return [(source, w_ref.at[quarter, tile_at(192 * shard, 192), :])]

    copies = bring(pieces, near_ref, far_ref, sems, scalars)
    x_in = x_ref[...].astype(full)
    scale = lax.rsqrt(jnp.mean(x_in * x_in, axis=-1, keepdims=True) + norm_eps)
    act_ref[...] = (x_in * scale * gain_ref[0:1, :]).astype(low)
    own_copy.wait()
    for quarter in range(4):
        w_ref[quarter, tile_at(192 * scalars[2], 192), :] = own_ref[quarter].astype(low)
    for copy in copies:
        copy.wait()
    for quarter, out in enumerate((q_ref, k_ref, v_ref)):
        out[...] = mdot(act_ref[...], w_ref[quarter]).astype(low)


def gelu_parts(gate):
    inner = 0.7978845608028654 * (gate + 0.044715 * gate * gate * gate)
    bent = jnp.tanh(inner)
    slope = 0.7978845608028654 * (1.0 + 3.0 * 0.044715 * gate * gate)
    value = 0.5 * gate * (1.0 + bent)
    return value, 0.5 * (1.0 + bent) + 0.5 * gate * (1.0 - bent * bent) * slope


def feed_kernel(
    scalars, x_ref, mix_own, mix_other, w_attn, wo_other, gain_ref, gy_ref, in_master, out_master, near_ref, far_ref,
    mid_ref, act_ref, hid_ref, part_ref, y_ref, grad_ref,
    mix_ref, wo_ref, win_ref, wout_ref, own_ref, gate_ref, up_ref, sems,
):
    core, shard = scalars[1], scalars[2]
    own_copy = fetch_part(out_master.at[tile_at(256 * core, 256), :], own_ref, sems.at[60])

    def pieces(source, quarter, shard):
        rows = tile_at(192 * shard, 192)
        found = []
        for k in range(2):
            columns = tile_at(512 * (quarter % 2) + 256 * k, 256)
            found.append((source.at[192 * k : 192 * k + 192, :], win_ref.at[quarter // 2, rows, columns]))
        rows = tile_at(256 * shard + 64 * quarter, 64)
        for i in range(3):
            part = source.at[384 + 64 * i : 448 + 64 * i, :]
            found.append((part, wout_ref.at[rows, 256 * i : 256 * i + 256]))
        return found

    copies = bring(pieces, near_ref, far_ref, sems, scalars)
    here, there = tile_at(384 * core, 384), tile_at(384 * (1 - core), 384)
    mix_ref[:, here] = mix_own[...]
    mix_ref[:, there] = mix_other[...]
    wo_ref[:, here] = w_attn[...]
    wo_ref[:, there] = wo_other[...]

    def middle(half, _):
        rows = tile_at(256 * half, 256)
        x_mid = x_ref[rows, :].astype(full) + mdot(mix_ref[rows, :], wo_ref[...])
        mid_ref[rows, :] = x_mid
        scale = lax.rsqrt(jnp.mean(x_mid * x_mid, axis=-1, keepdims=True) + norm_eps)
        act_ref[rows, :] = (x_mid * scale * gain_ref[1:2, :]).astype(low)
        return 0

    lax.fori_loop(0, 2, middle, 0)
    for i in range(2):
        for k in range(4):
            pair = in_master[i, :, 512 * k : 512 * k + 512]
            win_ref[i, tile_at(192 * shard, 192), 256 * k : 256 * k + 256] = jnp.where(
                core == 0, pair[:, :256], pair[:, 256:]
            ).astype(low)
    own_copy.wait()
    wout_ref[tile_at(256 * shard, 256), :] = own_ref[...].astype(low)
    for copy in copies:
        copy.wait()

    def hidden(at, _):
        rows, columns = tile_at(256 * (at // 2), 256), tile_at(512 * (at % 2), 512)
        gate = mdot(act_ref[rows, :], win_ref[0, :, columns])
        up = mdot(act_ref[rows, :], win_ref[1, :, columns])
        value, slope = gelu_parts(gate)
        hid_ref[rows, columns] = (value * up).astype(low)
        gate_ref[rows, columns] = slope * up
        up_ref[rows, columns] = value
        return 0

    lax.fori_loop(0, 4, hidden, 0)

    def inner(half, _):
        rows = tile_at(256 * half, 256)
        part = jnp.zeros((256, 768), full)
        for h in range(2):
            columns = slice(512 * h, 512 * h + 512)
            grad_hid = ndot(gy_ref[rows, :], wout_ref[columns, :])
            grad_gate = (grad_hid * gate_ref[rows, columns]).astype(low)
            grad_up = (grad_hid * up_ref[rows, columns]).astype(low)
            grad_ref[h, rows, :] = grad_gate
            grad_ref[2 + h, rows, :] = grad_up
            part = part + ndot(grad_gate, win_ref[0, :, columns]) + ndot(grad_up, win_ref[1, :, columns])
        part_ref[rows, :] = part
        y_ref[rows, :] = mdot(hid_ref[rows, :], wout_ref[...])
        return 0

    lax.fori_loop(0, 2, inner, 0)


def inner_part(turned_ref, grad_ref, plane, core, odd, out):
    def one(j, _):
        turn = odd * (1 + core) + j * (2 - core)
        found = mdot(turned_ref[...], grad_ref[xor(plane, turn)]).astype(low)
        for z in range(4):
            for i in range(2):
                out[tile_at(2304 * j + 576 * z + 192 * i, 192), :] = found[
                    192 * z : 192 * z + 192, 256 * i : 256 * i + 256
                ]
        return 0

    lax.fori_loop(0, 2, one, 0)


def sent_kernel(scalars, act_ref, grad_ref, hid_ref, gy_ref, send_ref, kept_ref, turned_ref, sum_ref):
    plane, core = scalars[0], scalars[1]
    turned_ref[...] = act_ref[...].astype(full).T.astype(low)
    inner_part(turned_ref, grad_ref, plane, core, 1, send_ref)

    def last(z, _):
        sum_ref[...] = tdot(hid_ref[:, tile_at(256 * z, 256)], gy_ref[...])
        for k, turn in enumerate(turns(core)):
            found = sum_ref[tile_at(64 * xor(plane, turn), 64), :].astype(low)
            for i in range(3):
                part = found[:, 256 * i : 256 * i + 256]
                if k % 2:
                    send_ref[tile_at(2304 * (k // 2) + 576 * z + 384 + 64 * i, 64), :] = part
                else:
                    kept_ref[tile_at(768 * (k // 2) + 192 * z + 64 * i, 64), :] = part
        return 0

    lax.fori_loop(0, 4, last, 0)


def kept_kernel(scalars, act_ref, grad_ref, kept_ref, keep_ref, turned_ref):
    plane, core = scalars[0], scalars[1]
    turned_ref[...] = act_ref[...].astype(full).T.astype(low)
    inner_part(turned_ref, grad_ref, plane, core, 0, keep_ref)
    for j in range(2):
        for z in range(4):
            at = 2304 * j + 576 * z + 384
            keep_ref[at : at + 192, :] = kept_ref[768 * j + 192 * z : 768 * j + 192 * z + 192, :]


def pick_kernel(scalars, b0, b1, b2, b3, place_ref, token_ref, out_ref):
    def rows_of(half, _):
        rows = tile_at(256 * half, 256)
        total = jnp.zeros((256, 768), full)
        for i, ref in enumerate((b0, b1, b2, b3)):
            same = place_ref[:, 256 * i : 256 * i + 256] == token_ref[rows, :]
            total = total + mdot(jnp.where(same, 1.0, 0.0).astype(low), ref[...])
        out_ref[rows, :] = total.astype(low)
        return 0

    lax.fori_loop(0, 2, rows_of, 0)


def spread(wanted_ref, token_ref, value, near_ref, own_ref, far_ref):
    for step, out in enumerate((own_ref, near_ref.at[0:256], far_ref, near_ref.at[256:512])):
        same = wanted_ref[256 * step : 256 * step + 256, :] == token_ref[...]
        out[...] = mdot(jnp.where(same, 1.0, 0.0).astype(low), value).astype(low)


def spread_y_kernel(
    scalars, mid_ref, own_part, other_part, wanted_ref, token_ref, near_ref, own_ref, far_ref, value_ref, *rest
):
    parts = (mid_ref, own_part, other_part)
    copies = [fetch_part(ref, held, rest[-1].at[i]) for i, (ref, held) in enumerate(zip(parts, rest[:-1]))]
    for copy in copies:
        copy.wait()
    value_ref[...] = (rest[0][...] + rest[1][...] + rest[2][...]).astype(low)
    spread(wanted_ref, token_ref, value_ref[...], near_ref, own_ref, far_ref)


def spread_x_kernel(
    scalars, own_part, other_part, x_ref, gain_ref, mid_ref, wanted_ref, token_ref, near_ref, own_ref, far_ref,
    value_ref, *rest
):
    parts = (own_part, other_part, mid_ref, x_ref)
    copies = [fetch_part(ref, held, rest[-1].at[i]) for i, (ref, held) in enumerate(zip(parts, rest[:-1]))]
    for copy in copies:
        copy.wait()
    own_part, other_part, mid_ref, x_ref = rest[:-1]
    x_in = x_ref[...].astype(full)
    scale = lax.rsqrt(jnp.mean(x_in * x_in, axis=-1, keepdims=True) + norm_eps)
    turned = (own_part[...] + other_part[...]) * gain_ref[0:1, :]
    lean = jnp.mean(turned * x_in, axis=-1, keepdims=True)
    value_ref[...] = (mid_ref[...] + scale * turned - x_in * (scale * scale * scale * lean)).astype(low)
    spread(wanted_ref, token_ref, value_ref[...], near_ref, own_ref, far_ref)


def add_kernel(scalars, value_ref, more_ref, out_ref):
    out_ref[...] = value_ref[...] + more_ref[256:512, :]


def back_kernel(
    scalars, own_part, other_part, mid_ref, gy_ref, gain_ref, w_ref, wo_other, q_ref, k_ref, v_ref, p_ref,
    grad_ref, right_ref, lined_ref, gain_out, attn_ref, mixed_ref, s_ref, ds_ref, acc_ref, *rest
):
    core = scalars[1]
    here, there = tile_at(384 * core, 384), tile_at(384 * (1 - core), 384)
    late = (own_part, other_part, mid_ref, gy_ref, wo_other, w_ref, q_ref, k_ref, v_ref, p_ref)
    copies = [fetch_part(ref, held, rest[-1].at[i]) for i, (ref, held) in enumerate(zip(late, rest[:-1]))]
    own_part, other_part, mid_ref, gy_ref, wo_other, wo_own, q_ref, k_ref, v_ref, p_ref = rest[:-1]
    for copy in copies[:4]:
        copy.wait()
    x_mid = mid_ref[...]
    scale = lax.rsqrt(jnp.mean(x_mid * x_mid, axis=-1, keepdims=True) + norm_eps)
    gain_out[...] = jnp.sum(own_part[...] * x_mid * scale, axis=0, keepdims=True)
    turned = (own_part[...] + other_part[...]) * gain_ref[1:2, :]
    lean = jnp.mean(turned * x_mid, axis=-1, keepdims=True)
    grad_mid = gy_ref[...].astype(full) + scale * turned - x_mid * (scale * scale * scale * lean)
    grad_ref[...] = grad_mid
    attn_ref[...] = grad_mid.astype(low)
    for copy in copies[4:]:
        copy.wait()
    mixed_ref[...] = (
        ndot(attn_ref[:, here], wo_own[here, :]) + ndot(attn_ref[:, there], wo_other[here, :])
    ).astype(low)

    def one(pair, _):
        lanes = tile_at(128 * pair, 128)
        attend_back_kernel(
            512, *[ref.at[:, lanes] for ref in (q_ref, k_ref, v_ref, mixed_ref)], p_ref.at[pl.ds(2 * pair, 2)],
            *[right_ref.at[i, :, lanes] for i in range(3)], lined_ref.at[pl.ds(pair, 1)], s_ref, ds_ref, acc_ref,
        )
        return 0

    lax.fori_loop(0, 3, one, 0)
    right_ref[3] = attn_ref[:, here]


def last_kernel(
    scalars, act_ref, mix_own, mix_other, right_ref, w_ref, x_ref, lined_ref, other_ref,
    send_ref, keep_ref, part_ref, turned_ref, *rest
):
    plane, core = scalars[0], scalars[1]
    here, there = tile_at(384 * core, 384), tile_at(384 * (1 - core), 384)
    late = (act_ref, mix_own, mix_other, right_ref, w_ref, x_ref)
    copies = [fetch_part(ref, held, rest[-1].at[i]) for i, (ref, held) in enumerate(zip(late, rest[:-1]))]
    act_ref, mix_own, mix_other, right_ref, w_ref, x_ref = rest[:-1]
    for copy in copies:
        copy.wait()
    turned_ref[0] = act_ref[...].astype(full).T.astype(low)
    turned_ref[1, here, :] = mix_own[...].astype(full).T.astype(low)
    turned_ref[1, there, :] = mix_other[...].astype(full).T.astype(low)

    def outer(j, _):
        for odd, out in enumerate((keep_ref, send_ref)):
            quarter = xor(plane, odd * (1 + core) + j * (2 - core))
            out[tile_at(768 * j, 768), :] = mdot(turned_ref[quarter // 3], right_ref[quarter]).astype(low)
        return 0

    lax.fori_loop(0, 2, outer, 0)
    part = ndot(right_ref[0], w_ref[0]) + ndot(right_ref[1], w_ref[1]) + ndot(right_ref[2], w_ref[2])
    part_ref[...] = part
    x_in = x_ref[...].astype(full)
    scale = lax.rsqrt(jnp.mean(x_in * x_in, axis=-1, keepdims=True) + norm_eps)
    gain = jnp.sum(part * x_in * scale, axis=0, keepdims=True)
    lined = jnp.concatenate([lined_ref[0], lined_ref[1], lined_ref[2]], 0)
    table = lax.dot_general(
        lined, hot_buckets(), (((1,), (1,)), ((), ())),
        precision=lax.Precision.HIGHEST, preferred_element_type=full,
    )
    table = jnp.concatenate([table, jnp.zeros((6, 352), full)], 1)
    other = other_ref[...]
    send_ref[1536:1552, :] = jnp.concatenate(
        [gain[:, :384], gain[:, 384:], other[:, :384], other[:, 384:], table, jnp.zeros((6, 384), full)], 0
    ).astype(low)


def wide(value):
    return value.astype(full)


def adam_kernel(steps, count, scalars, *refs):
    plane, core = scalars[0], scalars[1]
    lower = core == 0
    states, grads, outs = refs[:3], refs[3:5], refs[5 : 5 + count]
    own, other, brought, held, sems = refs[5 + count], refs[6 + count], refs[7 + count : 10 + count], refs[-5:-1], refs[-1]
    arrive = [fetch_part(grads[0], own, sems.at[8]), fetch_part(grads[1], other, sems.at[9])]
    loads = []
    for number, (where, _, _, _) in enumerate(steps):
        loads.append(
            [fetch_part(where(state), brought[i].at[number], sems.at[10 + 3 * number + i]) for i, state in enumerate(states)]
        )
    for copy in arrive:
        copy.wait()

    def place(own, other, quarter):
        turn = xor(plane, quarter)
        return own.at[stack_at(turn, core)], other.at[stack_at(turn, 1 - core)]

    flying = []
    for number, (_, quarter, read, targets) in enumerate(steps):
        slot = number % 2
        if number >= 2:
            for copy in flying[number - 2]:
                copy.wait()
        if quarter is None:
            grad = read(own, other, place, lower).astype(full)
        else:
            grad = read(*place(own, other, quarter), lower).astype(full)
        for copy in loads[number]:
            copy.wait()
        new = adam_step(brought[0][number], brought[1][number], brought[2][number], grad, True)
        copies = []
        for i, value in enumerate(new):
            order = (0, 1, 3, 2)[i]
            held[order][slot] = value
            copies.append(fetch_part(held[order].at[slot], targets(outs, i), sems.at[4 * slot + i]))
        flying.append(copies)
    for copies in flying[-2:]:
        for copy in copies:
            copy.wait()


def adam_call(spot, steps, block, states, grads, outputs, name):
    return call(
        functools.partial(adam_kernel, steps, len(outputs)), spot,
        [*[[state] for state in states], *[(grad,) for grad in grads]], outputs,
        [
            *[pltpu.VMEM(grads[0].shape, low)] * 2, *[pltpu.VMEM((len(steps),) + block, full)] * 3,
            *[pltpu.VMEM((2,) + block, full)] * 2, pltpu.VMEM((2,) + block, low), pltpu.VMEM((2,) + block, full),
            pltpu.SemaphoreType.DMA((10 + 3 * len(steps),)),
        ],
        name, 0, 60, range(len(outputs)),
    )


def small_kernel(
    scalars, own, other, gm_ref, gf_ref, gs_ref, bm_ref, bf_ref, bs_ref, gain_step, gain_first, gain_second,
    bias_step, bias_first, bias_second, table_ref,
):
    core, shard = scalars[1], scalars[2]
    total = own[...] + other[...]
    grads = []
    for j in range(2):
        row = jnp.where(shard // 2 == 1, total[2 * j + 1 : 2 * j + 2], total[2 * j : 2 * j + 1])
        grads.append(jnp.where(shard % 2 == 1, row[:, 192:], row[:, :192]))
    new = adam_step(gm_ref[...], gf_ref[...], gs_ref[...], jnp.concatenate(grads, 0), False)
    gain_step[...], gain_first[...], gain_second[...] = new[0] - gm_ref[...], new[1], new[2]
    mine, theirs = own[4:10, :32], other[4:10, :32]
    table = jnp.concatenate(chosen(core == 0, mine, theirs), 0)
    same = lax.broadcasted_iota(jnp.int32, (32, 32), 0) == lax.broadcasted_iota(jnp.int32, (32, 32), 1)
    table_ref[...] = lax.dot_general(
        jnp.where(same, 1.0, 0.0), table, (((1,), (1,)), ((), ())),
        precision=lax.Precision.HIGHEST, preferred_element_type=full,
    )
    grad = table_ref[tile_at(8 * shard, 8), :]
    new = adam_step(bm_ref[...], bf_ref[...], bs_ref[...], grad, False)
    bias_step[...], bias_first[...], bias_second[...] = new[0] - bm_ref[...], new[1], new[2]


def chosen(lower, mine, theirs):
    return jnp.where(lower, mine, theirs), jnp.where(lower, theirs, mine)


def attn_steps():
    def one(m):
        where = lambda ref: ref.at[m]

        def read(mine, theirs, lower):
            return jnp.concatenate(chosen(lower, mine[...], theirs[...]), 1)

        def targets(outs, i):
            if i == 2:
                return outs[2].at[m] if m < 3 else outs[3]
            return outs[(0, 1, 2, 4)[i]].at[m]

        return where, m, read, targets

    return [one(m) for m in range(4)]


def ffin_steps():
    def one(i, h):
        columns = slice(1024 * h, 1024 * h + 1024)
        where = lambda ref: ref.at[i, :, columns]

        def read(mine, theirs, lower):
            left, right = chosen(lower, mine[0:384, :], theirs[0:384, :])
            return jnp.concatenate([left[:192], right[:192], left[192:], right[192:]], 1)

        return where, 2 * i + h, read, lambda outs, n: where(outs[n])

    return [one(i, h) for i in range(2) for h in range(2)]


def ffout_steps():
    def one(c):
        rows = slice(256 * c, 256 * c + 256)
        where = lambda ref: ref.at[rows, :]

        def read(own, other, place, lower):
            found = []
            for q in range(4):
                mine, theirs = place(own, other, q)
                value = chosen(lower, mine[384:576, :], theirs[384:576, :])[c]
                found.append(jnp.concatenate([value[:64], value[64:128], value[128:]], 1))
            return jnp.concatenate(found, 0)

        return where, None, read, lambda outs, n: where(outs[n])

    return [one(c) for c in range(2)]


def body_fast(
    tokens,
    cotangent,
    lengths,
    deal,
    attn_master,
    ffin_master,
    ffout_master,
    gain_master,
    bias_master,
    attn_first,
    ffin_first,
    ffout_first,
    gain_first,
    bias_first,
    attn_second,
    ffin_second,
    ffout_second,
    gain_second,
    bias_second,
):
    plane, core, shard = (lax.axis_index(name) for name in ("plane", "core", "shard"))
    spot = jnp.stack([plane, core, shard])
    group, rest = shard // 2, shard % 2
    mine = group == core

    quarter = call(
        pack_attn_kernel, spot, [[attn_master], [gain_master], [bias_master]], [((208, 384), low)],
        [
            pltpu.VMEM((192, 384), full), pltpu.VMEM((2, 192), full), pltpu.VMEM((8, 12), full),
            pltpu.SemaphoreType.DMA((3,)),
        ],
        "pack_attn", 0, 60,
    )[0]
    attn_third = across(quarter, 3)

    unit = call(
        pack_ffn_kernel, spot, [[ffin_master], [ffout_master]], [((576, 256), low)],
        [pltpu.VMEM((2, 192, 256), full), pltpu.VMEM((64, 768), full), pltpu.SemaphoreType.DMA((3,))],
        "pack_ffn", 0, 60,
    )[0]
    attn_third = after(attn_third, unit)
    attn_pair = across(cat(spot, [quarter, attn_third], 208, "pair_attn_in"), 1)

    up_pairs = lambda pairs: [((p, 1, z), (p, 1, w)) for p in range(4) for z, w in pairs]
    down_pairs = lambda pairs: [((p, 0, 3 - z), (p, 0, 3 - w)) for p in range(4) for z, w in pairs]
    along = lambda value, *which: send(value, up_pairs(which) + down_pairs(which))

    def fetch_rest(own, one, gate=None):
        two = along(one, (1, 2), (2, 3))
        two = two if gate is None else after(two, gate)
        three = along(jnp.where(at_end, own, two), (2, 3), (3, 2))
        return own, one, two, three

    way = 1 - 2 * core
    at_end = shard == 3 * core
    blocks = jnp.stack(
        [shard, shard + way, shard + 2 * way, jnp.where(at_end, shard + 3 * way, shard - way)]
    )
    blocks = jnp.clip(blocks, 0, 3)
    tok_blocks = fetch_rest(tokens[0], along(tokens[0], (0, 1), (1, 2), (2, 3)))

    table_own = jnp.concatenate([lengths[0], deal[0]])
    table = jnp.where(mine, table_own, swap(table_own))
    lens, order = table[:4], table[4:]
    starts = jnp.cumsum(lens) - lens
    long_start = jnp.sum(jnp.where(lens == 512, starts, 0))
    at_half = jnp.arange(512, dtype=jnp.int32)
    token_here = jnp.where(rest == 0, long_start + at_half, at_half + 512 * (at_half >= long_start))
    seg_here = jnp.sum((token_here[:, None] >= starts[None, :]).astype(jnp.int32), axis=1)
    token_index = jnp.arange(1024, dtype=jnp.int32)

    token_column = token_here[:, None]
    token_row = jnp.where(mine, token_here, -1)[None, :]

    def wanted_by(place_of):
        rows = [lax.dynamic_slice_in_dim(place_of, 256 * xor(shard, step), 256) for step in range(4)]
        return jnp.concatenate(rows).reshape(1024, 1)

    wanted_y = wanted_by(order)
    wanted_x = wanted_by(token_index)

    def rows_here(place_of, pieces, gate=None):
        place = [lax.dynamic_slice_in_dim(place_of, blocks[i] * 256, 256) for i in range(4)]
        place = jnp.concatenate(place).reshape(1, 1024)
        chosen = call(
            pick_kernel, spot, [*pieces, after(place, wanted_y, wanted_x, token_row), token_column], [((512, 768), low)], [], "pick", 0, 8
        )[0]
        chosen = chosen if gate is None else after(chosen, *gate)
        return jnp.where(mine, chosen, swap(chosen))

    def rows_near(rows, *gates):
        pairs = [((p, c, z), (p, c, z ^ 1)) for p, c, z in ALL if z // 2 == c]
        return after(send(rows[0], pairs), *gates)

    def rows_far(rows, came, *gates):
        pairs = [((p, c, z), (p, c, z ^ 2)) for p, c, z in ALL if z // 2 == c]
        far = call(add_kernel, spot, [rows[2], came], [((256, 768), low)], [], "add_rows", 0, 4)[0]
        return after(send(far, pairs), *gates)

    def rows_back(rows, first_gate, second_gate):
        pairs = lambda step: [((p, c, z), (p, c, z ^ step)) for p, c, z in ALL if z // 2 == c]
        near, own, far = rows
        came = after(send(near, pairs(1)), first_gate)
        far = call(add_kernel, spot, [far, came], [((256, 768), low)], [], "add_rows", 0, 4)[0]
        last = after(send(far, pairs(2)), second_gate)
        return own + came[:256] + last, last


    gains, vectors = call(
        unpack_kernel, spot, [quarter, attn_pair, attn_third], [((2, 768), full), ((3, 2, 1024), full)],
        [pltpu.VMEM((32, 12), full)], "unpack", 0, 8,
    )

    def spread_plane(pieces, rows, gate=None, late=None):
        near = cat(spot, pieces, rows, "near")
        arrived = plane_first(near)
        if gate is not None:
            arrived = after(arrived, *gate)
        near = cat(spot, [near, arrived], rows, "nearest")
        return near, plane_second(near if late is None else after(near, late))

    unit = after(unit, attn_third)
    ffn_third = across(unit, 3)
    ffn_two = cat(spot, [unit, ffn_third], 576, "pair_ffn_in")
    near, far = spread_plane([attn_pair, attn_third], 192, [ffn_two])
    ffn_pair_in = across(ffn_two, 1)
    ffn_came = [ffn_pair_in, ffn_third]
    x_low = rows_here(token_index, tok_blocks, (far, *ffn_came))
    w_attn, act_one, query, key, value = call(
        project_kernel, spot,
        [x_low, gains, [attn_master], (near,), (far,)],
        [((4, 768, 384), low), ((512, 768), low)] + [((512, 384), low)] * 3,
        [pltpu.VMEM((4, 192, 384), full), pltpu.SemaphoreType.DMA((13,))], "project", 0, 60,
    )
    wo_own = w_attn[3]
    wo_other = swap(wo_own)


    cot_own = after(cotangent[0], *ffn_came)
    cot_one = along(cot_own, (1, 2), (2, 3))
    cot_two = along(cot_own, (0, 2), (1, 3))
    cot_three = along(cot_own, (0, 3), (3, 2))
    ffn_near, ffn_far = spread_plane(ffn_came, 576, [query, cot_one])
    mix_own, probs = call(
        attend_all_kernel, spot, [after(query, ffn_near), key, value, seg_here[:, None], seg_here[None, :], vectors],
        [((512, 384), low), ((6, 512, 512), low)],
        [pltpu.VMEM((512, 512), full), pltpu.VMEM((6, 512, 512), low), pltpu.SemaphoreType.DMA((3,))],
        "attend", 0, 60, (1,),
    )
    cot_blocks = (cot_own, *[after(piece, mix_own) for piece in (cot_one, cot_two, cot_three)])
    grad_y = rows_here(order, cot_blocks)
    mix_other = swap(mix_own)
    x_mid, act_two, hidden, part_two, y_part, grads_up = call(
        feed_kernel, spot,
        [
            x_low, mix_own, mix_other, wo_own, wo_other, gains, grad_y, ffin_master, [ffout_master],
            (ffn_near,), (ffn_far,),
        ],
        [
            ((512, 768), full), ((512, 768), low), ((512, 1024), low), ((512, 768), full), ((512, 768), full),
            ((4, 512, 512), low),
        ],
        [
            pltpu.VMEM((512, 768), low), pltpu.VMEM((768, 768), low), pltpu.VMEM((2, 768, 1024), low),
            pltpu.VMEM((1024, 768), low), pltpu.VMEM((256, 768), full), pltpu.VMEM((512, 1024), full),
            pltpu.VMEM((512, 1024), full), pltpu.SemaphoreType.DMA((61,)),
        ],
        "feed", 0, 24,
    )
    ffn_send, out_kept = call(
        sent_kernel, spot, [act_two, grads_up, hidden, grad_y], [((4608, 256), low), ((1536, 256), low)],
        [pltpu.VMEM((768, 512), low), pltpu.VMEM((256, 768), full)], "sent", 0, 12,
    )
    ffn_first = plane_first(ffn_send)
    ffn_keep = call(
        kept_kernel, spot, [act_two, after(grads_up, ffn_send), out_kept], [((4608, 256), low)],
        [pltpu.VMEM((768, 512), low)], "kept", 0, 12,
    )[0]
    part_other = after(swap(part_two), ffn_keep)

    grad_mid, right, lined, gain_two = call(
        back_kernel, spot,
        [
            (part_two,), (part_other,), (x_mid,), (grad_y,), gains, (wo_own,), (wo_other,),
            (query,), (key,), (value,), (probs,),
        ],
        [
            ((512, 768), full), ((4, 512, 384), low), ((3, 2, 1024), full), ((1, 768), full),
        ],
        [
            pltpu.VMEM((512, 768), low), pltpu.VMEM((512, 384), low), pltpu.VMEM((512, 512), full), pltpu.VMEM((512, 512), low),
            pltpu.VMEM((128, 1024), full), *[pltpu.VMEM((512, 768), full)] * 3, pltpu.VMEM((512, 768), low),
            *[pltpu.VMEM((768, 384), low)] * 2, *[pltpu.VMEM((512, 384), low)] * 3, pltpu.VMEM((6, 512, 512), low),
            pltpu.SemaphoreType.DMA((10,)),
        ],
        "back", 0, 60,
    )
    y_other = swap(after(y_part, part_other))
    y_rows = call(
        spread_y_kernel, spot, [(x_mid,), (after(y_part, right),), (y_other,), wanted_y, token_row],
        [((512, 768), low), ((256, 768), low), ((256, 768), low)],
        [pltpu.VMEM((512, 768), low), *[pltpu.VMEM((512, 768), full)] * 3, pltpu.SemaphoreType.DMA((3,))],
        "spread_y", 0, 60,
    )
    ffn_first = after(ffn_first, right, y_rows[0])
    one_out = lambda kernel, inputs, shape, name: call(kernel, spot, inputs, [(shape, low)], [], name, 0, 8)[0]
    ffn_passed = one_out(pass_ffn_kernel, [ffn_keep, ffn_first], (2304, 256), "pass_ffn")
    ffn_second = plane_second(ffn_passed)
    attn_send, attn_keep, part_one = call(
        last_kernel, spot,
        [
            (after(act_one, ffn_passed),), (mix_own,), (mix_other,), (right,), (w_attn,), (x_low,), lined, gain_two,
        ],
        [((1552, 384), low), ((1536, 384), low), ((512, 768), full)],
        [
            pltpu.VMEM((2, 768, 512), low), pltpu.VMEM((512, 768), low), *[pltpu.VMEM((512, 384), low)] * 2,
            pltpu.VMEM((4, 512, 384), low), pltpu.VMEM((4, 768, 384), low), pltpu.VMEM((512, 768), low),
            pltpu.SemaphoreType.DMA((6,)),
        ],
        "last", 0, 60,
    )
    y_near = rows_near([after(y_rows[0], ffn_passed)], part_one)
    ffn_second = after(ffn_second, part_one, y_near)
    ffn_own, ffn_two, ffn_far = call(
        sum_ffn_kernel, spot, [ffn_keep, ffn_first, ffn_second],
        [((576, 256), full), ((1152, 256), low), ((576, 256), full)], [], "sum_ffn", 0, 8,
    )
    ffn_near = across(ffn_two, 1)
    y_far = rows_far(y_rows, after(y_near, ffn_two))
    x_rows = call(
        spread_x_kernel, spot,
        [(part_one,), (swap(part_one),), (x_low,), gains, (grad_mid,), wanted_x, token_row],
        [((512, 768), low), ((256, 768), low), ((256, 768), low)],
        [
            pltpu.VMEM((512, 768), low), *[pltpu.VMEM((512, 768), full)] * 3, pltpu.VMEM((512, 768), low),
            pltpu.SemaphoreType.DMA((4,)),
        ],
        "spread_x", 0, 60,
    )
    ffn_send = call(far_kernel, spot, [ffn_far, after(ffn_near, *x_rows)], [((576, 256), low)], [], "far_ffn", 0, 8)[0]
    ffn_last = across(ffn_send, 3)
    y_far = after(y_far, ffn_send)
    attn_first_came = after(plane_first(after(attn_send, ffn_second)), ffn_send, y_far, *x_rows)
    passed = one_out(pass_attn_kernel, [attn_keep, attn_send, attn_first_came], (784, 384), "pass_attn")
    layer_out = y_rows[1] + y_near[:256] + y_far
    attn_second_came = plane_second(passed)
    attn_own, attn_two, attn_far = call(
        sum_attn_kernel, spot, [attn_keep, passed, attn_first_came, attn_second_came],
        [((208, 384), full), ((416, 384), low), ((208, 384), full)], [], "sum_attn", 0, 8,
    )

    attn_near_came = across(attn_two, 1)
    ffn_last = after(ffn_last, attn_two)
    ffn_sum = one_out(total_kernel, [ffn_own, ffn_near, ffn_last], (576, 256), "total_ffn")
    attn_far_send = call(far_kernel, spot, [attn_far, attn_near_came], [((208, 384), low)], [], "far_attn", 0, 8)[0]
    attn_last = across(attn_far_send, 3)
    ffn_pair = cat(spot, [ffn_sum, after(plane_first(ffn_sum), attn_far_send)], 576, "pair_ffn")
    ffn_stack = cat(spot, [ffn_pair, after(plane_second(ffn_pair), attn_last)], 576, "stack_ffn")
    ffn_sum = (ffn_stack, swap(ffn_stack))
    flat, wide_in = (512, 768), (2, 192, 2048)
    ffin_res = adam_call(
        spot, ffin_steps(), (192, 1024), [ffin_master, ffin_first, ffin_second], ffn_sum,
        [(wide_in, full), (wide_in, full), (wide_in, full), (wide_in, low)], "adam_ffin",
    )
    ffout_res = adam_call(
        spot, ffout_steps(), (256, 768), [ffout_master, ffout_first, ffout_second], ffn_sum,
        [(flat, full), (flat, full), (flat, full), (flat, low)], "adam_ffout",
    )
    attn_sum, small = call(
        total_kernel, spot, [attn_own, attn_near_came, after(attn_last, ffn_stack)],
        [((192, 384), low), ((16, 384), full)], [], "total_attn", 0, 8,
    )
    attn_near = cat(spot, [attn_sum, after(plane_first(attn_sum), ffin_res[0])], 192, "pair_attn")
    attn_stack = cat(spot, [attn_near, after(plane_second(attn_near), ffout_res[0])], 192, "stack_attn")
    attn_sum = (attn_stack, swap(attn_stack))
    x_rows = [after(value, small) for value in x_rows]
    input_grad, _ = rows_back(x_rows, ffin_res[0], ffout_res[0])
    small_other = swap(small)
    square = (4, 192, 768)
    attn_res = adam_call(
        spot, attn_steps(), (192, 768), [attn_master, attn_first, attn_second], attn_sum,
        [(square, full), (square, full), ((3, 192, 768), full), ((192, 768), full), (square, low)], "adam_attn",
    )
    smalls = call(
        small_kernel, spot,
        [small, small_other, gain_master, gain_first, gain_second, bias_master, bias_first, bias_second],
        [((2, 192), full)] * 3 + [((8, 12), full)] * 3, [pltpu.VMEM((32, 12), full)], "adam_small", 0, 4,
    )
    return (
        layer_out[None],
        input_grad[None],
        attn_res[0],
        ffin_res[0],
        ffout_res[0],
        smalls[0],
        smalls[3],
        attn_res[1],
        ffin_res[1],
        ffout_res[1],
        smalls[1],
        smalls[4],
        attn_res[2],
        attn_res[3],
        ffin_res[2],
        ffout_res[2],
        smalls[2],
        smalls[5],
        attn_res[4],
        ffin_res[3],
        ffout_res[3],
    )


def body_any(
    tokens,
    cotangent,
    lengths,
    deal,
    attn_master,
    ffin_master,
    ffout_master,
    gain_master,
    bias_master,
    attn_first,
    ffin_first,
    ffout_first,
    gain_first,
    bias_first,
    attn_second,
    ffin_second,
    ffout_second,
    gain_second,
    bias_second,
):
    shards = lax.axis_size("shard")
    core = lax.axis_index("core")
    shard = lax.axis_index("shard")
    tok_rows, model = tokens.shape[1], tokens.shape[2]
    heads = bias_master.shape[1]
    own_heads = heads // 2
    part = model // 2
    whole_len = tok_rows * shards
    half_len = whole_len // 2
    per_half = shards // 4
    rows = half_len // per_half
    place, sub = shard // per_half, shard % per_half
    group, rest = place // 2, place % 2
    mine = group == core
    siblings = [[a * per_half + b for b in range(per_half)] for a in range(4)]

    def join_half(value):
        if per_half == 1:
            return value
        return lax.all_gather(value, "shard", axis=0, tiled=True, axis_index_groups=siblings)

    table_own = jnp.concatenate([lengths[0], deal[0]])
    table = jnp.where(mine, table_own, swap(table_own))
    count = lengths.shape[1]
    lens, order = table[:count], table[count:]
    starts = jnp.cumsum(lens) - lens
    long_start = jnp.sum(jnp.where(lens == half_len, starts, 0))
    at_half = jnp.arange(half_len, dtype=jnp.int32)
    token_half = jnp.where(
        rest == 0, long_start + at_half, at_half + half_len * (at_half >= long_start)
    )
    seg_half = jnp.sum((token_half[:, None] >= starts[None, :]).astype(jnp.int32), axis=1)
    first_row = sub * rows
    token_here = lax.dynamic_slice_in_dim(token_half, first_row, rows)
    seg_here = lax.dynamic_slice_in_dim(seg_half, first_row, rows)

    def rows_here(place_of, own):
        gathered = lax.all_gather(own, "shard", axis=0, tiled=True)
        gathered = jnp.where(mine, gathered, swap(gathered))
        picked = (place_of[None, :] == token_here[:, None]).astype(low)
        return mdot(picked, gathered).astype(low)

    def rows_back(place_of, here):
        picked = (place_of[:, None] == token_here[None, :]) & mine
        spread = mdot(picked.astype(low), here).astype(low)
        return lax.psum_scatter(spread, "shard", scatter_dimension=0, tiled=True)

    ff_rows = ffout_master.shape[0]
    ff_part = ff_rows // 2
    attn_low = attn_master.astype(low)
    cols = lax.dynamic_slice_in_dim(attn_low[:3], core * part, part, 2)
    ffin_low = ffin_master.astype(low).reshape(2, -1, shards, 2, ff_part)
    ffin_low = lax.dynamic_index_in_dim(ffin_low, core, 3, keepdims=False)
    ffin_low = ffin_low.reshape(2, -1, shards * ff_part)
    ffout_low = lax.dynamic_slice_in_dim(ffout_master.astype(low), core * ff_part, ff_part, 0)
    w_qkv = lax.all_gather(cols, "shard", axis=1, tiled=True)
    w_o = lax.all_gather(attn_low[3], "shard", axis=0, tiled=True)
    w_in = lax.all_gather(ffin_low, "shard", axis=1, tiled=True)
    w_out = lax.all_gather(ffout_low, "shard", axis=0, tiled=True)
    gains = lax.all_gather(gain_master.astype(low), "shard", axis=1, tiled=True).astype(full)
    bias = lax.all_gather(bias_master.astype(low), "shard", axis=0, tiled=True).astype(full)

    token_index = jnp.arange(whole_len, dtype=jnp.int32)
    x_low = rows_here(token_index, tokens[0])
    grad_y = rows_here(order, cotangent[0])

    x_in = x_low.astype(full)
    scale_one = lax.rsqrt(jnp.mean(x_in * x_in, axis=-1, keepdims=True) + norm_eps)
    act_one = (x_in * scale_one * gains[0]).astype(low)
    query = mdot(act_one, w_qkv[0]).astype(low)
    key_own = mdot(act_one, w_qkv[1]).astype(low)
    value_own = mdot(act_one, w_qkv[2]).astype(low)
    key, value = join_half(key_own), join_half(value_own)
    span = rows + half_len
    relative = jnp.arange(span, dtype=jnp.int32) - rows - first_row
    ids = jnp.arange(bias.shape[0], dtype=jnp.int32)
    one_hot = (bucket_of(relative)[None, :] == ids[:, None]).astype(full)
    bias_own = lax.dynamic_slice_in_dim(bias, core * own_heads, own_heads, 1)
    vectors = lax.dot_general(
        bias_own, one_hot, (((0,), (0,)), ((), ())), precision=lax.Precision.HIGHEST
    )
    mix_own, probs = attend(
        query, key, value, seg_here[:, None], seg_half[None, :], vectors
    )
    mix = both_cores(mix_own, swap(mix_own), core, 1)
    x_mid = x_in + mdot(mix, w_o)
    scale_two = lax.rsqrt(jnp.mean(x_mid * x_mid, axis=-1, keepdims=True) + norm_eps)
    act_two = (x_mid * scale_two * gains[1]).astype(low)
    gate_pre = mdot(act_two, w_in[0])
    up_pre = mdot(act_two, w_in[1])
    gated, gelu_pull = jax.vjp(
        lambda gate_val, up_val: jax.nn.gelu(gate_val, approximate=True) * up_val, gate_pre, up_pre
    )
    hidden = gated.astype(low)
    y_part = mdot(hidden, w_out)
    y_here = (x_mid + y_part + swap(y_part)).astype(low)
    layer_out = rows_back(order, y_here)

    grad_gate, grad_up = gelu_pull(ndot(grad_y, w_out))
    grad_gate, grad_up = grad_gate.astype(low), grad_up.astype(low)
    d_out = tdot(hidden, grad_y).astype(low)
    d_in = jnp.stack([tdot(act_two, grad_gate), tdot(act_two, grad_up)]).astype(low)
    part_two = ndot(grad_gate, w_in[0]) + ndot(grad_up, w_in[1])
    grad_act_two = part_two + swap(part_two)
    turned = grad_act_two * gains[1]
    grad_mid = (
        grad_y.astype(full)
        + scale_two * turned
        - x_mid * scale_two**3 * jnp.mean(turned * x_mid, axis=-1, keepdims=True)
    )
    d_gain_two = jnp.sum(grad_act_two * x_mid * scale_two, axis=0)
    grad_attn = grad_mid.astype(low)
    w_o_own = lax.dynamic_slice_in_dim(w_o, core * part, part, 0)
    grad_mix = ndot(grad_attn, w_o_own).astype(low)
    d_wo = tdot(mix, lax.dynamic_slice_in_dim(grad_attn, core * part, part, 1)).astype(low)
    grad_q, grad_k, grad_v, diagonals = attend_back(query, key, value, grad_mix, probs, span)
    if per_half > 1:
        grad_k = lax.psum_scatter(
            grad_k, "shard", scatter_dimension=0, tiled=True, axis_index_groups=siblings
        )
        grad_v = lax.psum_scatter(
            grad_v, "shard", scatter_dimension=0, tiled=True, axis_index_groups=siblings
        )
    d_wq = tdot(act_one, grad_q).astype(low)
    d_wk = tdot(act_one, grad_k).astype(low)
    d_wv = tdot(act_one, grad_v).astype(low)
    part_one = ndot(grad_q, w_qkv[0]) + ndot(grad_k, w_qkv[1]) + ndot(grad_v, w_qkv[2])
    grad_act_one = part_one + swap(part_one)
    turned = grad_act_one * gains[0]
    grad_x = (
        grad_mid
        + scale_one * turned
        - x_in * scale_one**3 * jnp.mean(turned * x_in, axis=-1, keepdims=True)
    ).astype(low)
    d_gain_one = jnp.sum(grad_act_one * x_in * scale_one, axis=0)
    input_grad = rows_back(token_index, grad_x)

    lined = diagonals.reshape(own_heads, span)
    table_own = lax.dot_general(
        one_hot, lined, (((1,), (1,)), ((), ())), precision=lax.Precision.HIGHEST
    )
    empty = jnp.zeros_like(table_own)
    grad_table = jnp.where(
        core == 0,
        jnp.concatenate([table_own, empty], 1),
        jnp.concatenate([empty, table_own], 1),
    )
    grad_gain = jnp.where(core == 0, jnp.stack([d_gain_one, d_gain_two]), 0.0)

    d_attn = jnp.stack([d_wq, d_wk, d_wv, d_wo])

    def reduced(grad, axis):
        share = lax.psum_scatter(grad, "shard", scatter_dimension=axis, tiled=True)
        return lax.psum(share, "plane")

    g_attn = reduced(d_attn, 1)
    g_attn = both_cores(g_attn, swap(g_attn), core, 2).astype(full)
    g_in = reduced(d_in, 1)
    g_in = g_in.reshape(2, -1, shards, 1, ff_part)
    g_in = both_cores(g_in, swap(g_in), core, 3).reshape(ffin_master.shape).astype(full)
    g_out = reduced(d_out, 0)
    g_out = both_cores(g_out, swap(g_out), core, 0).astype(full)
    g_gain, g_bias = lax.psum((grad_gain, grad_table), ("plane", "core", "shard"))
    own_gain = gain_master.shape[1]
    g_gain = lax.dynamic_slice_in_dim(g_gain, shard * own_gain, own_gain, 1)
    own_bias = bias_master.shape[0]
    g_bias = lax.dynamic_slice_in_dim(g_bias, shard * own_bias, own_bias, 0)

    attn_res = adam_step(attn_master, attn_first, attn_second, g_attn, True)
    ffin_res = adam_step(ffin_master, ffin_first, ffin_second, g_in, True)
    ffout_res = adam_step(ffout_master, ffout_first, ffout_second, g_out, True)
    gain_res = adam_step(gain_master, gain_first, gain_second, g_gain, False)
    bias_res = adam_step(bias_master, bias_first, bias_second, g_bias, False)
    return (
        layer_out[None],
        input_grad[None],
        attn_res[0],
        ffin_res[0],
        ffout_res[0],
        gain_res[0] - gain_master,
        bias_res[0] - bias_master,
        attn_res[1],
        ffin_res[1],
        ffout_res[1],
        gain_res[1],
        bias_res[1],
        attn_res[2][:3],
        attn_res[2][3],
        ffin_res[2],
        ffout_res[2],
        gain_res[2],
        bias_res[2],
        attn_res[3],
        ffin_res[3],
        ffout_res[3],
    )


def solution(mesh):
    reps, shards = mesh.devices.shape
    cores = Mesh(mesh.devices.reshape(reps // 2, 2, shards), ("plane", "core", "shard"))
    rep = ("plane", "core")
    tok = P(rep, "shard", None)
    row = P(rep, None)
    second = P(None, "shard", None)
    first = P("shard", None)
    gain = P(None, "shard")
    states = (second, second, first, gain, first)
    in_specs = (tok, tok, row, row) + states * 3
    out_specs = (
        (tok, tok) + states + states + (second, first, second, first, gain, first) + states[:3]
    )
    body = body_fast if (reps, shards) == (8, 4) else body_any
    return jax.shard_map(body, mesh=cores, in_specs=in_specs, out_specs=out_specs, check_vma=False)
```

```python
import functools

import jax
import jax.numpy as jnp
from jax import lax
from jax.experimental import pallas as pl
from jax.experimental.pallas import tpu as pltpu
from jax.sharding import Mesh
from jax.sharding import PartitionSpec as P

norm_eps = 1e-06
far_below = -1e30
steps_beyond = (12, 16, 23, 32, 46, 64, 91)
first_rate = 0.9
second_rate = 0.95
learning = 0.05
shrink = 0.1
adam_eps = 1e-08
first_fix = 1.0 - 0.9**8
second_fix = 1.0 - 0.95**8
chips = ("plane", "shard")
low = jnp.bfloat16
full = jnp.float32


def bucket_of(relative):
    distance = jnp.abs(relative)
    beyond = 8 + sum(((distance >= threshold).astype(jnp.int32) for threshold in steps_beyond))
    near_part = jnp.where(distance < 8, distance, beyond)
    return near_part + 16 * (relative > 0).astype(jnp.int32)


def ndot(left, right):
    return lax.dot_general(left, right, (((1,), (1,)), ((), ())), preferred_element_type=full)


def tdot(left, right):
    return lax.dot_general(left, right, (((0,), (0,)), ((), ())), preferred_element_type=full)


def mdot(left, right):
    return jnp.dot(left, right, preferred_element_type=full)


def swap(value):
    return lax.ppermute(value, "core", [(0, 1), (1, 0)])


def both_cores(mine, other, core, axis):
    first = jnp.where(core == 0, mine, other)
    second = jnp.where(core == 0, other, mine)
    return jnp.concatenate([first, second], axis)


def adam_step(master, first, second, grad, decayed):
    new_first = first_rate * first + (1.0 - first_rate) * grad
    new_second = second_rate * second + (1.0 - second_rate) * grad * grad
    update = new_first / first_fix / (jnp.sqrt(new_second / second_fix) + adam_eps)
    if decayed:
        update = update + shrink * master
    new_master = master - learning * update
    return (new_master, new_first, new_second, new_master.astype(low))


def toeplitz_of(vector_row):
    wide = jnp.broadcast_to(vector_row, (128, vector_row.shape[1]))
    return pltpu.roll(wide, 0, 1, stride=1, stride_axis=0)


def attend_kernel(rows, q_ref, k_ref, v_ref, qseg_ref, kseg_ref, vec_ref, o_ref, p_ref, s_ref):
    keys = k_ref.shape[0]
    lane = lax.broadcasted_iota(jnp.int32, (rows, 128), 1)
    parts = []
    for head in range(2):
        mine = (lane < 64) if head == 0 else (lane >= 64)
        q_head = jnp.where(mine, q_ref[...], jnp.zeros((), low))
        s_ref[...] = ndot(q_head, k_ref[...])
        table = toeplitz_of(vec_ref[0, head : head + 1, :])
        for blk in range(rows // 128):
            here = slice(128 * blk, 128 * blk + 128)
            at = rows - 128 * blk
            scores = s_ref[here, :] + table[:, at : at + keys]
            scores = jnp.where(qseg_ref[here, :] == kseg_ref[...], scores, far_below)
            highest = jnp.max(scores, axis=1, keepdims=True)
            raised = jnp.exp(scores - highest)
            total = jnp.sum(raised, axis=1, keepdims=True)
            p_ref[head, here, :] = (raised * (1.0 / total)).astype(low)
        parts.append(mdot(p_ref[head], v_ref[...]))
    o_ref[...] = jnp.where(lane < 64, parts[0], parts[1]).astype(low)


def attend_back_kernel(
    rows, q_ref, k_ref, v_ref, do_ref, p_ref, dq_ref, dk_ref, dv_ref, diag_ref, s_ref, ds_ref, acc_ref
):
    keys = k_ref.shape[0]
    lane = lax.broadcasted_iota(jnp.int32, (rows, 128), 1)
    q_turned = q_ref[...].astype(full).T.astype(low)
    do_turned = do_ref[...].astype(full).T.astype(low)
    dq_parts, dk_parts, dv_parts = [], [], []
    for head in range(2):
        mine = (lane < 64) if head == 0 else (lane >= 64)
        do_head = jnp.where(mine, do_ref[...], jnp.zeros((), low))
        s_ref[...] = ndot(do_head, v_ref[...])
        acc_ref[...] = jnp.zeros_like(acc_ref)
        for blk in range(rows // 128):
            here = slice(128 * blk, 128 * blk + 128)
            at = rows - 128 * blk
            prob = p_ref[head, here, :].astype(full)
            grad = s_ref[here, :]
            delta = jnp.sum(prob * grad, axis=1, keepdims=True)
            dscore = (prob * (grad - delta)).astype(low)
            ds_ref[here, :] = dscore
            acc_ref[:, at : at + keys] += dscore.astype(full)
        dq_parts.append(mdot(ds_ref[...], k_ref[...]))
        own = slice(64 * head, 64 * head + 64)
        dk_parts.append(mdot(q_turned[own, :], ds_ref[...]))
        dv_parts.append(mdot(do_turned[own, :], p_ref[head]))
        summed = acc_ref[...]
        count = 128
        while count > 8:
            count //= 2
            width = summed.shape[1]
            summed = summed[:count] + pltpu.roll(summed[count:], width - count, 1)
        row = lax.broadcasted_iota(jnp.int32, summed.shape, 0)
        for bit in (1, 2, 4):
            turned = pltpu.roll(summed, summed.shape[1] - bit, 1)
            summed = jnp.where(jnp.bitwise_and(row, bit) > 0, turned, summed)
        diag_ref[0, head : head + 1, :] = jnp.sum(summed, axis=0, keepdims=True)
    dq_ref[...] = jnp.where(lane < 64, dq_parts[0], dq_parts[1]).astype(low)
    dk_ref[...] = jnp.concatenate(dk_parts, 0).T.astype(low)
    dv_ref[...] = jnp.concatenate(dv_parts, 0).T.astype(low)


def attend(query, key, value, query_seg, key_seg, vectors):
    rows, width = query.shape
    keys = key.shape[0]
    pairs = width // 128
    span = vectors.shape[-1]
    tall = pl.BlockSpec((rows, 128), lambda i: (0, i))
    wide = pl.BlockSpec((keys, 128), lambda i: (0, i))
    return pl.pallas_call(
        functools.partial(attend_kernel, rows),
        grid=(pairs,),
        in_specs=[
            tall,
            wide,
            wide,
            pl.BlockSpec((rows, 1), lambda i: (0, 0)),
            pl.BlockSpec((1, keys), lambda i: (0, 0)),
            pl.BlockSpec((1, 2, span), lambda i: (i, 0, 0)),
        ],
        out_specs=[tall, pl.BlockSpec((2, rows, keys), lambda i: (i, 0, 0))],
        out_shape=[
            jax.ShapeDtypeStruct((rows, width), low),
            jax.ShapeDtypeStruct((2 * pairs, rows, keys), low),
        ],
        scratch_shapes=[pltpu.VMEM((rows, keys), full)],
        name="attend",
        cost_estimate=pl.CostEstimate(
            flops=8 * pairs * rows * keys * 128,
            bytes_accessed=4 * pairs * rows * keys,
            transcendentals=2 * pairs * rows * keys,
        ),
    )(query, key, value, query_seg, key_seg, vectors.reshape(pairs, 2, span))


def attend_back(query, key, value, grad_out, probs, span):
    rows, width = query.shape
    keys = key.shape[0]
    pairs = width // 128
    tall = pl.BlockSpec((rows, 128), lambda i: (0, i))
    wide = pl.BlockSpec((keys, 128), lambda i: (0, i))
    return pl.pallas_call(
        functools.partial(attend_back_kernel, rows),
        grid=(pairs,),
        in_specs=[tall, wide, wide, tall, pl.BlockSpec((2, rows, keys), lambda i: (i, 0, 0))],
        out_specs=[tall, wide, wide, pl.BlockSpec((1, 2, span), lambda i: (i, 0, 0))],
        out_shape=[
            jax.ShapeDtypeStruct((rows, width), low),
            jax.ShapeDtypeStruct((keys, width), low),
            jax.ShapeDtypeStruct((keys, width), low),
            jax.ShapeDtypeStruct((pairs, 2, span), full),
        ],
        scratch_shapes=[
            pltpu.VMEM((rows, keys), full),
            pltpu.VMEM((rows, keys), low),
            pltpu.VMEM((128, span), full),
        ],
        name="attend_back",
        cost_estimate=pl.CostEstimate(
            flops=20 * pairs * rows * keys * 128,
            bytes_accessed=4 * pairs * rows * keys,
            transcendentals=0,
        ),
    )(query, key, value, grad_out, probs)


def xor(left, right):
    return jnp.bitwise_xor(left, right)


def by_shard(value, shard):
    pairs = value.reshape((2, 2) + value.shape[1:])
    pairs = jnp.where(shard % 2 == 1, pairs[:, ::-1], pairs)
    return jnp.where(shard // 2 == 1, pairs[::-1], pairs).reshape(value.shape)


def after(value, *others):
    return lax.optimization_barrier((value,) + others)[0]


def send(value, pairs):
    return lax.ppermute(
        value,
        ("plane", "core", "shard"),
        [((p * 2 + c) * 4 + z, (q * 2 + d) * 4 + w) for (p, c, z), (q, d, w) in pairs],
    )


ALL = [(p, c, z) for p in range(4) for c in range(2) for z in range(4)]


def plane_first(value):
    return send(value, [((p, c, z), (p ^ (1 + c), c, z)) for p, c, z in ALL])


def plane_second(value):
    return send(value, [((p, c, z), (p ^ (2 - c), c, z)) for p, c, z in ALL])


def across(value, step):
    return send(value, [((p, c, z), (p, c, z ^ step)) for p, c, z in ALL])


def turns(core):
    return (0, 1 + core, 2 - core, 3)


def stack_at(turn, core):
    return jnp.where((core == 1) & ((turn == 1) | (turn == 2)), 3 - turn, turn)


def tile_at(start, size):
    return pl.ds(pl.multiple_of(start, size), size)


vmem = pl.BlockSpec(memory_space=pltpu.VMEM)
anywhere = pl.BlockSpec(memory_space=pl.ANY)
fixed = pl.BlockSpec(memory_space=pltpu.HBM)


def call(kernel, spot, inputs, outputs, scratch, name, flops=0, grant=16, loose=()):
    arrays = [item[0] if isinstance(item, (tuple, list)) else item for item in inputs]
    specs = [
        anywhere if isinstance(item, tuple) else fixed if isinstance(item, list) else vmem for item in inputs
    ]
    return pl.pallas_call(
        kernel,
        in_specs=[pl.BlockSpec(memory_space=pltpu.SMEM)] + specs,
        out_specs=[anywhere if i in loose else vmem for i in range(len(outputs))],
        scratch_shapes=scratch,
        out_shape=[jax.ShapeDtypeStruct(shape, kind) for shape, kind in outputs],
        name=name,
        cost_estimate=pl.CostEstimate(flops=0, bytes_accessed=0, transcendentals=0),
        compiler_params=pltpu.CompilerParams(vmem_limit_bytes=grant << 20),
    )(spot, *arrays)


def fetch_part(source, target, sem):
    copy = pltpu.make_async_copy(source, target, sem)
    copy.start()
    return copy


def bring(pieces, near_ref, far_ref, sems, scalars):
    plane, core, shard = scalars[0], scalars[1], scalars[2]
    copies = []
    for k, turn in enumerate(turns(core)):
        quarter = xor(plane, turn)
        for step in (1, 2, 3):
            source = (near_ref, far_ref)[k // 2].at[3 * (k % 2) + step - 1]
            for part, target in pieces(source, quarter, xor(shard, step)):
                copies.append(fetch_part(part, target, sems.at[len(copies)]))
    return copies


def attend_all_kernel(scalars, q_ref, k_ref, v_ref, qseg_ref, kseg_ref, vec_ref, o_ref, p_out, s_ref, p_ref, sems):
    def leave(pair):
        here = pl.ds(2 * pair, 2)
        return pltpu.make_async_copy(p_ref.at[here], p_out.at[here], sems.at[pair])

    def one(pair, _):
        lanes = tile_at(128 * pair, 128)
        attend_kernel(
            512, q_ref.at[:, lanes], k_ref.at[:, lanes], v_ref.at[:, lanes], qseg_ref, kseg_ref,
            vec_ref.at[pl.ds(pair, 1)], o_ref.at[:, lanes], p_ref.at[pl.ds(2 * pair, 2)], s_ref,
        )
        leave(pair).start()
        return 0

    lax.fori_loop(0, 3, one, 0)
    for pair in range(3):
        leave(pair).wait()


def hot_buckets():
    relative = lax.broadcasted_iota(jnp.int32, (32, 1024), 1) - 512
    return jnp.where(bucket_of(relative) == lax.broadcasted_iota(jnp.int32, (32, 1024), 0), 1.0, 0.0)


def unpack_kernel(scalars, r0, pair, r3, gain_ref, vec_ref, bias_ref):
    core, shard = scalars[1], scalars[2]
    for z in range(4):
        rows = jnp.zeros((16, 384), full)
        for step, ref in enumerate((r0, pair.at[0], pair.at[1], r3)):
            rows = rows + jnp.where(xor(shard, step) == z, ref[192:208, :].astype(full), 0.0)
        gain_ref[:, 192 * z : 192 * z + 192] = rows[0:2, :192]
        bias_ref[8 * z : 8 * z + 8, :] = rows[2:10, :12]
    found = lax.dot_general(
        bias_ref[...], hot_buckets(), (((0,), (0,)), ((), ())),
        precision=lax.Precision.HIGHEST, preferred_element_type=full,
    )
    own = jnp.where(core == 0, found[0:6], found[6:12])
    for i in range(6):
        vec_ref[i // 2, i % 2 : i % 2 + 1, :] = own[i : i + 1]


def cat_kernel(rows, scalars, *refs):
    at = 0
    for ref in refs[:-1]:
        value = ref[...]
        if len(value.shape) == 2:
            value = value[None]
        refs[-1][at : at + value.shape[0]] = value[:, :rows]
        at += value.shape[0]


def cat(spot, pieces, rows, name):
    count = sum(1 if len(piece.shape) == 2 else piece.shape[0] for piece in pieces)
    shape = (count, rows, pieces[0].shape[-1])
    return call(functools.partial(cat_kernel, rows), spot, pieces, [(shape, pieces[0].dtype)], [], name, 0, 4)[0]


def pass_ffn_kernel(scalars, keep, first, out):
    def one(i, _):
        rows, later = tile_at(576 * i, 576), tile_at(2304 + 576 * i, 576)
        out[rows, :] = keep[later, :] + first[later, :]
        return 0

    lax.fori_loop(0, 4, one, 0)


def sum_ffn_kernel(scalars, keep, first, second, own, pair, far):
    for step, out in enumerate((own, pair.at[0:576], pair.at[576:1152], far)):
        rows = tile_at(576 * xor(scalars[2], step), 576)
        total = wide(keep[rows, :]) + wide(first[rows, :]) + wide(second[rows, :])
        out[...] = total.astype(out.dtype)


def pass_attn_kernel(scalars, keep, sent, first, out):
    out[0:768, :] = (wide(keep[768:1536, :]) + wide(first[768:1536, :])).astype(low)
    out[768:784, :] = (wide(sent[1536:1552, :]) + wide(first[1536:1552, :])).astype(low)


def sum_attn_kernel(scalars, keep, passed, first, second, own, pair, far):
    for step, out in enumerate((own, pair.at[0:208], pair.at[208:416], far)):
        rows = tile_at(192 * xor(scalars[2], step), 192)
        total = wide(keep[rows, :]) + wide(first[rows, :]) + wide(second[rows, :])
        out[0:192, :] = total.astype(out.dtype)
        small = wide(passed[768:784, :]) + wide(second[768:784, :])
        out[192:208, :] = small.astype(out.dtype)


def far_kernel(scalars, far, came, out):
    count = far.shape[0]
    out[...] = (far[...] + wide(came[count : 2 * count, :])).astype(low)


def total_kernel(scalars, own, near, far, out, *rest):
    total = own[...] + wide(near[0 : own.shape[0], :]) + wide(far[...])
    out[...] = total[: out.shape[0]].astype(low)
    if rest:
        rest[0][...] = total[out.shape[0] :]


def pack_attn_kernel(scalars, master_ref, gain_ref, bias_ref, out_ref, part_ref, gain_part, bias_part, sems):
    columns = tile_at(384 * scalars[1], 384)
    copies = [
        fetch_part(master_ref.at[scalars[0], :, columns], part_ref, sems.at[0]),
        fetch_part(gain_ref, gain_part, sems.at[1]),
        fetch_part(bias_ref, bias_part, sems.at[2]),
    ]
    for copy in copies:
        copy.wait()
    gains = jnp.concatenate([gain_part[...], jnp.zeros((2, 192), full)], 1)
    bias = jnp.concatenate([bias_part[...], jnp.zeros((8, 372), full)], 1)
    out_ref[192:208, :] = jnp.concatenate([gains, bias, jnp.zeros((6, 384), full)], 0).astype(low)
    out_ref[0:192, :] = part_ref[...].astype(low)


def pack_ffn_kernel(scalars, in_ref, out_ref, unit_ref, part_ref, rows_ref, sems):
    plane, core = scalars[0], scalars[1]
    copies = []
    for k in range(2):
        columns = tile_at(1024 * (plane % 2) + 512 * k + 256 * core, 256)
        copies.append(fetch_part(in_ref.at[plane // 2, :, columns], part_ref.at[k], sems.at[k]))
    rows = tile_at(256 * core + 64 * plane, 64)
    copies.append(fetch_part(out_ref.at[rows, :], rows_ref, sems.at[2]))
    for copy in copies:
        copy.wait()
    unit_ref[0:192, :] = part_ref[0].astype(low)
    unit_ref[192:384, :] = part_ref[1].astype(low)
    for i in range(3):
        unit_ref[384 + 64 * i : 448 + 64 * i, :] = rows_ref[:, 256 * i : 256 * i + 256].astype(low)


def project_kernel(
    scalars, x_ref, gain_ref, master_ref, near_ref, far_ref, w_ref, act_ref, q_ref, k_ref, v_ref, own_ref, sems
):
    columns = tile_at(384 * scalars[1], 384)
    own_copy = fetch_part(master_ref.at[:, :, columns], own_ref, sems.at[12])

    def pieces(source, quarter, shard):
        return [(source, w_ref.at[quarter, tile_at(192 * shard, 192), :])]

    copies = bring(pieces, near_ref, far_ref, sems, scalars)
    x_in = x_ref[...].astype(full)
    scale = lax.rsqrt(jnp.mean(x_in * x_in, axis=-1, keepdims=True) + norm_eps)
    act_ref[...] = (x_in * scale * gain_ref[0:1, :]).astype(low)
    own_copy.wait()
    for quarter in range(4):
        w_ref[quarter, tile_at(192 * scalars[2], 192), :] = own_ref[quarter].astype(low)
    for copy in copies:
        copy.wait()
    for quarter, out in enumerate((q_ref, k_ref, v_ref)):
        out[...] = mdot(act_ref[...], w_ref[quarter]).astype(low)


def gelu_parts(gate):
    inner = 0.7978845608028654 * (gate + 0.044715 * gate * gate * gate)
    bent = jnp.tanh(inner)
    slope = 0.7978845608028654 * (1.0 + 3.0 * 0.044715 * gate * gate)
    value = 0.5 * gate * (1.0 + bent)
    return value, 0.5 * (1.0 + bent) + 0.5 * gate * (1.0 - bent * bent) * slope


def feed_kernel(
    scalars, x_ref, mix_own, mix_other, w_attn, wo_other, gain_ref, gy_ref, in_master, out_master, near_ref, far_ref,
    mid_ref, act_ref, hid_ref, part_ref, y_ref, grad_ref,
    mix_ref, wo_ref, win_ref, wout_ref, own_ref, gate_ref, up_ref, sems,
):
    core, shard = scalars[1], scalars[2]
    own_copy = fetch_part(out_master.at[tile_at(256 * core, 256), :], own_ref, sems.at[60])

    def pieces(source, quarter, shard):
        rows = tile_at(192 * shard, 192)
        found = []
        for k in range(2):
            columns = tile_at(512 * (quarter % 2) + 256 * k, 256)
            found.append((source.at[192 * k : 192 * k + 192, :], win_ref.at[quarter // 2, rows, columns]))
        rows = tile_at(256 * shard + 64 * quarter, 64)
        for i in range(3):
            part = source.at[384 + 64 * i : 448 + 64 * i, :]
            found.append((part, wout_ref.at[rows, 256 * i : 256 * i + 256]))
        return found

    copies = bring(pieces, near_ref, far_ref, sems, scalars)
    here, there = tile_at(384 * core, 384), tile_at(384 * (1 - core), 384)
    mix_ref[:, here] = mix_own[...]
    mix_ref[:, there] = mix_other[...]
    wo_ref[:, here] = w_attn[...]
    wo_ref[:, there] = wo_other[...]

    def middle(half, _):
        rows = tile_at(256 * half, 256)
        x_mid = x_ref[rows, :].astype(full) + mdot(mix_ref[rows, :], wo_ref[...])
        mid_ref[rows, :] = x_mid
        scale = lax.rsqrt(jnp.mean(x_mid * x_mid, axis=-1, keepdims=True) + norm_eps)
        act_ref[rows, :] = (x_mid * scale * gain_ref[1:2, :]).astype(low)
        return 0

    lax.fori_loop(0, 2, middle, 0)
    for i in range(2):
        for k in range(4):
            pair = in_master[i, :, 512 * k : 512 * k + 512]
            win_ref[i, tile_at(192 * shard, 192), 256 * k : 256 * k + 256] = jnp.where(
                core == 0, pair[:, :256], pair[:, 256:]
            ).astype(low)
    own_copy.wait()
    wout_ref[tile_at(256 * shard, 256), :] = own_ref[...].astype(low)
    for copy in copies:
        copy.wait()

    def hidden(at, _):
        rows, columns = tile_at(256 * (at // 2), 256), tile_at(512 * (at % 2), 512)
        gate = mdot(act_ref[rows, :], win_ref[0, :, columns])
        up = mdot(act_ref[rows, :], win_ref[1, :, columns])
        value, slope = gelu_parts(gate)
        hid_ref[rows, columns] = (value * up).astype(low)
        gate_ref[rows, columns] = slope * up
        up_ref[rows, columns] = value
        return 0

    lax.fori_loop(0, 4, hidden, 0)

    def inner(half, _):
        rows = tile_at(256 * half, 256)
        part = jnp.zeros((256, 768), full)
        for h in range(2):
            columns = slice(512 * h, 512 * h + 512)
            grad_hid = ndot(gy_ref[rows, :], wout_ref[columns, :])
            grad_gate = (grad_hid * gate_ref[rows, columns]).astype(low)
            grad_up = (grad_hid * up_ref[rows, columns]).astype(low)
            grad_ref[h, rows, :] = grad_gate
            grad_ref[2 + h, rows, :] = grad_up
            part = part + ndot(grad_gate, win_ref[0, :, columns]) + ndot(grad_up, win_ref[1, :, columns])
        part_ref[rows, :] = part
        y_ref[rows, :] = mdot(hid_ref[rows, :], wout_ref[...])
        return 0

    lax.fori_loop(0, 2, inner, 0)


def inner_part(turned_ref, grad_ref, plane, core, odd, out):
    def one(j, _):
        turn = odd * (1 + core) + j * (2 - core)
        found = mdot(turned_ref[...], grad_ref[xor(plane, turn)]).astype(low)
        for z in range(4):
            for i in range(2):
                out[tile_at(2304 * j + 576 * z + 192 * i, 192), :] = found[
                    192 * z : 192 * z + 192, 256 * i : 256 * i + 256
                ]
        return 0

    lax.fori_loop(0, 2, one, 0)


def sent_kernel(scalars, act_ref, grad_ref, hid_ref, gy_ref, send_ref, kept_ref, turned_ref, sum_ref):
    plane, core = scalars[0], scalars[1]
    turned_ref[...] = act_ref[...].astype(full).T.astype(low)
    inner_part(turned_ref, grad_ref, plane, core, 1, send_ref)

    def last(z, _):
        sum_ref[...] = tdot(hid_ref[:, tile_at(256 * z, 256)], gy_ref[...])
        for k, turn in enumerate(turns(core)):
            found = sum_ref[tile_at(64 * xor(plane, turn), 64), :].astype(low)
            for i in range(3):
                part = found[:, 256 * i : 256 * i + 256]
                if k % 2:
                    send_ref[tile_at(2304 * (k // 2) + 576 * z + 384 + 64 * i, 64), :] = part
                else:
                    kept_ref[tile_at(768 * (k // 2) + 192 * z + 64 * i, 64), :] = part
        return 0

    lax.fori_loop(0, 4, last, 0)


def kept_kernel(scalars, act_ref, grad_ref, kept_ref, keep_ref, turned_ref):
    plane, core = scalars[0], scalars[1]
    turned_ref[...] = act_ref[...].astype(full).T.astype(low)
    inner_part(turned_ref, grad_ref, plane, core, 0, keep_ref)
    for j in range(2):
        for z in range(4):
            at = 2304 * j + 576 * z + 384
            keep_ref[at : at + 192, :] = kept_ref[768 * j + 192 * z : 768 * j + 192 * z + 192, :]


def pick_kernel(scalars, b0, b1, b2, b3, place_ref, token_ref, out_ref):
    def rows_of(half, _):
        rows = tile_at(256 * half, 256)
        total = jnp.zeros((256, 768), full)
        for i, ref in enumerate((b0, b1, b2, b3)):
            same = place_ref[:, 256 * i : 256 * i + 256] == token_ref[rows, :]
            total = total + mdot(jnp.where(same, 1.0, 0.0).astype(low), ref[...])
        out_ref[rows, :] = total.astype(low)
        return 0

    lax.fori_loop(0, 2, rows_of, 0)


def spread(wanted_ref, token_ref, value, near_ref, own_ref, far_ref):
    for step, out in enumerate((own_ref, near_ref.at[0:256], far_ref, near_ref.at[256:512])):
        same = wanted_ref[256 * step : 256 * step + 256, :] == token_ref[...]
        out[...] = mdot(jnp.where(same, 1.0, 0.0).astype(low), value).astype(low)


def spread_y_kernel(
    scalars, mid_ref, own_part, other_part, wanted_ref, token_ref, near_ref, own_ref, far_ref, value_ref, *rest
):
    parts = (mid_ref, own_part, other_part)
    copies = [fetch_part(ref, held, rest[-1].at[i]) for i, (ref, held) in enumerate(zip(parts, rest[:-1]))]
    for copy in copies:
        copy.wait()
    value_ref[...] = (rest[0][...] + rest[1][...] + rest[2][...]).astype(low)
    spread(wanted_ref, token_ref, value_ref[...], near_ref, own_ref, far_ref)


def spread_x_kernel(
    scalars, own_part, other_part, x_ref, gain_ref, mid_ref, wanted_ref, token_ref, near_ref, own_ref, far_ref,
    value_ref, *rest
):
    parts = (own_part, other_part, mid_ref, x_ref)
    copies = [fetch_part(ref, held, rest[-1].at[i]) for i, (ref, held) in enumerate(zip(parts, rest[:-1]))]
    for copy in copies:
        copy.wait()
    own_part, other_part, mid_ref, x_ref = rest[:-1]
    x_in = x_ref[...].astype(full)
    scale = lax.rsqrt(jnp.mean(x_in * x_in, axis=-1, keepdims=True) + norm_eps)
    turned = (own_part[...] + other_part[...]) * gain_ref[0:1, :]
    lean = jnp.mean(turned * x_in, axis=-1, keepdims=True)
    value_ref[...] = (mid_ref[...] + scale * turned - x_in * (scale * scale * scale * lean)).astype(low)
    spread(wanted_ref, token_ref, value_ref[...], near_ref, own_ref, far_ref)


def add_kernel(scalars, value_ref, more_ref, out_ref):
    out_ref[...] = value_ref[...] + more_ref[256:512, :]


def back_kernel(
    scalars, own_part, other_part, mid_ref, gy_ref, gain_ref, w_ref, wo_other, q_ref, k_ref, v_ref, p_ref,
    grad_ref, right_ref, lined_ref, gain_out, attn_ref, mixed_ref, s_ref, ds_ref, acc_ref, *rest
):
    core = scalars[1]
    here, there = tile_at(384 * core, 384), tile_at(384 * (1 - core), 384)
    late = (own_part, other_part, mid_ref, gy_ref, wo_other, w_ref, q_ref, k_ref, v_ref, p_ref)
    copies = [fetch_part(ref, held, rest[-1].at[i]) for i, (ref, held) in enumerate(zip(late, rest[:-1]))]
    own_part, other_part, mid_ref, gy_ref, wo_other, wo_own, q_ref, k_ref, v_ref, p_ref = rest[:-1]
    for copy in copies[:4]:
        copy.wait()
    x_mid = mid_ref[...]
    scale = lax.rsqrt(jnp.mean(x_mid * x_mid, axis=-1, keepdims=True) + norm_eps)
    gain_out[...] = jnp.sum(own_part[...] * x_mid * scale, axis=0, keepdims=True)
    turned = (own_part[...] + other_part[...]) * gain_ref[1:2, :]
    lean = jnp.mean(turned * x_mid, axis=-1, keepdims=True)
    grad_mid = gy_ref[...].astype(full) + scale * turned - x_mid * (scale * scale * scale * lean)
    grad_ref[...] = grad_mid
    attn_ref[...] = grad_mid.astype(low)
    for copy in copies[4:]:
        copy.wait()
    mixed_ref[...] = (
        ndot(attn_ref[:, here], wo_own[here, :]) + ndot(attn_ref[:, there], wo_other[here, :])
    ).astype(low)

    def one(pair, _):
        lanes = tile_at(128 * pair, 128)
        attend_back_kernel(
            512, *[ref.at[:, lanes] for ref in (q_ref, k_ref, v_ref, mixed_ref)], p_ref.at[pl.ds(2 * pair, 2)],
            *[right_ref.at[i, :, lanes] for i in range(3)], lined_ref.at[pl.ds(pair, 1)], s_ref, ds_ref, acc_ref,
        )
        return 0

    lax.fori_loop(0, 3, one, 0)
    right_ref[3] = attn_ref[:, here]


def last_kernel(
    scalars, act_ref, mix_own, mix_other, right_ref, w_ref, x_ref, lined_ref, other_ref,
    send_ref, keep_ref, part_ref, turned_ref, *rest
):
    plane, core = scalars[0], scalars[1]
    here, there = tile_at(384 * core, 384), tile_at(384 * (1 - core), 384)
    late = (act_ref, mix_own, mix_other, right_ref, w_ref, x_ref)
    copies = [fetch_part(ref, held, rest[-1].at[i]) for i, (ref, held) in enumerate(zip(late, rest[:-1]))]
    act_ref, mix_own, mix_other, right_ref, w_ref, x_ref = rest[:-1]
    for copy in copies:
        copy.wait()
    turned_ref[0] = act_ref[...].astype(full).T.astype(low)
    turned_ref[1, here, :] = mix_own[...].astype(full).T.astype(low)
    turned_ref[1, there, :] = mix_other[...].astype(full).T.astype(low)

    def outer(j, _):
        for odd, out in enumerate((keep_ref, send_ref)):
            quarter = xor(plane, odd * (1 + core) + j * (2 - core))
            out[tile_at(768 * j, 768), :] = mdot(turned_ref[quarter // 3], right_ref[quarter]).astype(low)
        return 0

    lax.fori_loop(0, 2, outer, 0)
    part = ndot(right_ref[0], w_ref[0]) + ndot(right_ref[1], w_ref[1]) + ndot(right_ref[2], w_ref[2])
    part_ref[...] = part
    x_in = x_ref[...].astype(full)
    scale = lax.rsqrt(jnp.mean(x_in * x_in, axis=-1, keepdims=True) + norm_eps)
    gain = jnp.sum(part * x_in * scale, axis=0, keepdims=True)
    lined = jnp.concatenate([lined_ref[0], lined_ref[1], lined_ref[2]], 0)
    table = lax.dot_general(
        lined, hot_buckets(), (((1,), (1,)), ((), ())),
        precision=lax.Precision.HIGHEST, preferred_element_type=full,
    )
    table = jnp.concatenate([table, jnp.zeros((6, 352), full)], 1)
    other = other_ref[...]
    send_ref[1536:1552, :] = jnp.concatenate(
        [gain[:, :384], gain[:, 384:], other[:, :384], other[:, 384:], table, jnp.zeros((6, 384), full)], 0
    ).astype(low)


def wide(value):
    return value.astype(full)


def adam_kernel(steps, count, scalars, *refs):
    plane, core = scalars[0], scalars[1]
    lower = core == 0
    states, grads, outs = refs[:3], refs[3:5], refs[5 : 5 + count]
    own, other, brought, held, sems = refs[5 + count], refs[6 + count], refs[7 + count : 10 + count], refs[-5:-1], refs[-1]
    arrive = [fetch_part(grads[0], own, sems.at[8]), fetch_part(grads[1], other, sems.at[9])]
    loads = []
    for number, (where, _, _, _) in enumerate(steps):
        loads.append(
            [fetch_part(where(state), brought[i].at[number], sems.at[10 + 3 * number + i]) for i, state in enumerate(states)]
        )
    for copy in arrive:
        copy.wait()

    def place(own, other, quarter):
        turn = xor(plane, quarter)
        return own.at[stack_at(turn, core)], other.at[stack_at(turn, 1 - core)]

    flying = []
    for number, (_, quarter, read, targets) in enumerate(steps):
        slot = number % 2
        if number >= 2:
            for copy in flying[number - 2]:
                copy.wait()
        if quarter is None:
            grad = read(own, other, place, lower).astype(full)
        else:
            grad = read(*place(own, other, quarter), lower).astype(full)
        for copy in loads[number]:
            copy.wait()
        new = adam_step(brought[0][number], brought[1][number], brought[2][number], grad, True)
        copies = []
        for i, value in enumerate(new):
            order = (0, 1, 3, 2)[i]
            held[order][slot] = value
            copies.append(fetch_part(held[order].at[slot], targets(outs, i), sems.at[4 * slot + i]))
        flying.append(copies)
    for copies in flying[-2:]:
        for copy in copies:
            copy.wait()


def adam_call(spot, steps, block, states, grads, outputs, name):
    return call(
        functools.partial(adam_kernel, steps, len(outputs)), spot,
        [*[[state] for state in states], *[(grad,) for grad in grads]], outputs,
        [
            *[pltpu.VMEM(grads[0].shape, low)] * 2, *[pltpu.VMEM((len(steps),) + block, full)] * 3,
            *[pltpu.VMEM((2,) + block, full)] * 2, pltpu.VMEM((2,) + block, low), pltpu.VMEM((2,) + block, full),
            pltpu.SemaphoreType.DMA((10 + 3 * len(steps),)),
        ],
        name, 0, 60, range(len(outputs)),
    )


def small_kernel(
    scalars, own, other, gm_ref, gf_ref, gs_ref, bm_ref, bf_ref, bs_ref, gain_step, gain_first, gain_second,
    bias_step, bias_first, bias_second, table_ref,
):
    core, shard = scalars[1], scalars[2]
    total = own[...] + other[...]
    grads = []
    for j in range(2):
        row = jnp.where(shard // 2 == 1, total[2 * j + 1 : 2 * j + 2], total[2 * j : 2 * j + 1])
        grads.append(jnp.where(shard % 2 == 1, row[:, 192:], row[:, :192]))
    new = adam_step(gm_ref[...], gf_ref[...], gs_ref[...], jnp.concatenate(grads, 0), False)
    gain_step[...], gain_first[...], gain_second[...] = new[0] - gm_ref[...], new[1], new[2]
    mine, theirs = own[4:10, :32], other[4:10, :32]
    table = jnp.concatenate(chosen(core == 0, mine, theirs), 0)
    same = lax.broadcasted_iota(jnp.int32, (32, 32), 0) == lax.broadcasted_iota(jnp.int32, (32, 32), 1)
    table_ref[...] = lax.dot_general(
        jnp.where(same, 1.0, 0.0), table, (((1,), (1,)), ((), ())),
        precision=lax.Precision.HIGHEST, preferred_element_type=full,
    )
    grad = table_ref[tile_at(8 * shard, 8), :]
    new = adam_step(bm_ref[...], bf_ref[...], bs_ref[...], grad, False)
    bias_step[...], bias_first[...], bias_second[...] = new[0] - bm_ref[...], new[1], new[2]


def chosen(lower, mine, theirs):
    return jnp.where(lower, mine, theirs), jnp.where(lower, theirs, mine)


def attn_steps():
    def one(m):
        where = lambda ref: ref.at[m]

        def read(mine, theirs, lower):
            return jnp.concatenate(chosen(lower, mine[...], theirs[...]), 1)

        def targets(outs, i):
            if i == 2:
                return outs[2].at[m] if m < 3 else outs[3]
            return outs[(0, 1, 2, 4)[i]].at[m]

        return where, m, read, targets

    return [one(m) for m in range(4)]


def ffin_steps():
    def one(i, h):
        columns = slice(1024 * h, 1024 * h + 1024)
        where = lambda ref: ref.at[i, :, columns]

        def read(mine, theirs, lower):
            left, right = chosen(lower, mine[0:384, :], theirs[0:384, :])
            return jnp.concatenate([left[:192], right[:192], left[192:], right[192:]], 1)

        return where, 2 * i + h, read, lambda outs, n: where(outs[n])

    return [one(i, h) for i in range(2) for h in range(2)]


def ffout_steps():
    def one(c):
        rows = slice(256 * c, 256 * c + 256)
        where = lambda ref: ref.at[rows, :]

        def read(own, other, place, lower):
            found = []
            for q in range(4):
                mine, theirs = place(own, other, q)
                value = chosen(lower, mine[384:576, :], theirs[384:576, :])[c]
                found.append(jnp.concatenate([value[:64], value[64:128], value[128:]], 1))
            return jnp.concatenate(found, 0)

        return where, None, read, lambda outs, n: where(outs[n])

    return [one(c) for c in range(2)]


def body_fast(
    tokens,
    cotangent,
    lengths,
    deal,
    attn_master,
    ffin_master,
    ffout_master,
    gain_master,
    bias_master,
    attn_first,
    ffin_first,
    ffout_first,
    gain_first,
    bias_first,
    attn_second,
    ffin_second,
    ffout_second,
    gain_second,
    bias_second,
):
    plane, core, shard = (lax.axis_index(name) for name in ("plane", "core", "shard"))
    spot = jnp.stack([plane, core, shard])
    group, rest = shard // 2, shard % 2
    mine = group == core

    quarter = call(
        pack_attn_kernel, spot, [[attn_master], [gain_master], [bias_master]], [((208, 384), low)],
        [
            pltpu.VMEM((192, 384), full), pltpu.VMEM((2, 192), full), pltpu.VMEM((8, 12), full),
            pltpu.SemaphoreType.DMA((3,)),
        ],
        "pack_attn", 0, 60,
    )[0]
    attn_third = across(quarter, 3)

    unit = call(
        pack_ffn_kernel, spot, [[ffin_master], [ffout_master]], [((576, 256), low)],
        [pltpu.VMEM((2, 192, 256), full), pltpu.VMEM((64, 768), full), pltpu.SemaphoreType.DMA((3,))],
        "pack_ffn", 0, 60,
    )[0]
    attn_third = after(attn_third, unit)
    attn_pair = across(cat(spot, [quarter, attn_third], 208, "pair_attn_in"), 1)

    up_pairs = lambda pairs: [((p, 1, z), (p, 1, w)) for p in range(4) for z, w in pairs]
    down_pairs = lambda pairs: [((p, 0, 3 - z), (p, 0, 3 - w)) for p in range(4) for z, w in pairs]
    along = lambda value, *which: send(value, up_pairs(which) + down_pairs(which))

    def fetch_rest(own, one, gate=None):
        two = along(one, (1, 2), (2, 3))
        two = two if gate is None else after(two, gate)
        three = along(jnp.where(at_end, own, two), (2, 3), (3, 2))
        return own, one, two, three

    way = 1 - 2 * core
    at_end = shard == 3 * core
    blocks = jnp.stack(
        [shard, shard + way, shard + 2 * way, jnp.where(at_end, shard + 3 * way, shard - way)]
    )
    blocks = jnp.clip(blocks, 0, 3)
    tok_blocks = fetch_rest(tokens[0], along(tokens[0], (0, 1), (1, 2), (2, 3)))

    table_own = jnp.concatenate([lengths[0], deal[0]])
    table = jnp.where(mine, table_own, swap(table_own))
    lens, order = table[:4], table[4:]
    starts = jnp.cumsum(lens) - lens
    long_start = jnp.sum(jnp.where(lens == 512, starts, 0))
    at_half = jnp.arange(512, dtype=jnp.int32)
    token_here = jnp.where(rest == 0, long_start + at_half, at_half + 512 * (at_half >= long_start))
    seg_here = jnp.sum((token_here[:, None] >= starts[None, :]).astype(jnp.int32), axis=1)
    token_index = jnp.arange(1024, dtype=jnp.int32)

    token_column = token_here[:, None]
    token_row = jnp.where(mine, token_here, -1)[None, :]

    def wanted_by(place_of):
        rows = [lax.dynamic_slice_in_dim(place_of, 256 * xor(shard, step), 256) for step in range(4)]
        return jnp.concatenate(rows).reshape(1024, 1)

    wanted_y = wanted_by(order)
    wanted_x = wanted_by(token_index)

    def rows_here(place_of, pieces, gate=None):
        place = [lax.dynamic_slice_in_dim(place_of, blocks[i] * 256, 256) for i in range(4)]
        place = jnp.concatenate(place).reshape(1, 1024)
        chosen = call(
            pick_kernel, spot, [*pieces, after(place, wanted_y, wanted_x, token_row), token_column], [((512, 768), low)], [], "pick", 0, 8
        )[0]
        chosen = chosen if gate is None else after(chosen, *gate)
        return jnp.where(mine, chosen, swap(chosen))

    def rows_near(rows, *gates):
        pairs = [((p, c, z), (p, c, z ^ 1)) for p, c, z in ALL if z // 2 == c]
        return after(send(rows[0], pairs), *gates)

    def rows_far(rows, came, *gates):
        pairs = [((p, c, z), (p, c, z ^ 2)) for p, c, z in ALL if z // 2 == c]
        far = call(add_kernel, spot, [rows[2], came], [((256, 768), low)], [], "add_rows", 0, 4)[0]
        return after(send(far, pairs), *gates)

    def rows_back(rows, first_gate, second_gate):
        pairs = lambda step: [((p, c, z), (p, c, z ^ step)) for p, c, z in ALL if z // 2 == c]
        near, own, far = rows
        came = after(send(near, pairs(1)), first_gate)
        far = call(add_kernel, spot, [far, came], [((256, 768), low)], [], "add_rows", 0, 4)[0]
        last = after(send(far, pairs(2)), second_gate)
        return own + came[:256] + last, last


    gains, vectors = call(
        unpack_kernel, spot, [quarter, attn_pair, attn_third], [((2, 768), full), ((3, 2, 1024), full)],
        [pltpu.VMEM((32, 12), full)], "unpack", 0, 8,
    )

    def spread_plane(pieces, rows, gate=None, late=None):
        near = cat(spot, pieces, rows, "near")
        arrived = plane_first(near)
        if gate is not None:
            arrived = after(arrived, *gate)
        near = cat(spot, [near, arrived], rows, "nearest")
        return near, plane_second(near if late is None else after(near, late))

    unit = after(unit, attn_third)
    ffn_third = across(unit, 3)
    ffn_two = cat(spot, [unit, ffn_third], 576, "pair_ffn_in")
    near, far = spread_plane([attn_pair, attn_third], 192, [ffn_two])
    ffn_pair_in = across(ffn_two, 1)
    ffn_came = [ffn_pair_in, ffn_third]
    x_low = rows_here(token_index, tok_blocks, (far, *ffn_came))
    w_attn, act_one, query, key, value = call(
        project_kernel, spot,
        [x_low, gains, [attn_master], (near,), (far,)],
        [((4, 768, 384), low), ((512, 768), low)] + [((512, 384), low)] * 3,
        [pltpu.VMEM((4, 192, 384), full), pltpu.SemaphoreType.DMA((13,))], "project", 0, 60,
    )
    wo_own = w_attn[3]
    wo_other = swap(wo_own)


    cot_own = after(cotangent[0], *ffn_came)
    cot_one = along(cot_own, (1, 2), (2, 3))
    cot_two = along(cot_own, (0, 2), (1, 3))
    cot_three = along(cot_own, (0, 3), (3, 2))
    ffn_near, ffn_far = spread_plane(ffn_came, 576, [query, cot_one])
    mix_own, probs = call(
        attend_all_kernel, spot, [after(query, ffn_near), key, value, seg_here[:, None], seg_here[None, :], vectors],
        [((512, 384), low), ((6, 512, 512), low)],
        [pltpu.VMEM((512, 512), full), pltpu.VMEM((6, 512, 512), low), pltpu.SemaphoreType.DMA((3,))],
        "attend", 0, 60, (1,),
    )
    cot_blocks = (cot_own, *[after(piece, mix_own) for piece in (cot_one, cot_two, cot_three)])
    grad_y = rows_here(order, cot_blocks)
    mix_other = swap(mix_own)
    x_mid, act_two, hidden, part_two, y_part, grads_up = call(
        feed_kernel, spot,
        [
            x_low, mix_own, mix_other, wo_own, wo_other, gains, grad_y, ffin_master, [ffout_master],
            (ffn_near,), (ffn_far,),
        ],
        [
            ((512, 768), full), ((512, 768), low), ((512, 1024), low), ((512, 768), full), ((512, 768), full),
            ((4, 512, 512), low),
        ],
        [
            pltpu.VMEM((512, 768), low), pltpu.VMEM((768, 768), low), pltpu.VMEM((2, 768, 1024), low),
            pltpu.VMEM((1024, 768), low), pltpu.VMEM((256, 768), full), pltpu.VMEM((512, 1024), full),
            pltpu.VMEM((512, 1024), full), pltpu.SemaphoreType.DMA((61,)),
        ],
        "feed", 0, 24,
    )
    ffn_send, out_kept = call(
        sent_kernel, spot, [act_two, grads_up, hidden, grad_y], [((4608, 256), low), ((1536, 256), low)],
        [pltpu.VMEM((768, 512), low), pltpu.VMEM((256, 768), full)], "sent", 0, 12,
    )
    ffn_first = plane_first(ffn_send)
    ffn_keep = call(
        kept_kernel, spot, [act_two, after(grads_up, ffn_send), out_kept], [((4608, 256), low)],
        [pltpu.VMEM((768, 512), low)], "kept", 0, 12,
    )[0]
    part_other = after(swap(part_two), ffn_keep)

    grad_mid, right, lined, gain_two = call(
        back_kernel, spot,
        [
            (part_two,), (part_other,), (x_mid,), (grad_y,), gains, (wo_own,), (wo_other,),
            (query,), (key,), (value,), (probs,),
        ],
        [
            ((512, 768), full), ((4, 512, 384), low), ((3, 2, 1024), full), ((1, 768), full),
        ],
        [
            pltpu.VMEM((512, 768), low), pltpu.VMEM((512, 384), low), pltpu.VMEM((512, 512), full), pltpu.VMEM((512, 512), low),
            pltpu.VMEM((128, 1024), full), *[pltpu.VMEM((512, 768), full)] * 3, pltpu.VMEM((512, 768), low),
            *[pltpu.VMEM((768, 384), low)] * 2, *[pltpu.VMEM((512, 384), low)] * 3, pltpu.VMEM((6, 512, 512), low),
            pltpu.SemaphoreType.DMA((10,)),
        ],
        "back", 0, 60,
    )
    y_other = swap(after(y_part, part_other))
    y_rows = call(
        spread_y_kernel, spot, [(x_mid,), (after(y_part, right),), (y_other,), wanted_y, token_row],
        [((512, 768), low), ((256, 768), low), ((256, 768), low)],
        [pltpu.VMEM((512, 768), low), *[pltpu.VMEM((512, 768), full)] * 3, pltpu.SemaphoreType.DMA((3,))],
        "spread_y", 0, 60,
    )
    ffn_first = after(ffn_first, right, y_rows[0])
    one_out = lambda kernel, inputs, shape, name: call(kernel, spot, inputs, [(shape, low)], [], name, 0, 8)[0]
    ffn_passed = one_out(pass_ffn_kernel, [ffn_keep, ffn_first], (2304, 256), "pass_ffn")
    ffn_second = plane_second(ffn_passed)
    attn_send, attn_keep, part_one = call(
        last_kernel, spot,
        [
            (after(act_one, ffn_passed),), (mix_own,), (mix_other,), (right,), (w_attn,), (x_low,), lined, gain_two,
        ],
        [((1552, 384), low), ((1536, 384), low), ((512, 768), full)],
        [
            pltpu.VMEM((2, 768, 512), low), pltpu.VMEM((512, 768), low), *[pltpu.VMEM((512, 384), low)] * 2,
            pltpu.VMEM((4, 512, 384), low), pltpu.VMEM((4, 768, 384), low), pltpu.VMEM((512, 768), low),
            pltpu.SemaphoreType.DMA((6,)),
        ],
        "last", 0, 60,
    )
    y_near = rows_near([after(y_rows[0], ffn_passed)], part_one)
    ffn_second = after(ffn_second, part_one, y_near)
    ffn_own, ffn_two, ffn_far = call(
        sum_ffn_kernel, spot, [ffn_keep, ffn_first, ffn_second],
        [((576, 256), full), ((1152, 256), low), ((576, 256), full)], [], "sum_ffn", 0, 8,
    )
    ffn_near = across(ffn_two, 1)
    x_rows = call(
        spread_x_kernel, spot,
        [(part_one,), (swap(part_one),), (x_low,), gains, (grad_mid,), wanted_x, token_row],
        [((512, 768), low), ((256, 768), low), ((256, 768), low)],
        [
            pltpu.VMEM((512, 768), low), *[pltpu.VMEM((512, 768), full)] * 3, pltpu.VMEM((512, 768), low),
            pltpu.SemaphoreType.DMA((4,)),
        ],
        "spread_x", 0, 60,
    )
    ffn_send = call(far_kernel, spot, [ffn_far, after(ffn_near, *x_rows)], [((576, 256), low)], [], "far_ffn", 0, 8)[0]
    ffn_last = across(ffn_send, 3)
    attn_first_came = after(plane_first(after(attn_send, ffn_second)), ffn_send, *x_rows)
    passed = one_out(pass_attn_kernel, [attn_keep, attn_send, attn_first_came], (784, 384), "pass_attn")
    attn_second_came = plane_second(passed)
    attn_own, attn_two, attn_far = call(
        sum_attn_kernel, spot, [attn_keep, passed, attn_first_came, attn_second_came],
        [((208, 384), full), ((416, 384), low), ((208, 384), full)], [], "sum_attn", 0, 8,
    )

    attn_near_came = across(attn_two, 1)
    ffn_last = after(ffn_last, attn_two)
    ffn_sum = one_out(total_kernel, [ffn_own, ffn_near, ffn_last], (576, 256), "total_ffn")
    attn_far_send = call(far_kernel, spot, [attn_far, attn_near_came], [((208, 384), low)], [], "far_attn", 0, 8)[0]
    attn_last = across(attn_far_send, 3)
    ffn_pair = cat(spot, [ffn_sum, after(plane_first(ffn_sum), attn_far_send)], 576, "pair_ffn")
    ffn_stack = cat(spot, [ffn_pair, after(plane_second(ffn_pair), attn_last)], 576, "stack_ffn")
    ffn_sum = (ffn_stack, swap(ffn_stack))
    flat, wide_in = (512, 768), (2, 192, 2048)
    ffin_res = adam_call(
        spot, ffin_steps(), (192, 1024), [ffin_master, ffin_first, ffin_second], ffn_sum,
        [(wide_in, full), (wide_in, full), (wide_in, full), (wide_in, low)], "adam_ffin",
    )
    ffout_res = adam_call(
        spot, ffout_steps(), (256, 768), [ffout_master, ffout_first, ffout_second], ffn_sum,
        [(flat, full), (flat, full), (flat, full), (flat, low)], "adam_ffout",
    )
    attn_sum, small = call(
        total_kernel, spot, [attn_own, attn_near_came, after(attn_last, ffn_stack)],
        [((192, 384), low), ((16, 384), full)], [], "total_attn", 0, 8,
    )
    attn_near = cat(spot, [attn_sum, after(plane_first(attn_sum), ffin_res[0])], 192, "pair_attn")
    attn_stack = cat(spot, [attn_near, after(plane_second(attn_near), ffout_res[0])], 192, "stack_attn")
    attn_sum = (attn_stack, swap(attn_stack))
    x_rows = [after(value, small) for value in x_rows]
    y_far = rows_far(y_rows, after(y_near, small), ffin_res[0])
    layer_out = y_rows[1] + y_near[:256] + y_far
    input_grad, _ = rows_back(x_rows, ffin_res[0], ffout_res[0])
    small_other = swap(small)
    square = (4, 192, 768)
    attn_res = adam_call(
        spot, attn_steps(), (192, 768), [attn_master, attn_first, attn_second], attn_sum,
        [(square, full), (square, full), ((3, 192, 768), full), ((192, 768), full), (square, low)], "adam_attn",
    )
    smalls = call(
        small_kernel, spot,
        [small, small_other, gain_master, gain_first, gain_second, bias_master, bias_first, bias_second],
        [((2, 192), full)] * 3 + [((8, 12), full)] * 3, [pltpu.VMEM((32, 12), full)], "adam_small", 0, 4,
    )
    return (
        layer_out[None],
        input_grad[None],
        attn_res[0],
        ffin_res[0],
        ffout_res[0],
        smalls[0],
        smalls[3],
        attn_res[1],
        ffin_res[1],
        ffout_res[1],
        smalls[1],
        smalls[4],
        attn_res[2],
        attn_res[3],
        ffin_res[2],
        ffout_res[2],
        smalls[2],
        smalls[5],
        attn_res[4],
        ffin_res[3],
        ffout_res[3],
    )


def body_any(
    tokens,
    cotangent,
    lengths,
    deal,
    attn_master,
    ffin_master,
    ffout_master,
    gain_master,
    bias_master,
    attn_first,
    ffin_first,
    ffout_first,
    gain_first,
    bias_first,
    attn_second,
    ffin_second,
    ffout_second,
    gain_second,
    bias_second,
):
    shards = lax.axis_size("shard")
    core = lax.axis_index("core")
    shard = lax.axis_index("shard")
    tok_rows, model = tokens.shape[1], tokens.shape[2]
    heads = bias_master.shape[1]
    own_heads = heads // 2
    part = model // 2
    whole_len = tok_rows * shards
    half_len = whole_len // 2
    per_half = shards // 4
    rows = half_len // per_half
    place, sub = shard // per_half, shard % per_half
    group, rest = place // 2, place % 2
    mine = group == core
    siblings = [[a * per_half + b for b in range(per_half)] for a in range(4)]

    def join_half(value):
        if per_half == 1:
            return value
        return lax.all_gather(value, "shard", axis=0, tiled=True, axis_index_groups=siblings)

    table_own = jnp.concatenate([lengths[0], deal[0]])
    table = jnp.where(mine, table_own, swap(table_own))
    count = lengths.shape[1]
    lens, order = table[:count], table[count:]
    starts = jnp.cumsum(lens) - lens
    long_start = jnp.sum(jnp.where(lens == half_len, starts, 0))
    at_half = jnp.arange(half_len, dtype=jnp.int32)
    token_half = jnp.where(
        rest == 0, long_start + at_half, at_half + half_len * (at_half >= long_start)
    )
    seg_half = jnp.sum((token_half[:, None] >= starts[None, :]).astype(jnp.int32), axis=1)
    first_row = sub * rows
    token_here = lax.dynamic_slice_in_dim(token_half, first_row, rows)
    seg_here = lax.dynamic_slice_in_dim(seg_half, first_row, rows)

    def rows_here(place_of, own):
        gathered = lax.all_gather(own, "shard", axis=0, tiled=True)
        gathered = jnp.where(mine, gathered, swap(gathered))
        picked = (place_of[None, :] == token_here[:, None]).astype(low)
        return mdot(picked, gathered).astype(low)

    def rows_back(place_of, here):
        picked = (place_of[:, None] == token_here[None, :]) & mine
        spread = mdot(picked.astype(low), here).astype(low)
        return lax.psum_scatter(spread, "shard", scatter_dimension=0, tiled=True)

    ff_rows = ffout_master.shape[0]
    ff_part = ff_rows // 2
    attn_low = attn_master.astype(low)
    cols = lax.dynamic_slice_in_dim(attn_low[:3], core * part, part, 2)
    ffin_low = ffin_master.astype(low).reshape(2, -1, shards, 2, ff_part)
    ffin_low = lax.dynamic_index_in_dim(ffin_low, core, 3, keepdims=False)
    ffin_low = ffin_low.reshape(2, -1, shards * ff_part)
    ffout_low = lax.dynamic_slice_in_dim(ffout_master.astype(low), core * ff_part, ff_part, 0)
    w_qkv = lax.all_gather(cols, "shard", axis=1, tiled=True)
    w_o = lax.all_gather(attn_low[3], "shard", axis=0, tiled=True)
    w_in = lax.all_gather(ffin_low, "shard", axis=1, tiled=True)
    w_out = lax.all_gather(ffout_low, "shard", axis=0, tiled=True)
    gains = lax.all_gather(gain_master.astype(low), "shard", axis=1, tiled=True).astype(full)
    bias = lax.all_gather(bias_master.astype(low), "shard", axis=0, tiled=True).astype(full)

    token_index = jnp.arange(whole_len, dtype=jnp.int32)
    x_low = rows_here(token_index, tokens[0])
    grad_y = rows_here(order, cotangent[0])

    x_in = x_low.astype(full)
    scale_one = lax.rsqrt(jnp.mean(x_in * x_in, axis=-1, keepdims=True) + norm_eps)
    act_one = (x_in * scale_one * gains[0]).astype(low)
    query = mdot(act_one, w_qkv[0]).astype(low)
    key_own = mdot(act_one, w_qkv[1]).astype(low)
    value_own = mdot(act_one, w_qkv[2]).astype(low)
    key, value = join_half(key_own), join_half(value_own)
    span = rows + half_len
    relative = jnp.arange(span, dtype=jnp.int32) - rows - first_row
    ids = jnp.arange(bias.shape[0], dtype=jnp.int32)
    one_hot = (bucket_of(relative)[None, :] == ids[:, None]).astype(full)
    bias_own = lax.dynamic_slice_in_dim(bias, core * own_heads, own_heads, 1)
    vectors = lax.dot_general(
        bias_own, one_hot, (((0,), (0,)), ((), ())), precision=lax.Precision.HIGHEST
    )
    mix_own, probs = attend(
        query, key, value, seg_here[:, None], seg_half[None, :], vectors
    )
    mix = both_cores(mix_own, swap(mix_own), core, 1)
    x_mid = x_in + mdot(mix, w_o)
    scale_two = lax.rsqrt(jnp.mean(x_mid * x_mid, axis=-1, keepdims=True) + norm_eps)
    act_two = (x_mid * scale_two * gains[1]).astype(low)
    gate_pre = mdot(act_two, w_in[0])
    up_pre = mdot(act_two, w_in[1])
    gated, gelu_pull = jax.vjp(
        lambda gate_val, up_val: jax.nn.gelu(gate_val, approximate=True) * up_val, gate_pre, up_pre
    )
    hidden = gated.astype(low)
    y_part = mdot(hidden, w_out)
    y_here = (x_mid + y_part + swap(y_part)).astype(low)
    layer_out = rows_back(order, y_here)

    grad_gate, grad_up = gelu_pull(ndot(grad_y, w_out))
    grad_gate, grad_up = grad_gate.astype(low), grad_up.astype(low)
    d_out = tdot(hidden, grad_y).astype(low)
    d_in = jnp.stack([tdot(act_two, grad_gate), tdot(act_two, grad_up)]).astype(low)
    part_two = ndot(grad_gate, w_in[0]) + ndot(grad_up, w_in[1])
    grad_act_two = part_two + swap(part_two)
    turned = grad_act_two * gains[1]
    grad_mid = (
        grad_y.astype(full)
        + scale_two * turned
        - x_mid * scale_two**3 * jnp.mean(turned * x_mid, axis=-1, keepdims=True)
    )
    d_gain_two = jnp.sum(grad_act_two * x_mid * scale_two, axis=0)
    grad_attn = grad_mid.astype(low)
    w_o_own = lax.dynamic_slice_in_dim(w_o, core * part, part, 0)
    grad_mix = ndot(grad_attn, w_o_own).astype(low)
    d_wo = tdot(mix, lax.dynamic_slice_in_dim(grad_attn, core * part, part, 1)).astype(low)
    grad_q, grad_k, grad_v, diagonals = attend_back(query, key, value, grad_mix, probs, span)
    if per_half > 1:
        grad_k = lax.psum_scatter(
            grad_k, "shard", scatter_dimension=0, tiled=True, axis_index_groups=siblings
        )
        grad_v = lax.psum_scatter(
            grad_v, "shard", scatter_dimension=0, tiled=True, axis_index_groups=siblings
        )
    d_wq = tdot(act_one, grad_q).astype(low)
    d_wk = tdot(act_one, grad_k).astype(low)
    d_wv = tdot(act_one, grad_v).astype(low)
    part_one = ndot(grad_q, w_qkv[0]) + ndot(grad_k, w_qkv[1]) + ndot(grad_v, w_qkv[2])
    grad_act_one = part_one + swap(part_one)
    turned = grad_act_one * gains[0]
    grad_x = (
        grad_mid
        + scale_one * turned
        - x_in * scale_one**3 * jnp.mean(turned * x_in, axis=-1, keepdims=True)
    ).astype(low)
    d_gain_one = jnp.sum(grad_act_one * x_in * scale_one, axis=0)
    input_grad = rows_back(token_index, grad_x)

    lined = diagonals.reshape(own_heads, span)
    table_own = lax.dot_general(
        one_hot, lined, (((1,), (1,)), ((), ())), precision=lax.Precision.HIGHEST
    )
    empty = jnp.zeros_like(table_own)
    grad_table = jnp.where(
        core == 0,
        jnp.concatenate([table_own, empty], 1),
        jnp.concatenate([empty, table_own], 1),
    )
    grad_gain = jnp.where(core == 0, jnp.stack([d_gain_one, d_gain_two]), 0.0)

    d_attn = jnp.stack([d_wq, d_wk, d_wv, d_wo])

    def reduced(grad, axis):
        share = lax.psum_scatter(grad, "shard", scatter_dimension=axis, tiled=True)
        return lax.psum(share, "plane")

    g_attn = reduced(d_attn, 1)
    g_attn = both_cores(g_attn, swap(g_attn), core, 2).astype(full)
    g_in = reduced(d_in, 1)
    g_in = g_in.reshape(2, -1, shards, 1, ff_part)
    g_in = both_cores(g_in, swap(g_in), core, 3).reshape(ffin_master.shape).astype(full)
    g_out = reduced(d_out, 0)
    g_out = both_cores(g_out, swap(g_out), core, 0).astype(full)
    g_gain, g_bias = lax.psum((grad_gain, grad_table), ("plane", "core", "shard"))
    own_gain = gain_master.shape[1]
    g_gain = lax.dynamic_slice_in_dim(g_gain, shard * own_gain, own_gain, 1)
    own_bias = bias_master.shape[0]
    g_bias = lax.dynamic_slice_in_dim(g_bias, shard * own_bias, own_bias, 0)

    attn_res = adam_step(attn_master, attn_first, attn_second, g_attn, True)
    ffin_res = adam_step(ffin_master, ffin_first, ffin_second, g_in, True)
    ffout_res = adam_step(ffout_master, ffout_first, ffout_second, g_out, True)
    gain_res = adam_step(gain_master, gain_first, gain_second, g_gain, False)
    bias_res = adam_step(bias_master, bias_first, bias_second, g_bias, False)
    return (
        layer_out[None],
        input_grad[None],
        attn_res[0],
        ffin_res[0],
        ffout_res[0],
        gain_res[0] - gain_master,
        bias_res[0] - bias_master,
        attn_res[1],
        ffin_res[1],
        ffout_res[1],
        gain_res[1],
        bias_res[1],
        attn_res[2][:3],
        attn_res[2][3],
        ffin_res[2],
        ffout_res[2],
        gain_res[2],
        bias_res[2],
        attn_res[3],
        ffin_res[3],
        ffout_res[3],
    )


def solution(mesh):
    reps, shards = mesh.devices.shape
    cores = Mesh(mesh.devices.reshape(reps // 2, 2, shards), ("plane", "core", "shard"))
    rep = ("plane", "core")
    tok = P(rep, "shard", None)
    row = P(rep, None)
    second = P(None, "shard", None)
    first = P("shard", None)
    gain = P(None, "shard")
    states = (second, second, first, gain, first)
    in_specs = (tok, tok, row, row) + states * 3
    out_specs = (
        (tok, tok) + states + states + (second, first, second, first, gain, first) + states[:3]
    )
    body = body_fast if (reps, shards) == (8, 4) else body_any
    return jax.shard_map(body, mesh=cores, in_specs=in_specs, out_specs=out_specs, check_vma=False)
```

```python
import functools

import jax
import jax.numpy as jnp
from jax import lax
from jax.experimental import pallas as pl
from jax.experimental.pallas import tpu as pltpu
from jax.sharding import Mesh
from jax.sharding import PartitionSpec as P

norm_eps = 1e-06
far_below = -1e30
steps_beyond = (12, 16, 23, 32, 46, 64, 91)
first_rate = 0.9
second_rate = 0.95
learning = 0.05
shrink = 0.1
adam_eps = 1e-08
first_fix = 1.0 - 0.9**8
second_fix = 1.0 - 0.95**8
chips = ("plane", "shard")
low = jnp.bfloat16
full = jnp.float32


def bucket_of(relative):
    distance = jnp.abs(relative)
    beyond = 8 + sum(((distance >= threshold).astype(jnp.int32) for threshold in steps_beyond))
    near_part = jnp.where(distance < 8, distance, beyond)
    return near_part + 16 * (relative > 0).astype(jnp.int32)


def ndot(left, right):
    return lax.dot_general(left, right, (((1,), (1,)), ((), ())), preferred_element_type=full)


def tdot(left, right):
    return lax.dot_general(left, right, (((0,), (0,)), ((), ())), preferred_element_type=full)


def mdot(left, right):
    return jnp.dot(left, right, preferred_element_type=full)


def swap(value):
    return lax.ppermute(value, "core", [(0, 1), (1, 0)])


def both_cores(mine, other, core, axis):
    first = jnp.where(core == 0, mine, other)
    second = jnp.where(core == 0, other, mine)
    return jnp.concatenate([first, second], axis)


def adam_step(master, first, second, grad, decayed):
    new_first = first_rate * first + (1.0 - first_rate) * grad
    new_second = second_rate * second + (1.0 - second_rate) * grad * grad
    update = new_first / first_fix / (jnp.sqrt(new_second / second_fix) + adam_eps)
    if decayed:
        update = update + shrink * master
    new_master = master - learning * update
    return (new_master, new_first, new_second, new_master.astype(low))


def toeplitz_of(vector_row):
    wide = jnp.broadcast_to(vector_row, (128, vector_row.shape[1]))
    return pltpu.roll(wide, 0, 1, stride=1, stride_axis=0)


def attend_kernel(rows, q_ref, k_ref, v_ref, qseg_ref, kseg_ref, vec_ref, o_ref, p_ref, s_ref):
    keys = k_ref.shape[0]
    lane = lax.broadcasted_iota(jnp.int32, (rows, 128), 1)
    parts = []
    for head in range(2):
        mine = (lane < 64) if head == 0 else (lane >= 64)
        q_head = jnp.where(mine, q_ref[...], jnp.zeros((), low))
        s_ref[...] = ndot(q_head, k_ref[...])
        table = toeplitz_of(vec_ref[0, head : head + 1, :])
        for blk in range(rows // 128):
            here = slice(128 * blk, 128 * blk + 128)
            at = rows - 128 * blk
            scores = s_ref[here, :] + table[:, at : at + keys]
            scores = jnp.where(qseg_ref[here, :] == kseg_ref[...], scores, far_below)
            highest = jnp.max(scores, axis=1, keepdims=True)
            raised = jnp.exp(scores - highest)
            total = jnp.sum(raised, axis=1, keepdims=True)
            p_ref[head, here, :] = (raised * (1.0 / total)).astype(low)
        parts.append(mdot(p_ref[head], v_ref[...]))
    o_ref[...] = jnp.where(lane < 64, parts[0], parts[1]).astype(low)


def attend_back_kernel(
    rows, q_ref, k_ref, v_ref, do_ref, p_ref, dq_ref, dk_ref, dv_ref, diag_ref, s_ref, ds_ref, acc_ref
):
    keys = k_ref.shape[0]
    lane = lax.broadcasted_iota(jnp.int32, (rows, 128), 1)
    q_turned = q_ref[...].astype(full).T.astype(low)
    do_turned = do_ref[...].astype(full).T.astype(low)
    dq_parts, dk_parts, dv_parts = [], [], []
    for head in range(2):
        mine = (lane < 64) if head == 0 else (lane >= 64)
        do_head = jnp.where(mine, do_ref[...], jnp.zeros((), low))
        s_ref[...] = ndot(do_head, v_ref[...])
        acc_ref[...] = jnp.zeros_like(acc_ref)
        for blk in range(rows // 128):
            here = slice(128 * blk, 128 * blk + 128)
            at = rows - 128 * blk
            prob = p_ref[head, here, :].astype(full)
            grad = s_ref[here, :]
            delta = jnp.sum(prob * grad, axis=1, keepdims=True)
            dscore = (prob * (grad - delta)).astype(low)
            ds_ref[here, :] = dscore
            acc_ref[:, at : at + keys] += dscore.astype(full)
        dq_parts.append(mdot(ds_ref[...], k_ref[...]))
        own = slice(64 * head, 64 * head + 64)
        dk_parts.append(mdot(q_turned[own, :], ds_ref[...]))
        dv_parts.append(mdot(do_turned[own, :], p_ref[head]))
        summed = acc_ref[...]
        count = 128
        while count > 8:
            count //= 2
            width = summed.shape[1]
            summed = summed[:count] + pltpu.roll(summed[count:], width - count, 1)
        row = lax.broadcasted_iota(jnp.int32, summed.shape, 0)
        for bit in (1, 2, 4):
            turned = pltpu.roll(summed, summed.shape[1] - bit, 1)
            summed = jnp.where(jnp.bitwise_and(row, bit) > 0, turned, summed)
        diag_ref[0, head : head + 1, :] = jnp.sum(summed, axis=0, keepdims=True)
    dq_ref[...] = jnp.where(lane < 64, dq_parts[0], dq_parts[1]).astype(low)
    dk_ref[...] = jnp.concatenate(dk_parts, 0).T.astype(low)
    dv_ref[...] = jnp.concatenate(dv_parts, 0).T.astype(low)


def attend(query, key, value, query_seg, key_seg, vectors):
    rows, width = query.shape
    keys = key.shape[0]
    pairs = width // 128
    span = vectors.shape[-1]
    tall = pl.BlockSpec((rows, 128), lambda i: (0, i))
    wide = pl.BlockSpec((keys, 128), lambda i: (0, i))
    return pl.pallas_call(
        functools.partial(attend_kernel, rows),
        grid=(pairs,),
        in_specs=[
            tall,
            wide,
            wide,
            pl.BlockSpec((rows, 1), lambda i: (0, 0)),
            pl.BlockSpec((1, keys), lambda i: (0, 0)),
            pl.BlockSpec((1, 2, span), lambda i: (i, 0, 0)),
        ],
        out_specs=[tall, pl.BlockSpec((2, rows, keys), lambda i: (i, 0, 0))],
        out_shape=[
            jax.ShapeDtypeStruct((rows, width), low),
            jax.ShapeDtypeStruct((2 * pairs, rows, keys), low),
        ],
        scratch_shapes=[pltpu.VMEM((rows, keys), full)],
        name="attend",
        cost_estimate=pl.CostEstimate(
            flops=8 * pairs * rows * keys * 128,
            bytes_accessed=4 * pairs * rows * keys,
            transcendentals=2 * pairs * rows * keys,
        ),
    )(query, key, value, query_seg, key_seg, vectors.reshape(pairs, 2, span))


def attend_back(query, key, value, grad_out, probs, span):
    rows, width = query.shape
    keys = key.shape[0]
    pairs = width // 128
    tall = pl.BlockSpec((rows, 128), lambda i: (0, i))
    wide = pl.BlockSpec((keys, 128), lambda i: (0, i))
    return pl.pallas_call(
        functools.partial(attend_back_kernel, rows),
        grid=(pairs,),
        in_specs=[tall, wide, wide, tall, pl.BlockSpec((2, rows, keys), lambda i: (i, 0, 0))],
        out_specs=[tall, wide, wide, pl.BlockSpec((1, 2, span), lambda i: (i, 0, 0))],
        out_shape=[
            jax.ShapeDtypeStruct((rows, width), low),
            jax.ShapeDtypeStruct((keys, width), low),
            jax.ShapeDtypeStruct((keys, width), low),
            jax.ShapeDtypeStruct((pairs, 2, span), full),
        ],
        scratch_shapes=[
            pltpu.VMEM((rows, keys), full),
            pltpu.VMEM((rows, keys), low),
            pltpu.VMEM((128, span), full),
        ],
        name="attend_back",
        cost_estimate=pl.CostEstimate(
            flops=20 * pairs * rows * keys * 128,
            bytes_accessed=4 * pairs * rows * keys,
            transcendentals=0,
        ),
    )(query, key, value, grad_out, probs)


def xor(left, right):
    return jnp.bitwise_xor(left, right)


def by_shard(value, shard):
    pairs = value.reshape((2, 2) + value.shape[1:])
    pairs = jnp.where(shard % 2 == 1, pairs[:, ::-1], pairs)
    return jnp.where(shard // 2 == 1, pairs[::-1], pairs).reshape(value.shape)


def after(value, *others):
    return lax.optimization_barrier((value,) + others)[0]


def send(value, pairs):
    return lax.ppermute(
        value,
        ("plane", "core", "shard"),
        [((p * 2 + c) * 4 + z, (q * 2 + d) * 4 + w) for (p, c, z), (q, d, w) in pairs],
    )


ALL = [(p, c, z) for p in range(4) for c in range(2) for z in range(4)]


def plane_first(value):
    return send(value, [((p, c, z), (p ^ (1 + c), c, z)) for p, c, z in ALL])


def plane_second(value):
    return send(value, [((p, c, z), (p ^ (2 - c), c, z)) for p, c, z in ALL])


def across(value, step):
    return send(value, [((p, c, z), (p, c, z ^ step)) for p, c, z in ALL])


def turns(core):
    return (0, 1 + core, 2 - core, 3)


def stack_at(turn, core):
    return jnp.where((core == 1) & ((turn == 1) | (turn == 2)), 3 - turn, turn)


def tile_at(start, size):
    return pl.ds(pl.multiple_of(start, size), size)


vmem = pl.BlockSpec(memory_space=pltpu.VMEM)
anywhere = pl.BlockSpec(memory_space=pl.ANY)
fixed = pl.BlockSpec(memory_space=pltpu.HBM)


def call(kernel, spot, inputs, outputs, scratch, name, flops=0, grant=16, loose=()):
    arrays = [item[0] if isinstance(item, (tuple, list)) else item for item in inputs]
    specs = [
        anywhere if isinstance(item, tuple) else fixed if isinstance(item, list) else vmem for item in inputs
    ]
    return pl.pallas_call(
        kernel,
        in_specs=[pl.BlockSpec(memory_space=pltpu.SMEM)] + specs,
        out_specs=[anywhere if i in loose else vmem for i in range(len(outputs))],
        scratch_shapes=scratch,
        out_shape=[jax.ShapeDtypeStruct(shape, kind) for shape, kind in outputs],
        name=name,
        cost_estimate=pl.CostEstimate(flops=0, bytes_accessed=0, transcendentals=0),
        compiler_params=pltpu.CompilerParams(vmem_limit_bytes=grant << 20),
    )(spot, *arrays)


def fetch_part(source, target, sem):
    copy = pltpu.make_async_copy(source, target, sem)
    copy.start()
    return copy


def bring(pieces, near_ref, far_ref, sems, scalars):
    plane, core, shard = scalars[0], scalars[1], scalars[2]
    copies = []
    for k, turn in enumerate(turns(core)):
        quarter = xor(plane, turn)
        for step in (1, 2, 3):
            source = (near_ref, far_ref)[k // 2].at[3 * (k % 2) + step - 1]
            for part, target in pieces(source, quarter, xor(shard, step)):
                copies.append(fetch_part(part, target, sems.at[len(copies)]))
    return copies


def attend_all_kernel(scalars, q_ref, k_ref, v_ref, qseg_ref, kseg_ref, vec_ref, o_ref, p_out, s_ref, p_ref, sems):
    def leave(pair):
        here = pl.ds(2 * pair, 2)
        return pltpu.make_async_copy(p_ref.at[here], p_out.at[here], sems.at[pair])

    def one(pair, _):
        lanes = tile_at(128 * pair, 128)
        attend_kernel(
            512, q_ref.at[:, lanes], k_ref.at[:, lanes], v_ref.at[:, lanes], qseg_ref, kseg_ref,
            vec_ref.at[pl.ds(pair, 1)], o_ref.at[:, lanes], p_ref.at[pl.ds(2 * pair, 2)], s_ref,
        )
        leave(pair).start()
        return 0

    lax.fori_loop(0, 3, one, 0)
    for pair in range(3):
        leave(pair).wait()


def hot_buckets():
    relative = lax.broadcasted_iota(jnp.int32, (32, 1024), 1) - 512
    return jnp.where(bucket_of(relative) == lax.broadcasted_iota(jnp.int32, (32, 1024), 0), 1.0, 0.0)


def unpack_kernel(scalars, r0, pair, r3, gain_ref, vec_ref, bias_ref):
    core, shard = scalars[1], scalars[2]
    for z in range(4):
        rows = jnp.zeros((16, 384), full)
        for step, ref in enumerate((r0, pair.at[0], pair.at[1], r3)):
            rows = rows + jnp.where(xor(shard, step) == z, ref[192:208, :].astype(full), 0.0)
        gain_ref[:, 192 * z : 192 * z + 192] = rows[0:2, :192]
        bias_ref[8 * z : 8 * z + 8, :] = rows[2:10, :12]
    found = lax.dot_general(
        bias_ref[...], hot_buckets(), (((0,), (0,)), ((), ())),
        precision=lax.Precision.HIGHEST, preferred_element_type=full,
    )
    own = jnp.where(core == 0, found[0:6], found[6:12])
    for i in range(6):
        vec_ref[i // 2, i % 2 : i % 2 + 1, :] = own[i : i + 1]


def cat_kernel(rows, scalars, *refs):
    at = 0
    for ref in refs[:-1]:
        value = ref[...]
        if len(value.shape) == 2:
            value = value[None]
        refs[-1][at : at + value.shape[0]] = value[:, :rows]
        at += value.shape[0]


def cat(spot, pieces, rows, name):
    count = sum(1 if len(piece.shape) == 2 else piece.shape[0] for piece in pieces)
    shape = (count, rows, pieces[0].shape[-1])
    return call(functools.partial(cat_kernel, rows), spot, pieces, [(shape, pieces[0].dtype)], [], name, 0, 4)[0]


def pass_ffn_kernel(scalars, keep, first, out):
    def one(i, _):
        rows, later = tile_at(576 * i, 576), tile_at(2304 + 576 * i, 576)
        out[rows, :] = keep[later, :] + first[later, :]
        return 0

    lax.fori_loop(0, 4, one, 0)


def sum_ffn_kernel(scalars, keep, first, second, own_out, pair, far_out, own, far, sems):
    copies = []
    for step, out in ((0, own), (3, far), (1, pair.at[0:576]), (2, pair.at[576:1152])):
        rows = tile_at(576 * xor(scalars[2], step), 576)
        total = wide(keep[rows, :]) + wide(first[rows, :]) + wide(second[rows, :])
        out[...] = total.astype(out.dtype)
        if step in (0, 3):
            copies.append(fetch_part(out, own_out if step == 0 else far_out, sems.at[step // 3]))
    for copy in copies:
        copy.wait()


def pass_attn_kernel(scalars, keep, sent, first, out):
    out[0:768, :] = (wide(keep[768:1536, :]) + wide(first[768:1536, :])).astype(low)
    out[768:784, :] = (wide(sent[1536:1552, :]) + wide(first[1536:1552, :])).astype(low)


def sum_attn_kernel(scalars, keep, passed, first, second, own, pair, far):
    for step, out in enumerate((own, pair.at[0:208], pair.at[208:416], far)):
        rows = tile_at(192 * xor(scalars[2], step), 192)
        total = wide(keep[rows, :]) + wide(first[rows, :]) + wide(second[rows, :])
        out[0:192, :] = total.astype(out.dtype)
        small = wide(passed[768:784, :]) + wide(second[768:784, :])
        out[192:208, :] = small.astype(out.dtype)


def far_kernel(scalars, far, came, out):
    count = far.shape[0]
    out[...] = (far[...] + wide(came[count : 2 * count, :])).astype(low)


def total_kernel(scalars, own, near, far, out, *rest):
    total = own[...] + wide(near[0 : own.shape[0], :]) + wide(far[...])
    out[...] = total[: out.shape[0]].astype(low)
    if rest:
        rest[0][...] = total[out.shape[0] :]


def pack_attn_kernel(scalars, master_ref, gain_ref, bias_ref, out_ref, part_ref, gain_part, bias_part, sems):
    columns = tile_at(384 * scalars[1], 384)
    copies = [
        fetch_part(master_ref.at[scalars[0], :, columns], part_ref, sems.at[0]),
        fetch_part(gain_ref, gain_part, sems.at[1]),
        fetch_part(bias_ref, bias_part, sems.at[2]),
    ]
    for copy in copies:
        copy.wait()
    gains = jnp.concatenate([gain_part[...], jnp.zeros((2, 192), full)], 1)
    bias = jnp.concatenate([bias_part[...], jnp.zeros((8, 372), full)], 1)
    out_ref[192:208, :] = jnp.concatenate([gains, bias, jnp.zeros((6, 384), full)], 0).astype(low)
    out_ref[0:192, :] = part_ref[...].astype(low)


def pack_ffn_kernel(scalars, in_ref, out_ref, unit_ref, part_ref, rows_ref, sems):
    plane, core = scalars[0], scalars[1]
    copies = []
    for k in range(2):
        columns = tile_at(1024 * (plane % 2) + 512 * k + 256 * core, 256)
        copies.append(fetch_part(in_ref.at[plane // 2, :, columns], part_ref.at[k], sems.at[k]))
    rows = tile_at(256 * core + 64 * plane, 64)
    copies.append(fetch_part(out_ref.at[rows, :], rows_ref, sems.at[2]))
    for copy in copies:
        copy.wait()
    unit_ref[0:192, :] = part_ref[0].astype(low)
    unit_ref[192:384, :] = part_ref[1].astype(low)
    for i in range(3):
        unit_ref[384 + 64 * i : 448 + 64 * i, :] = rows_ref[:, 256 * i : 256 * i + 256].astype(low)


def project_kernel(
    scalars, x_ref, gain_ref, master_ref, near_ref, far_ref, w_ref, act_ref, q_ref, k_ref, v_ref, own_ref, sems
):
    columns = tile_at(384 * scalars[1], 384)
    own_copy = fetch_part(master_ref.at[:, :, columns], own_ref, sems.at[12])

    def pieces(source, quarter, shard):
        return [(source, w_ref.at[quarter, tile_at(192 * shard, 192), :])]

    copies = bring(pieces, near_ref, far_ref, sems, scalars)
    x_in = x_ref[...].astype(full)
    scale = lax.rsqrt(jnp.mean(x_in * x_in, axis=-1, keepdims=True) + norm_eps)
    act_ref[...] = (x_in * scale * gain_ref[0:1, :]).astype(low)
    own_copy.wait()
    for quarter in range(4):
        w_ref[quarter, tile_at(192 * scalars[2], 192), :] = own_ref[quarter].astype(low)
    for copy in copies:
        copy.wait()
    for quarter, out in enumerate((q_ref, k_ref, v_ref)):
        out[...] = mdot(act_ref[...], w_ref[quarter]).astype(low)


def gelu_parts(gate):
    inner = 0.7978845608028654 * (gate + 0.044715 * gate * gate * gate)
    bent = jnp.tanh(inner)
    slope = 0.7978845608028654 * (1.0 + 3.0 * 0.044715 * gate * gate)
    value = 0.5 * gate * (1.0 + bent)
    return value, 0.5 * (1.0 + bent) + 0.5 * gate * (1.0 - bent * bent) * slope


def feed_kernel(
    scalars, x_ref, mix_own, mix_other, w_attn, wo_other, gain_ref, gy_ref, in_master, out_master, near_ref, far_ref,
    mid_ref, act_ref, hid_ref, part_ref, y_ref, grad_ref,
    mix_ref, wo_ref, win_ref, wout_ref, own_ref, gate_ref, up_ref, sems,
):
    core, shard = scalars[1], scalars[2]
    own_copy = fetch_part(out_master.at[tile_at(256 * core, 256), :], own_ref, sems.at[60])

    def pieces(source, quarter, shard):
        rows = tile_at(192 * shard, 192)
        found = []
        for k in range(2):
            columns = tile_at(512 * (quarter % 2) + 256 * k, 256)
            found.append((source.at[192 * k : 192 * k + 192, :], win_ref.at[quarter // 2, rows, columns]))
        rows = tile_at(256 * shard + 64 * quarter, 64)
        for i in range(3):
            part = source.at[384 + 64 * i : 448 + 64 * i, :]
            found.append((part, wout_ref.at[rows, 256 * i : 256 * i + 256]))
        return found

    copies = bring(pieces, near_ref, far_ref, sems, scalars)
    here, there = tile_at(384 * core, 384), tile_at(384 * (1 - core), 384)
    mix_ref[:, here] = mix_own[...]
    mix_ref[:, there] = mix_other[...]
    wo_ref[:, here] = w_attn[...]
    wo_ref[:, there] = wo_other[...]

    def middle(half, _):
        rows = tile_at(256 * half, 256)
        x_mid = x_ref[rows, :].astype(full) + mdot(mix_ref[rows, :], wo_ref[...])
        mid_ref[rows, :] = x_mid
        scale = lax.rsqrt(jnp.mean(x_mid * x_mid, axis=-1, keepdims=True) + norm_eps)
        act_ref[rows, :] = (x_mid * scale * gain_ref[1:2, :]).astype(low)
        return 0

    lax.fori_loop(0, 2, middle, 0)
    for i in range(2):
        for k in range(4):
            pair = in_master[i, :, 512 * k : 512 * k + 512]
            win_ref[i, tile_at(192 * shard, 192), 256 * k : 256 * k + 256] = jnp.where(
                core == 0, pair[:, :256], pair[:, 256:]
            ).astype(low)
    own_copy.wait()
    wout_ref[tile_at(256 * shard, 256), :] = own_ref[...].astype(low)
    for copy in copies:
        copy.wait()

    def hidden(at, _):
        rows, columns = tile_at(256 * (at // 2), 256), tile_at(512 * (at % 2), 512)
        gate = mdot(act_ref[rows, :], win_ref[0, :, columns])
        up = mdot(act_ref[rows, :], win_ref[1, :, columns])
        value, slope = gelu_parts(gate)
        hid_ref[rows, columns] = (value * up).astype(low)
        gate_ref[rows, columns] = slope * up
        up_ref[rows, columns] = value
        return 0

    lax.fori_loop(0, 4, hidden, 0)

    def inner(half, _):
        rows = tile_at(256 * half, 256)
        part = jnp.zeros((256, 768), full)
        for h in range(2):
            columns = slice(512 * h, 512 * h + 512)
            grad_hid = ndot(gy_ref[rows, :], wout_ref[columns, :])
            grad_gate = (grad_hid * gate_ref[rows, columns]).astype(low)
            grad_up = (grad_hid * up_ref[rows, columns]).astype(low)
            grad_ref[h, rows, :] = grad_gate
            grad_ref[2 + h, rows, :] = grad_up
            part = part + ndot(grad_gate, win_ref[0, :, columns]) + ndot(grad_up, win_ref[1, :, columns])
        part_ref[rows, :] = part
        y_ref[rows, :] = mdot(hid_ref[rows, :], wout_ref[...])
        return 0

    lax.fori_loop(0, 2, inner, 0)


def inner_part(turned_ref, grad_ref, plane, core, odd, out):
    def one(j, _):
        turn = odd * (1 + core) + j * (2 - core)
        found = mdot(turned_ref[...], grad_ref[xor(plane, turn)]).astype(low)
        for z in range(4):
            for i in range(2):
                out[tile_at(2304 * j + 576 * z + 192 * i, 192), :] = found[
                    192 * z : 192 * z + 192, 256 * i : 256 * i + 256
                ]
        return 0

    lax.fori_loop(0, 2, one, 0)


def sent_kernel(scalars, act_ref, grad_ref, hid_ref, gy_ref, send_ref, kept_ref, turned_ref, sum_ref):
    plane, core = scalars[0], scalars[1]
    turned_ref[...] = act_ref[...].astype(full).T.astype(low)
    inner_part(turned_ref, grad_ref, plane, core, 1, send_ref)

    def last(z, _):
        sum_ref[...] = tdot(hid_ref[:, tile_at(256 * z, 256)], gy_ref[...])
        for k, turn in enumerate(turns(core)):
            found = sum_ref[tile_at(64 * xor(plane, turn), 64), :].astype(low)
            for i in range(3):
                part = found[:, 256 * i : 256 * i + 256]
                if k % 2:
                    send_ref[tile_at(2304 * (k // 2) + 576 * z + 384 + 64 * i, 64), :] = part
                else:
                    kept_ref[tile_at(768 * (k // 2) + 192 * z + 64 * i, 64), :] = part
        return 0

    lax.fori_loop(0, 4, last, 0)


def kept_kernel(scalars, act_ref, grad_ref, kept_ref, keep_ref, turned_ref):
    plane, core = scalars[0], scalars[1]
    turned_ref[...] = act_ref[...].astype(full).T.astype(low)
    inner_part(turned_ref, grad_ref, plane, core, 0, keep_ref)
    for j in range(2):
        for z in range(4):
            at = 2304 * j + 576 * z + 384
            keep_ref[at : at + 192, :] = kept_ref[768 * j + 192 * z : 768 * j + 192 * z + 192, :]


def pick_kernel(scalars, b0, b1, b2, b3, place_ref, token_ref, out_ref):
    def rows_of(half, _):
        rows = tile_at(256 * half, 256)
        total = jnp.zeros((256, 768), full)
        for i, ref in enumerate((b0, b1, b2, b3)):
            same = place_ref[:, 256 * i : 256 * i + 256] == token_ref[rows, :]
            total = total + mdot(jnp.where(same, 1.0, 0.0).astype(low), ref[...])
        out_ref[rows, :] = total.astype(low)
        return 0

    lax.fori_loop(0, 2, rows_of, 0)


def spread(wanted_ref, token_ref, value, near_ref, own_ref, far_ref):
    for step, out in enumerate((own_ref, near_ref.at[0:256], far_ref, near_ref.at[256:512])):
        same = wanted_ref[256 * step : 256 * step + 256, :] == token_ref[...]
        out[...] = mdot(jnp.where(same, 1.0, 0.0).astype(low), value).astype(low)


def spread_y_kernel(
    scalars, mid_ref, own_part, other_part, wanted_ref, token_ref, near_ref, own_ref, far_ref, value_ref, *rest
):
    parts = (mid_ref, own_part, other_part)
    copies = [fetch_part(ref, held, rest[-1].at[i]) for i, (ref, held) in enumerate(zip(parts, rest[:-1]))]
    for copy in copies:
        copy.wait()
    value_ref[...] = (rest[0][...] + rest[1][...] + rest[2][...]).astype(low)
    spread(wanted_ref, token_ref, value_ref[...], near_ref, own_ref, far_ref)


def spread_x_kernel(
    scalars, own_part, other_part, x_ref, gain_ref, mid_ref, wanted_ref, token_ref, near_ref, own_ref, far_ref,
    value_ref, *rest
):
    parts = (own_part, other_part, mid_ref, x_ref)
    copies = [fetch_part(ref, held, rest[-1].at[i]) for i, (ref, held) in enumerate(zip(parts, rest[:-1]))]
    for copy in copies:
        copy.wait()
    own_part, other_part, mid_ref, x_ref = rest[:-1]
    x_in = x_ref[...].astype(full)
    scale = lax.rsqrt(jnp.mean(x_in * x_in, axis=-1, keepdims=True) + norm_eps)
    turned = (own_part[...] + other_part[...]) * gain_ref[0:1, :]
    lean = jnp.mean(turned * x_in, axis=-1, keepdims=True)
    value_ref[...] = (mid_ref[...] + scale * turned - x_in * (scale * scale * scale * lean)).astype(low)
    spread(wanted_ref, token_ref, value_ref[...], near_ref, own_ref, far_ref)


def add_kernel(scalars, value_ref, more_ref, out_ref):
    out_ref[...] = value_ref[...] + more_ref[256:512, :]


def back_kernel(
    scalars, own_part, other_part, mid_ref, gy_ref, gain_ref, w_ref, wo_other, q_ref, k_ref, v_ref, p_ref,
    grad_ref, right_ref, lined_ref, gain_out, attn_ref, mixed_ref, s_ref, ds_ref, acc_ref, *rest
):
    core = scalars[1]
    here, there = tile_at(384 * core, 384), tile_at(384 * (1 - core), 384)
    late = (own_part, other_part, mid_ref, gy_ref, wo_other, w_ref, q_ref, k_ref, v_ref, p_ref)
    copies = [fetch_part(ref, held, rest[-1].at[i]) for i, (ref, held) in enumerate(zip(late, rest[:-1]))]
    own_part, other_part, mid_ref, gy_ref, wo_other, wo_own, q_ref, k_ref, v_ref, p_ref = rest[:-1]
    for copy in copies[:4]:
        copy.wait()
    x_mid = mid_ref[...]
    scale = lax.rsqrt(jnp.mean(x_mid * x_mid, axis=-1, keepdims=True) + norm_eps)
    gain_out[...] = jnp.sum(own_part[...] * x_mid * scale, axis=0, keepdims=True)
    turned = (own_part[...] + other_part[...]) * gain_ref[1:2, :]
    lean = jnp.mean(turned * x_mid, axis=-1, keepdims=True)
    grad_mid = gy_ref[...].astype(full) + scale * turned - x_mid * (scale * scale * scale * lean)
    grad_ref[...] = grad_mid
    attn_ref[...] = grad_mid.astype(low)
    for copy in copies[4:]:
        copy.wait()
    mixed_ref[...] = (
        ndot(attn_ref[:, here], wo_own[here, :]) + ndot(attn_ref[:, there], wo_other[here, :])
    ).astype(low)

    def one(pair, _):
        lanes = tile_at(128 * pair, 128)
        attend_back_kernel(
            512, *[ref.at[:, lanes] for ref in (q_ref, k_ref, v_ref, mixed_ref)], p_ref.at[pl.ds(2 * pair, 2)],
            *[right_ref.at[i, :, lanes] for i in range(3)], lined_ref.at[pl.ds(pair, 1)], s_ref, ds_ref, acc_ref,
        )
        return 0

    lax.fori_loop(0, 3, one, 0)
    right_ref[3] = attn_ref[:, here]


def last_kernel(
    scalars, act_ref, mix_own, mix_other, right_ref, w_ref, x_ref, lined_ref, other_ref,
    send_ref, keep_ref, part_ref, turned_ref, *rest
):
    plane, core = scalars[0], scalars[1]
    here, there = tile_at(384 * core, 384), tile_at(384 * (1 - core), 384)
    late = (act_ref, mix_own, mix_other, right_ref, w_ref, x_ref)
    copies = [fetch_part(ref, held, rest[-1].at[i]) for i, (ref, held) in enumerate(zip(late, rest[:-1]))]
    act_ref, mix_own, mix_other, right_ref, w_ref, x_ref = rest[:-1]
    for copy in copies:
        copy.wait()
    turned_ref[0] = act_ref[...].astype(full).T.astype(low)
    turned_ref[1, here, :] = mix_own[...].astype(full).T.astype(low)
    turned_ref[1, there, :] = mix_other[...].astype(full).T.astype(low)

    def outer(j, _):
        for odd, out in enumerate((keep_ref, send_ref)):
            quarter = xor(plane, odd * (1 + core) + j * (2 - core))
            out[tile_at(768 * j, 768), :] = mdot(turned_ref[quarter // 3], right_ref[quarter]).astype(low)
        return 0

    lax.fori_loop(0, 2, outer, 0)
    part = ndot(right_ref[0], w_ref[0]) + ndot(right_ref[1], w_ref[1]) + ndot(right_ref[2], w_ref[2])
    part_ref[...] = part
    x_in = x_ref[...].astype(full)
    scale = lax.rsqrt(jnp.mean(x_in * x_in, axis=-1, keepdims=True) + norm_eps)
    gain = jnp.sum(part * x_in * scale, axis=0, keepdims=True)
    lined = jnp.concatenate([lined_ref[0], lined_ref[1], lined_ref[2]], 0)
    table = lax.dot_general(
        lined, hot_buckets(), (((1,), (1,)), ((), ())),
        precision=lax.Precision.HIGHEST, preferred_element_type=full,
    )
    table = jnp.concatenate([table, jnp.zeros((6, 352), full)], 1)
    other = other_ref[...]
    send_ref[1536:1552, :] = jnp.concatenate(
        [gain[:, :384], gain[:, 384:], other[:, :384], other[:, 384:], table, jnp.zeros((6, 384), full)], 0
    ).astype(low)


def wide(value):
    return value.astype(full)


def adam_kernel(steps, count, scalars, *refs):
    plane, core = scalars[0], scalars[1]
    lower = core == 0
    states, grads, outs = refs[:3], refs[3:5], refs[5 : 5 + count]
    own, other, brought, held, sems = refs[5 + count], refs[6 + count], refs[7 + count : 10 + count], refs[-5:-1], refs[-1]
    arrive = [fetch_part(grads[0], own, sems.at[8]), fetch_part(grads[1], other, sems.at[9])]
    loads = []
    for number, (where, _, _, _) in enumerate(steps):
        loads.append(
            [fetch_part(where(state), brought[i].at[number], sems.at[10 + 3 * number + i]) for i, state in enumerate(states)]
        )
    for copy in arrive:
        copy.wait()

    def place(own, other, quarter):
        turn = xor(plane, quarter)
        return own.at[stack_at(turn, core)], other.at[stack_at(turn, 1 - core)]

    flying = []
    for number, (_, quarter, read, targets) in enumerate(steps):
        slot = number % 2
        if number >= 2:
            for copy in flying[number - 2]:
                copy.wait()
        if quarter is None:
            grad = read(own, other, place, lower).astype(full)
        else:
            grad = read(*place(own, other, quarter), lower).astype(full)
        for copy in loads[number]:
            copy.wait()
        new = adam_step(brought[0][number], brought[1][number], brought[2][number], grad, True)
        copies = []
        for i, value in enumerate(new):
            order = (0, 1, 3, 2)[i]
            held[order][slot] = value
            copies.append(fetch_part(held[order].at[slot], targets(outs, i), sems.at[4 * slot + i]))
        flying.append(copies)
    for copies in flying[-2:]:
        for copy in copies:
            copy.wait()


def adam_call(spot, steps, block, states, grads, outputs, name):
    return call(
        functools.partial(adam_kernel, steps, len(outputs)), spot,
        [*[[state] for state in states], *[(grad,) for grad in grads]], outputs,
        [
            *[pltpu.VMEM(grads[0].shape, low)] * 2, *[pltpu.VMEM((len(steps),) + block, full)] * 3,
            *[pltpu.VMEM((2,) + block, full)] * 2, pltpu.VMEM((2,) + block, low), pltpu.VMEM((2,) + block, full),
            pltpu.SemaphoreType.DMA((10 + 3 * len(steps),)),
        ],
        name, 0, 60, range(len(outputs)),
    )


def small_kernel(
    scalars, own, other, gm_ref, gf_ref, gs_ref, bm_ref, bf_ref, bs_ref, gain_step, gain_first, gain_second,
    bias_step, bias_first, bias_second, table_ref,
):
    core, shard = scalars[1], scalars[2]
    total = own[...] + other[...]
    grads = []
    for j in range(2):
        row = jnp.where(shard // 2 == 1, total[2 * j + 1 : 2 * j + 2], total[2 * j : 2 * j + 1])
        grads.append(jnp.where(shard % 2 == 1, row[:, 192:], row[:, :192]))
    new = adam_step(gm_ref[...], gf_ref[...], gs_ref[...], jnp.concatenate(grads, 0), False)
    gain_step[...], gain_first[...], gain_second[...] = new[0] - gm_ref[...], new[1], new[2]
    mine, theirs = own[4:10, :32], other[4:10, :32]
    table = jnp.concatenate(chosen(core == 0, mine, theirs), 0)
    same = lax.broadcasted_iota(jnp.int32, (32, 32), 0) == lax.broadcasted_iota(jnp.int32, (32, 32), 1)
    table_ref[...] = lax.dot_general(
        jnp.where(same, 1.0, 0.0), table, (((1,), (1,)), ((), ())),
        precision=lax.Precision.HIGHEST, preferred_element_type=full,
    )
    grad = table_ref[tile_at(8 * shard, 8), :]
    new = adam_step(bm_ref[...], bf_ref[...], bs_ref[...], grad, False)
    bias_step[...], bias_first[...], bias_second[...] = new[0] - bm_ref[...], new[1], new[2]


def chosen(lower, mine, theirs):
    return jnp.where(lower, mine, theirs), jnp.where(lower, theirs, mine)


def attn_steps():
    def one(m):
        where = lambda ref: ref.at[m]

        def read(mine, theirs, lower):
            return jnp.concatenate(chosen(lower, mine[...], theirs[...]), 1)

        def targets(outs, i):
            if i == 2:
                return outs[2].at[m] if m < 3 else outs[3]
            return outs[(0, 1, 2, 4)[i]].at[m]

        return where, m, read, targets

    return [one(m) for m in range(4)]


def ffin_steps():
    def one(i, h):
        columns = slice(1024 * h, 1024 * h + 1024)
        where = lambda ref: ref.at[i, :, columns]

        def read(mine, theirs, lower):
            left, right = chosen(lower, mine[0:384, :], theirs[0:384, :])
            return jnp.concatenate([left[:192], right[:192], left[192:], right[192:]], 1)

        return where, 2 * i + h, read, lambda outs, n: where(outs[n])

    return [one(i, h) for i in range(2) for h in range(2)]


def ffout_steps():
    def one(c):
        rows = slice(256 * c, 256 * c + 256)
        where = lambda ref: ref.at[rows, :]

        def read(own, other, place, lower):
            found = []
            for q in range(4):
                mine, theirs = place(own, other, q)
                value = chosen(lower, mine[384:576, :], theirs[384:576, :])[c]
                found.append(jnp.concatenate([value[:64], value[64:128], value[128:]], 1))
            return jnp.concatenate(found, 0)

        return where, None, read, lambda outs, n: where(outs[n])

    return [one(c) for c in range(2)]


def body_fast(
    tokens,
    cotangent,
    lengths,
    deal,
    attn_master,
    ffin_master,
    ffout_master,
    gain_master,
    bias_master,
    attn_first,
    ffin_first,
    ffout_first,
    gain_first,
    bias_first,
    attn_second,
    ffin_second,
    ffout_second,
    gain_second,
    bias_second,
):
    plane, core, shard = (lax.axis_index(name) for name in ("plane", "core", "shard"))
    spot = jnp.stack([plane, core, shard])
    group, rest = shard // 2, shard % 2
    mine = group == core

    quarter = call(
        pack_attn_kernel, spot, [[attn_master], [gain_master], [bias_master]], [((208, 384), low)],
        [
            pltpu.VMEM((192, 384), full), pltpu.VMEM((2, 192), full), pltpu.VMEM((8, 12), full),
            pltpu.SemaphoreType.DMA((3,)),
        ],
        "pack_attn", 0, 60,
    )[0]
    attn_third = across(quarter, 3)

    unit = call(
        pack_ffn_kernel, spot, [[ffin_master], [ffout_master]], [((576, 256), low)],
        [pltpu.VMEM((2, 192, 256), full), pltpu.VMEM((64, 768), full), pltpu.SemaphoreType.DMA((3,))],
        "pack_ffn", 0, 60,
    )[0]
    attn_third = after(attn_third, unit)
    attn_pair = across(cat(spot, [quarter, attn_third], 208, "pair_attn_in"), 1)

    up_pairs = lambda pairs: [((p, 1, z), (p, 1, w)) for p in range(4) for z, w in pairs]
    down_pairs = lambda pairs: [((p, 0, 3 - z), (p, 0, 3 - w)) for p in range(4) for z, w in pairs]
    along = lambda value, *which: send(value, up_pairs(which) + down_pairs(which))

    def fetch_rest(own, one, gate=None):
        two = along(one, (1, 2), (2, 3))
        two = two if gate is None else after(two, gate)
        three = along(jnp.where(at_end, own, two), (2, 3), (3, 2))
        return own, one, two, three

    way = 1 - 2 * core
    at_end = shard == 3 * core
    blocks = jnp.stack(
        [shard, shard + way, shard + 2 * way, jnp.where(at_end, shard + 3 * way, shard - way)]
    )
    blocks = jnp.clip(blocks, 0, 3)
    tok_blocks = fetch_rest(tokens[0], along(tokens[0], (0, 1), (1, 2), (2, 3)))

    table_own = jnp.concatenate([lengths[0], deal[0]])
    table = jnp.where(mine, table_own, swap(table_own))
    lens, order = table[:4], table[4:]
    starts = jnp.cumsum(lens) - lens
    long_start = jnp.sum(jnp.where(lens == 512, starts, 0))
    at_half = jnp.arange(512, dtype=jnp.int32)
    token_here = jnp.where(rest == 0, long_start + at_half, at_half + 512 * (at_half >= long_start))
    seg_here = jnp.sum((token_here[:, None] >= starts[None, :]).astype(jnp.int32), axis=1)
    token_index = jnp.arange(1024, dtype=jnp.int32)

    token_column = token_here[:, None]
    token_row = jnp.where(mine, token_here, -1)[None, :]

    def wanted_by(place_of):
        rows = [lax.dynamic_slice_in_dim(place_of, 256 * xor(shard, step), 256) for step in range(4)]
        return jnp.concatenate(rows).reshape(1024, 1)

    wanted_y = wanted_by(order)
    wanted_x = wanted_by(token_index)

    def rows_here(place_of, pieces, gate=None):
        place = [lax.dynamic_slice_in_dim(place_of, blocks[i] * 256, 256) for i in range(4)]
        place = jnp.concatenate(place).reshape(1, 1024)
        chosen = call(
            pick_kernel, spot, [*pieces, after(place, wanted_y, wanted_x, token_row), token_column], [((512, 768), low)], [], "pick", 0, 8
        )[0]
        chosen = chosen if gate is None else after(chosen, *gate)
        return jnp.where(mine, chosen, swap(chosen))

    def rows_near(rows, *gates):
        pairs = [((p, c, z), (p, c, z ^ 1)) for p, c, z in ALL if z // 2 == c]
        return after(send(rows[0], pairs), *gates)

    def rows_far(rows, came, *gates):
        pairs = [((p, c, z), (p, c, z ^ 2)) for p, c, z in ALL if z // 2 == c]
        far = call(add_kernel, spot, [rows[2], came], [((256, 768), low)], [], "add_rows", 0, 4)[0]
        return after(send(far, pairs), *gates)

    def rows_back(rows, first_gate, second_gate):
        pairs = lambda step: [((p, c, z), (p, c, z ^ step)) for p, c, z in ALL if z // 2 == c]
        near, own, far = rows
        came = after(send(near, pairs(1)), first_gate)
        far = call(add_kernel, spot, [far, came], [((256, 768), low)], [], "add_rows", 0, 4)[0]
        last = after(send(far, pairs(2)), second_gate)
        return own + came[:256] + last, last


    gains, vectors = call(
        unpack_kernel, spot, [quarter, attn_pair, attn_third], [((2, 768), full), ((3, 2, 1024), full)],
        [pltpu.VMEM((32, 12), full)], "unpack", 0, 8,
    )

    def spread_plane(pieces, rows, gate=None, late=None):
        near = cat(spot, pieces, rows, "near")
        arrived = plane_first(near)
        if gate is not None:
            arrived = after(arrived, *gate)
        near = cat(spot, [near, arrived], rows, "nearest")
        return near, plane_second(near if late is None else after(near, late))

    unit = after(unit, attn_third)
    ffn_third = across(unit, 3)
    ffn_two = cat(spot, [unit, ffn_third], 576, "pair_ffn_in")
    near, far = spread_plane([attn_pair, attn_third], 192, [ffn_two])
    ffn_pair_in = across(ffn_two, 1)
    ffn_came = [ffn_pair_in, ffn_third]
    x_low = rows_here(token_index, tok_blocks, (far, *ffn_came))
    w_attn, act_one, query, key, value = call(
        project_kernel, spot,
        [x_low, gains, [attn_master], (near,), (far,)],
        [((4, 768, 384), low), ((512, 768), low)] + [((512, 384), low)] * 3,
        [pltpu.VMEM((4, 192, 384), full), pltpu.SemaphoreType.DMA((13,))], "project", 0, 60,
    )
    wo_own = w_attn[3]
    wo_other = swap(wo_own)


    cot_own = after(cotangent[0], *ffn_came)
    cot_one = along(cot_own, (1, 2), (2, 3))
    cot_two = along(cot_own, (0, 2), (1, 3))
    cot_three = along(cot_own, (0, 3), (3, 2))
    ffn_near, ffn_far = spread_plane(ffn_came, 576, [query, cot_one])
    mix_own, probs = call(
        attend_all_kernel, spot, [after(query, ffn_near), key, value, seg_here[:, None], seg_here[None, :], vectors],
        [((512, 384), low), ((6, 512, 512), low)],
        [pltpu.VMEM((512, 512), full), pltpu.VMEM((6, 512, 512), low), pltpu.SemaphoreType.DMA((3,))],
        "attend", 0, 60, (1,),
    )
    cot_blocks = (cot_own, *[after(piece, mix_own) for piece in (cot_one, cot_two, cot_three)])
    grad_y = rows_here(order, cot_blocks)
    mix_other = swap(mix_own)
    x_mid, act_two, hidden, part_two, y_part, grads_up = call(
        feed_kernel, spot,
        [
            x_low, mix_own, mix_other, wo_own, wo_other, gains, grad_y, ffin_master, [ffout_master],
            (ffn_near,), (ffn_far,),
        ],
        [
            ((512, 768), full), ((512, 768), low), ((512, 1024), low), ((512, 768), full), ((512, 768), full),
            ((4, 512, 512), low),
        ],
        [
            pltpu.VMEM((512, 768), low), pltpu.VMEM((768, 768), low), pltpu.VMEM((2, 768, 1024), low),
            pltpu.VMEM((1024, 768), low), pltpu.VMEM((256, 768), full), pltpu.VMEM((512, 1024), full),
            pltpu.VMEM((512, 1024), full), pltpu.SemaphoreType.DMA((61,)),
        ],
        "feed", 0, 24,
    )
    ffn_send, out_kept = call(
        sent_kernel, spot, [act_two, grads_up, hidden, grad_y], [((4608, 256), low), ((1536, 256), low)],
        [pltpu.VMEM((768, 512), low), pltpu.VMEM((256, 768), full)], "sent", 0, 12,
    )
    ffn_first = plane_first(ffn_send)
    ffn_keep = call(
        kept_kernel, spot, [act_two, after(grads_up, ffn_send), out_kept], [((4608, 256), low)],
        [pltpu.VMEM((768, 512), low)], "kept", 0, 12,
    )[0]
    part_other = after(swap(part_two), ffn_keep)

    grad_mid, right, lined, gain_two = call(
        back_kernel, spot,
        [
            (part_two,), (part_other,), (x_mid,), (grad_y,), gains, (wo_own,), (wo_other,),
            (query,), (key,), (value,), (probs,),
        ],
        [
            ((512, 768), full), ((4, 512, 384), low), ((3, 2, 1024), full), ((1, 768), full),
        ],
        [
            pltpu.VMEM((512, 768), low), pltpu.VMEM((512, 384), low), pltpu.VMEM((512, 512), full), pltpu.VMEM((512, 512), low),
            pltpu.VMEM((128, 1024), full), *[pltpu.VMEM((512, 768), full)] * 3, pltpu.VMEM((512, 768), low),
            *[pltpu.VMEM((768, 384), low)] * 2, *[pltpu.VMEM((512, 384), low)] * 3, pltpu.VMEM((6, 512, 512), low),
            pltpu.SemaphoreType.DMA((10,)),
        ],
        "back", 0, 60,
    )
    y_other = swap(after(y_part, part_other))
    y_rows = call(
        spread_y_kernel, spot, [(x_mid,), (after(y_part, right),), (y_other,), wanted_y, token_row],
        [((512, 768), low), ((256, 768), low), ((256, 768), low)],
        [pltpu.VMEM((512, 768), low), *[pltpu.VMEM((512, 768), full)] * 3, pltpu.SemaphoreType.DMA((3,))],
        "spread_y", 0, 60,
    )
    ffn_first = after(ffn_first, right, y_rows[0])
    one_out = lambda kernel, inputs, shape, name: call(kernel, spot, inputs, [(shape, low)], [], name, 0, 8)[0]
    ffn_passed = one_out(pass_ffn_kernel, [ffn_keep, ffn_first], (2304, 256), "pass_ffn")
    ffn_second = plane_second(ffn_passed)
    attn_send, attn_keep, part_one = call(
        last_kernel, spot,
        [
            (after(act_one, ffn_passed),), (mix_own,), (mix_other,), (right,), (w_attn,), (x_low,), lined, gain_two,
        ],
        [((1552, 384), low), ((1536, 384), low), ((512, 768), full)],
        [
            pltpu.VMEM((2, 768, 512), low), pltpu.VMEM((512, 768), low), *[pltpu.VMEM((512, 384), low)] * 2,
            pltpu.VMEM((4, 512, 384), low), pltpu.VMEM((4, 768, 384), low), pltpu.VMEM((512, 768), low),
            pltpu.SemaphoreType.DMA((6,)),
        ],
        "last", 0, 60,
    )
    y_near = rows_near([after(y_rows[0], ffn_passed)], part_one)
    ffn_second = after(ffn_second, part_one, y_near)
    ffn_own, ffn_two, ffn_far = call(
        sum_ffn_kernel, spot, [ffn_keep, ffn_first, ffn_second],
        [((576, 256), full), ((1152, 256), low), ((576, 256), full)],
        [pltpu.VMEM((576, 256), full), pltpu.VMEM((576, 256), full), pltpu.SemaphoreType.DMA((2,))],
        "sum_ffn", 0, 8, (0, 2),
    )
    ffn_near = across(ffn_two, 1)
    x_rows = call(
        spread_x_kernel, spot,
        [(part_one,), (swap(part_one),), (x_low,), gains, (grad_mid,), wanted_x, token_row],
        [((512, 768), low), ((256, 768), low), ((256, 768), low)],
        [
            pltpu.VMEM((512, 768), low), *[pltpu.VMEM((512, 768), full)] * 3, pltpu.VMEM((512, 768), low),
            pltpu.SemaphoreType.DMA((4,)),
        ],
        "spread_x", 0, 60,
    )
    ffn_send = call(far_kernel, spot, [ffn_far, after(ffn_near, *x_rows)], [((576, 256), low)], [], "far_ffn", 0, 8)[0]
    ffn_last = across(ffn_send, 3)
    attn_first_came = after(plane_first(after(attn_send, ffn_second)), ffn_send, *x_rows)
    passed = one_out(pass_attn_kernel, [attn_keep, attn_send, attn_first_came], (784, 384), "pass_attn")
    attn_second_came = plane_second(passed)
    attn_own, attn_two, attn_far = call(
        sum_attn_kernel, spot, [attn_keep, passed, attn_first_came, attn_second_came],
        [((208, 384), full), ((416, 384), low), ((208, 384), full)], [], "sum_attn", 0, 8,
    )

    attn_near_came = across(attn_two, 1)
    ffn_last = after(ffn_last, attn_two)
    ffn_sum = one_out(total_kernel, [ffn_own, ffn_near, ffn_last], (576, 256), "total_ffn")
    attn_far_send = call(far_kernel, spot, [attn_far, attn_near_came], [((208, 384), low)], [], "far_attn", 0, 8)[0]
    attn_last = across(attn_far_send, 3)
    ffn_pair = cat(spot, [ffn_sum, after(plane_first(ffn_sum), attn_far_send)], 576, "pair_ffn")
    ffn_stack = cat(spot, [ffn_pair, after(plane_second(ffn_pair), attn_last)], 576, "stack_ffn")
    ffn_sum = (ffn_stack, swap(ffn_stack))
    flat, wide_in = (512, 768), (2, 192, 2048)
    ffin_res = adam_call(
        spot, ffin_steps(), (192, 1024), [ffin_master, ffin_first, ffin_second], ffn_sum,
        [(wide_in, full), (wide_in, full), (wide_in, full), (wide_in, low)], "adam_ffin",
    )
    ffout_res = adam_call(
        spot, ffout_steps(), (256, 768), [ffout_master, ffout_first, ffout_second], ffn_sum,
        [(flat, full), (flat, full), (flat, full), (flat, low)], "adam_ffout",
    )
    attn_sum, small = call(
        total_kernel, spot, [attn_own, attn_near_came, after(attn_last, ffn_stack)],
        [((192, 384), low), ((16, 384), full)], [], "total_attn", 0, 8,
    )
    attn_near = cat(spot, [attn_sum, after(plane_first(attn_sum), ffin_res[0])], 192, "pair_attn")
    attn_stack = cat(spot, [attn_near, after(plane_second(attn_near), ffout_res[0])], 192, "stack_attn")
    attn_sum = (attn_stack, swap(attn_stack))
    x_rows = [after(value, small) for value in x_rows]
    y_far = rows_far(y_rows, after(y_near, small), ffin_res[0])
    layer_out = y_rows[1] + y_near[:256] + y_far
    input_grad, _ = rows_back(x_rows, ffin_res[0], ffout_res[0])
    small_other = swap(small)
    square = (4, 192, 768)
    attn_res = adam_call(
        spot, attn_steps(), (192, 768), [attn_master, attn_first, attn_second], attn_sum,
        [(square, full), (square, full), ((3, 192, 768), full), ((192, 768), full), (square, low)], "adam_attn",
    )
    smalls = call(
        small_kernel, spot,
        [small, small_other, gain_master, gain_first, gain_second, bias_master, bias_first, bias_second],
        [((2, 192), full)] * 3 + [((8, 12), full)] * 3, [pltpu.VMEM((32, 12), full)], "adam_small", 0, 4,
    )
    return (
        layer_out[None],
        input_grad[None],
        attn_res[0],
        ffin_res[0],
        ffout_res[0],
        smalls[0],
        smalls[3],
        attn_res[1],
        ffin_res[1],
        ffout_res[1],
        smalls[1],
        smalls[4],
        attn_res[2],
        attn_res[3],
        ffin_res[2],
        ffout_res[2],
        smalls[2],
        smalls[5],
        attn_res[4],
        ffin_res[3],
        ffout_res[3],
    )


def body_any(
    tokens,
    cotangent,
    lengths,
    deal,
    attn_master,
    ffin_master,
    ffout_master,
    gain_master,
    bias_master,
    attn_first,
    ffin_first,
    ffout_first,
    gain_first,
    bias_first,
    attn_second,
    ffin_second,
    ffout_second,
    gain_second,
    bias_second,
):
    shards = lax.axis_size("shard")
    core = lax.axis_index("core")
    shard = lax.axis_index("shard")
    tok_rows, model = tokens.shape[1], tokens.shape[2]
    heads = bias_master.shape[1]
    own_heads = heads // 2
    part = model // 2
    whole_len = tok_rows * shards
    half_len = whole_len // 2
    per_half = shards // 4
    rows = half_len // per_half
    place, sub = shard // per_half, shard % per_half
    group, rest = place // 2, place % 2
    mine = group == core
    siblings = [[a * per_half + b for b in range(per_half)] for a in range(4)]

    def join_half(value):
        if per_half == 1:
            return value
        return lax.all_gather(value, "shard", axis=0, tiled=True, axis_index_groups=siblings)

    table_own = jnp.concatenate([lengths[0], deal[0]])
    table = jnp.where(mine, table_own, swap(table_own))
    count = lengths.shape[1]
    lens, order = table[:count], table[count:]
    starts = jnp.cumsum(lens) - lens
    long_start = jnp.sum(jnp.where(lens == half_len, starts, 0))
    at_half = jnp.arange(half_len, dtype=jnp.int32)
    token_half = jnp.where(
        rest == 0, long_start + at_half, at_half + half_len * (at_half >= long_start)
    )
    seg_half = jnp.sum((token_half[:, None] >= starts[None, :]).astype(jnp.int32), axis=1)
    first_row = sub * rows
    token_here = lax.dynamic_slice_in_dim(token_half, first_row, rows)
    seg_here = lax.dynamic_slice_in_dim(seg_half, first_row, rows)

    def rows_here(place_of, own):
        gathered = lax.all_gather(own, "shard", axis=0, tiled=True)
        gathered = jnp.where(mine, gathered, swap(gathered))
        picked = (place_of[None, :] == token_here[:, None]).astype(low)
        return mdot(picked, gathered).astype(low)

    def rows_back(place_of, here):
        picked = (place_of[:, None] == token_here[None, :]) & mine
        spread = mdot(picked.astype(low), here).astype(low)
        return lax.psum_scatter(spread, "shard", scatter_dimension=0, tiled=True)

    ff_rows = ffout_master.shape[0]
    ff_part = ff_rows // 2
    attn_low = attn_master.astype(low)
    cols = lax.dynamic_slice_in_dim(attn_low[:3], core * part, part, 2)
    ffin_low = ffin_master.astype(low).reshape(2, -1, shards, 2, ff_part)
    ffin_low = lax.dynamic_index_in_dim(ffin_low, core, 3, keepdims=False)
    ffin_low = ffin_low.reshape(2, -1, shards * ff_part)
    ffout_low = lax.dynamic_slice_in_dim(ffout_master.astype(low), core * ff_part, ff_part, 0)
    w_qkv = lax.all_gather(cols, "shard", axis=1, tiled=True)
    w_o = lax.all_gather(attn_low[3], "shard", axis=0, tiled=True)
    w_in = lax.all_gather(ffin_low, "shard", axis=1, tiled=True)
    w_out = lax.all_gather(ffout_low, "shard", axis=0, tiled=True)
    gains = lax.all_gather(gain_master.astype(low), "shard", axis=1, tiled=True).astype(full)
    bias = lax.all_gather(bias_master.astype(low), "shard", axis=0, tiled=True).astype(full)

    token_index = jnp.arange(whole_len, dtype=jnp.int32)
    x_low = rows_here(token_index, tokens[0])
    grad_y = rows_here(order, cotangent[0])

    x_in = x_low.astype(full)
    scale_one = lax.rsqrt(jnp.mean(x_in * x_in, axis=-1, keepdims=True) + norm_eps)
    act_one = (x_in * scale_one * gains[0]).astype(low)
    query = mdot(act_one, w_qkv[0]).astype(low)
    key_own = mdot(act_one, w_qkv[1]).astype(low)
    value_own = mdot(act_one, w_qkv[2]).astype(low)
    key, value = join_half(key_own), join_half(value_own)
    span = rows + half_len
    relative = jnp.arange(span, dtype=jnp.int32) - rows - first_row
    ids = jnp.arange(bias.shape[0], dtype=jnp.int32)
    one_hot = (bucket_of(relative)[None, :] == ids[:, None]).astype(full)
    bias_own = lax.dynamic_slice_in_dim(bias, core * own_heads, own_heads, 1)
    vectors = lax.dot_general(
        bias_own, one_hot, (((0,), (0,)), ((), ())), precision=lax.Precision.HIGHEST
    )
    mix_own, probs = attend(
        query, key, value, seg_here[:, None], seg_half[None, :], vectors
    )
    mix = both_cores(mix_own, swap(mix_own), core, 1)
    x_mid = x_in + mdot(mix, w_o)
    scale_two = lax.rsqrt(jnp.mean(x_mid * x_mid, axis=-1, keepdims=True) + norm_eps)
    act_two = (x_mid * scale_two * gains[1]).astype(low)
    gate_pre = mdot(act_two, w_in[0])
    up_pre = mdot(act_two, w_in[1])
    gated, gelu_pull = jax.vjp(
        lambda gate_val, up_val: jax.nn.gelu(gate_val, approximate=True) * up_val, gate_pre, up_pre
    )
    hidden = gated.astype(low)
    y_part = mdot(hidden, w_out)
    y_here = (x_mid + y_part + swap(y_part)).astype(low)
    layer_out = rows_back(order, y_here)

    grad_gate, grad_up = gelu_pull(ndot(grad_y, w_out))
    grad_gate, grad_up = grad_gate.astype(low), grad_up.astype(low)
    d_out = tdot(hidden, grad_y).astype(low)
    d_in = jnp.stack([tdot(act_two, grad_gate), tdot(act_two, grad_up)]).astype(low)
    part_two = ndot(grad_gate, w_in[0]) + ndot(grad_up, w_in[1])
    grad_act_two = part_two + swap(part_two)
    turned = grad_act_two * gains[1]
    grad_mid = (
        grad_y.astype(full)
        + scale_two * turned
        - x_mid * scale_two**3 * jnp.mean(turned * x_mid, axis=-1, keepdims=True)
    )
    d_gain_two = jnp.sum(grad_act_two * x_mid * scale_two, axis=0)
    grad_attn = grad_mid.astype(low)
    w_o_own = lax.dynamic_slice_in_dim(w_o, core * part, part, 0)
    grad_mix = ndot(grad_attn, w_o_own).astype(low)
    d_wo = tdot(mix, lax.dynamic_slice_in_dim(grad_attn, core * part, part, 1)).astype(low)
    grad_q, grad_k, grad_v, diagonals = attend_back(query, key, value, grad_mix, probs, span)
    if per_half > 1:
        grad_k = lax.psum_scatter(
            grad_k, "shard", scatter_dimension=0, tiled=True, axis_index_groups=siblings
        )
        grad_v = lax.psum_scatter(
            grad_v, "shard", scatter_dimension=0, tiled=True, axis_index_groups=siblings
        )
    d_wq = tdot(act_one, grad_q).astype(low)
    d_wk = tdot(act_one, grad_k).astype(low)
    d_wv = tdot(act_one, grad_v).astype(low)
    part_one = ndot(grad_q, w_qkv[0]) + ndot(grad_k, w_qkv[1]) + ndot(grad_v, w_qkv[2])
    grad_act_one = part_one + swap(part_one)
    turned = grad_act_one * gains[0]
    grad_x = (
        grad_mid
        + scale_one * turned
        - x_in * scale_one**3 * jnp.mean(turned * x_in, axis=-1, keepdims=True)
    ).astype(low)
    d_gain_one = jnp.sum(grad_act_one * x_in * scale_one, axis=0)
    input_grad = rows_back(token_index, grad_x)

    lined = diagonals.reshape(own_heads, span)
    table_own = lax.dot_general(
        one_hot, lined, (((1,), (1,)), ((), ())), precision=lax.Precision.HIGHEST
    )
    empty = jnp.zeros_like(table_own)
    grad_table = jnp.where(
        core == 0,
        jnp.concatenate([table_own, empty], 1),
        jnp.concatenate([empty, table_own], 1),
    )
    grad_gain = jnp.where(core == 0, jnp.stack([d_gain_one, d_gain_two]), 0.0)

    d_attn = jnp.stack([d_wq, d_wk, d_wv, d_wo])

    def reduced(grad, axis):
        share = lax.psum_scatter(grad, "shard", scatter_dimension=axis, tiled=True)
        return lax.psum(share, "plane")

    g_attn = reduced(d_attn, 1)
    g_attn = both_cores(g_attn, swap(g_attn), core, 2).astype(full)
    g_in = reduced(d_in, 1)
    g_in = g_in.reshape(2, -1, shards, 1, ff_part)
    g_in = both_cores(g_in, swap(g_in), core, 3).reshape(ffin_master.shape).astype(full)
    g_out = reduced(d_out, 0)
    g_out = both_cores(g_out, swap(g_out), core, 0).astype(full)
    g_gain, g_bias = lax.psum((grad_gain, grad_table), ("plane", "core", "shard"))
    own_gain = gain_master.shape[1]
    g_gain = lax.dynamic_slice_in_dim(g_gain, shard * own_gain, own_gain, 1)
    own_bias = bias_master.shape[0]
    g_bias = lax.dynamic_slice_in_dim(g_bias, shard * own_bias, own_bias, 0)

    attn_res = adam_step(attn_master, attn_first, attn_second, g_attn, True)
    ffin_res = adam_step(ffin_master, ffin_first, ffin_second, g_in, True)
    ffout_res = adam_step(ffout_master, ffout_first, ffout_second, g_out, True)
    gain_res = adam_step(gain_master, gain_first, gain_second, g_gain, False)
    bias_res = adam_step(bias_master, bias_first, bias_second, g_bias, False)
    return (
        layer_out[None],
        input_grad[None],
        attn_res[0],
        ffin_res[0],
        ffout_res[0],
        gain_res[0] - gain_master,
        bias_res[0] - bias_master,
        attn_res[1],
        ffin_res[1],
        ffout_res[1],
        gain_res[1],
        bias_res[1],
        attn_res[2][:3],
        attn_res[2][3],
        ffin_res[2],
        ffout_res[2],
        gain_res[2],
        bias_res[2],
        attn_res[3],
        ffin_res[3],
        ffout_res[3],
    )


def solution(mesh):
    reps, shards = mesh.devices.shape
    cores = Mesh(mesh.devices.reshape(reps // 2, 2, shards), ("plane", "core", "shard"))
    rep = ("plane", "core")
    tok = P(rep, "shard", None)
    row = P(rep, None)
    second = P(None, "shard", None)
    first = P("shard", None)
    gain = P(None, "shard")
    states = (second, second, first, gain, first)
    in_specs = (tok, tok, row, row) + states * 3
    out_specs = (
        (tok, tok) + states + states + (second, first, second, first, gain, first) + states[:3]
    )
    body = body_fast if (reps, shards) == (8, 4) else body_any
    return jax.shard_map(body, mesh=cores, in_specs=in_specs, out_specs=out_specs, check_vma=False)
```
